32 devices in a mesh: gx: 2 (over core), gy: 16 (over z, y, x).
Axes of the slice: x: 2, y: 2, z: 4, core: 2. Of those that a mesh axis runs over, the one named last changes fastest.
Arguments:
- frame_input: bfloat16 [8192, 1024], P(('gx', 'gy')), may hold values from -6 to 6
- code_embed: bfloat16 [8192, 3, 1024], P(('gx', 'gy')), may hold values from -6 to 6
- segment_ids: int32 [32, 256], P(('gx', 'gy')), may hold values from 0 to 3, never falling along the last dimension, each value on 1 to 128 neighbouring positions
- frame_cotangent: bfloat16 [8192, 1024], P(('gx', 'gy')), may hold values from -6 to 6
- code_cotangent: bfloat16 [8192, 3, 1024], P(('gx', 'gy')), may hold values from -6 to 6
- frame_prenorm: bfloat16 [1024], P(('gx', 'gy')), may hold values from 0.5 to 1.5
- frame_query: bfloat16 [1024, 1024], P(('gx', 'gy')), may hold values from -0.1875 to 0.1875
- frame_keys: bfloat16 [1024, 1024], P(('gx', 'gy')), may hold values from -0.1875 to 0.1875
- frame_values: bfloat16 [1024, 1024], P(('gx', 'gy')), may hold values from -0.1875 to 0.1875
- frame_outproj: bfloat16 [1024, 1024], P(('gx', 'gy')), may hold values from -0.75 to 0.75
- frame_midnorm: bfloat16 [1024], P(('gx', 'gy')), may hold values from 0.5 to 1.5
- frame_upproj: bfloat16 [1024, 4096], P(('gx', 'gy')), may hold values from -0.1875 to 0.1875
- frame_upbias: bfloat16 [4096], P(('gx', 'gy')), may hold values from -3 to 3
- frame_downproj: bfloat16 [4096, 1024], P(('gx', 'gy')), may hold values from -0.09375 to 0.09375
- frame_downbias: bfloat16 [1024], P(('gx', 'gy')), may hold values from -3 to 3
- code_prenorm: bfloat16 [1024], P(('gx', 'gy')), may hold values from 0.5 to 1.5
- code_query: bfloat16 [1024, 1024], P(('gx', 'gy')), may hold values from -0.1875 to 0.1875
- code_keys: bfloat16 [1024, 1024], P(('gx', 'gy')), may hold values from -0.1875 to 0.1875
- code_values: bfloat16 [1024, 1024], P(('gx', 'gy')), may hold values from -0.1875 to 0.1875
- code_outproj: bfloat16 [1024, 1024], P(('gx', 'gy')), may hold values from -0.25 to 0.25
- code_midnorm: bfloat16 [1024], P(('gx', 'gy')), may hold values from 0.5 to 1.5
- code_upproj: bfloat16 [1024, 4096], P(('gx', 'gy')), may hold values from -0.1875 to 0.1875
- code_upbias: bfloat16 [4096], P(('gx', 'gy')), may hold values from -3 to 3
- code_downproj: bfloat16 [4096, 1024], P(('gx', 'gy')), may hold values from -0.09375 to 0.09375
- code_downbias: bfloat16 [1024], P(('gx', 'gy')), may hold values from -3 to 3
Outputs:
- frame_output: bfloat16 [8192, 1024], P(('gx', 'gy'))
- code_output: bfloat16 [8192, 3, 1024], P(('gx', 'gy'))
- frame_input_grad: float32 [8192, 1024], P(('gx', 'gy'))
- code_embed_grad: float32 [8192, 3, 1024], P(('gx', 'gy'))
- frame_prenorm_grad: float32 [1024], P(('gx', 'gy'))
- frame_query_grad: float32 [1024, 1024], P(('gx', 'gy'))
- frame_keys_grad: float32 [1024, 1024], P(('gx', 'gy'))
- frame_values_grad: float32 [1024, 1024], P(('gx', 'gy'))
- frame_outproj_grad: float32 [1024, 1024], P(('gx', 'gy'))
- frame_midnorm_grad: float32 [1024], P(('gx', 'gy'))
- frame_upproj_grad: float32 [1024, 4096], P(('gx', 'gy'))
- frame_upbias_grad: float32 [4096], P(('gx', 'gy'))
- frame_downproj_grad: float32 [4096, 1024], P(('gx', 'gy'))
- frame_downbias_grad: float32 [1024], P(('gx', 'gy'))
- code_prenorm_grad: float32 [1024], P(('gx', 'gy'))
- code_query_grad: float32 [1024, 1024], P(('gx', 'gy'))
- code_keys_grad: float32 [1024, 1024], P(('gx', 'gy'))
- code_values_grad: float32 [1024, 1024], P(('gx', 'gy'))
- code_outproj_grad: float32 [1024, 1024], P(('gx', 'gy'))
- code_midnorm_grad: float32 [1024], P(('gx', 'gy'))
- code_upproj_grad: float32 [1024, 4096], P(('gx', 'gy'))
- code_upbias_grad: float32 [4096], P(('gx', 'gy'))
- code_downproj_grad: float32 [4096, 1024], P(('gx', 'gy'))
- code_downbias_grad: float32 [1024], P(('gx', 'gy'))
The draws below stay inside these ranges and needn't reach their ends.
Inputs may be any that keep to these rules, and one draw needn't show every extreme that they name: `segment_ids`: within each row of 256 frames the ids never fall; every segment covers 1 to 128 frames and one covers exactly 128.
All inputs are finite; a program needn't handle non-finite values.
Results may differ from the reference program's by a relative error of at most 0.025.
Values may be sent and summed in bfloat16 or wider, within the bound.
No kernel may reach another device: no remote copies, remote signals or barrier semaphores. Data moves between devices by JAX's collectives and lax.ppermute only.
A program may use at most 320 MiB of HBM per device.

```python
import math
import jax
import jax.numpy as jnp
import numpy as np
from jax import lax

D = 1024
HEADS = 16
HD = 64
FF = 4096
CB = 3
FR_DEV = 256
SEGS = 4
SEG_MOST = 128
FRAMES = 8192
N_GX = 2
N_GY = 16


def strengthened(entries, key, source, target, parts, factor):
    owner, partner = [(jnp.arange(entries.shape[axis_at]) // (entries.shape[axis_at] // parts)).reshape([-1 if axis == axis_at else 1 for axis in range(entries.ndim)]) for axis_at in (source, target)]
    chosen = jax.random.permutation(key, parts)[partner]
    strong = (owner == chosen) | (owner == (partner + parts // 2) % parts)
    return jnp.where(strong, factor * entries, entries)


def levels(rng, dims, shards, least, top_value):
    loudness, own = 1.0, jax.random.fold_in(rng, 6)
    for position, blocks in shards:
        steps = jnp.exp(jax.random.uniform(jax.random.fold_in(own, position), (blocks,), jnp.float32, least / len(shards), top_value / len(shards)))
        loudness = loudness * jnp.repeat(steps, dims[position] // blocks).reshape([-1 if axis == position else 1 for axis in range(len(dims))])
    return loudness


def length_profile(amount, total, bound, slope):
    portions = [(1 << 20) // math.isqrt(rank ** slope) + 1 for rank in range(2, amount + 1)]
    surplus, given = total - bound - (amount - 1), [1] * (amount - 1)
    while surplus > 0:
        free = [i for i in range(amount - 1) if given[i] < bound]
        pool, budget = sum([portions[i] for i in free]), surplus
        for i in free:
            addition = min(bound - given[i], max(1, budget * portions[i] // pool), surplus)
            given[i] = given[i] + addition
            surplus = surplus - addition
    return np.array([bound] + given)


def uneven(own_key, count, total, most, lean):
    if count == 2:
        one = jax.random.randint(own_key, (), max(1, total - most), min(most, total - 1) + 1)
        return jnp.stack([one, total - one])
    lengths = jnp.asarray(length_profile(count, total, most, lean), jnp.int32)
    couples = (count - 1) // 2
    giver, receiver = lengths[1:1 + 2 * couples:2], lengths[2:2 + 2 * couples:2]
    room = jnp.minimum(giver - 1, most - receiver)
    passed = jax.random.randint(jax.random.fold_in(own_key, 1), (couples,), 0, 1 << 20) % (room + 1)
    lengths = lengths.at[1:1 + 2 * couples:2].set(giver - passed).at[2:2 + 2 * couples:2].set(receiver + passed)
    return lengths[jax.random.permutation(jax.random.fold_in(own_key, 2), count)]


def noise(rng, extent, scale, reach, cuts=(), dtype=jnp.bfloat16):
    level = levels(rng, extent, cuts, -0.22, 0.18) if cuts else 1.0
    entries = jax.random.normal(rng, extent, jnp.float32) * scale * level
    return jnp.minimum(jnp.maximum(entries, -reach), reach).astype(dtype)


def gaussian_with(own_key, shape, scale, most, shards, heavy, held_as=jnp.bfloat16):
    values = scale * jax.random.normal(own_key, shape, jnp.float32)
    if shards:
        values = values * levels(own_key, shape, shards, -0.22, 0.18)
    return jnp.clip(strengthened(values, jax.random.fold_in(own_key, 3), *heavy), -most, most).astype(held_as)


def setup_inputs(seed: int = 0) -> dict:
    streams_of = jax.random.split(jax.random.key(seed), 26)
    frame_input = gaussian_with(streams_of[0], (FRAMES, D), 1.0, 6.0, ((0, 32),), (0, 1, 32, 2.75))
    code_embed = gaussian_with(streams_of[1], (FRAMES, CB, D), 1.0, 6.0, ((0, 32),), (0, 2, 32, 2.75))
    segment_ids = jax.vmap(lambda own: jnp.searchsorted(jnp.cumsum(uneven(own, SEGS, FR_DEV, SEG_MOST, 0)), jnp.arange(FR_DEV), side="right"))(jax.random.split(streams_of[2], (N_GX * N_GY))).reshape((N_GX * N_GY, FR_DEV)).astype(jnp.int32)
    frame_cotangent = noise(streams_of[3], (FRAMES, D), 1.0, 6.0, ((0, 32),))
    code_cotangent = noise(streams_of[4], (FRAMES, CB, D), 1.0, 6.0, ((0, 32),))
    frame_prenorm = jnp.clip(1.0 + 0.1 * jax.random.normal(streams_of[5], (D,), jnp.float32), 0.5, 1.5).astype(jnp.bfloat16)
    frame_query = noise(streams_of[6], (D, D), D ** -0.5, 0.1875, ((0, 32),))
    frame_keys = noise(streams_of[7], (D, D), D ** -0.5, 0.1875, ((0, 32),))
    frame_values = noise(streams_of[8], (D, D), D ** -0.5, 0.1875, ((0, 32),))
    frame_outproj = noise(streams_of[9], (D, D), (D // 16) ** -0.5, 0.75, ((0, 32),))
    frame_midnorm = jnp.clip(1.0 + 0.1 * jax.random.normal(streams_of[10], (D,), jnp.float32), 0.5, 1.5).astype(jnp.bfloat16)
    frame_upproj = noise(streams_of[11], (D, FF), D ** -0.5, 0.1875, ((0, 32),))
    frame_upbias = noise(streams_of[12], (FF,), 0.5, 3.0, ((0, 32),))
    frame_downproj = noise(streams_of[13], (FF, D), FF ** -0.5, 0.09375, ((0, 32),))
    frame_downbias = noise(streams_of[14], (D,), 0.3, 3.0, ((0, 32),))
    code_prenorm = jnp.clip(1.0 + 0.1 * jax.random.normal(streams_of[15], (D,), jnp.float32), 0.5, 1.5).astype(jnp.bfloat16)
    code_query = noise(streams_of[16], (D, D), D ** -0.5, 0.1875, ((0, 32),))
    code_keys = noise(streams_of[17], (D, D), D ** -0.5, 0.1875, ((0, 32),))
    code_values = noise(streams_of[18], (D, D), D ** -0.5, 0.1875, ((0, 32),))
    code_outproj = noise(streams_of[19], (D, D), (D // 2) ** -0.5, 0.25, ((0, 32),))
    code_midnorm = jnp.clip(1.0 + 0.1 * jax.random.normal(streams_of[20], (D,), jnp.float32), 0.5, 1.5).astype(jnp.bfloat16)
    code_upproj = noise(streams_of[21], (D, FF), D ** -0.5, 0.1875, ((0, 32),))
    code_upbias = noise(streams_of[22], (FF,), 0.5, 3.0, ((0, 32),))
    code_downproj = noise(streams_of[23], (FF, D), FF ** -0.5, 0.09375, ((0, 32),))
    code_downbias = noise(streams_of[24], (D,), 0.3, 3.0, ((0, 32),))
    return {"frame_input": frame_input, "code_embed": code_embed, "segment_ids": segment_ids, "frame_cotangent": frame_cotangent, "code_cotangent": code_cotangent, "frame_prenorm": frame_prenorm, "frame_query": frame_query, "frame_keys": frame_keys, "frame_values": frame_values, "frame_outproj": frame_outproj, "frame_midnorm": frame_midnorm, "frame_upproj": frame_upproj, "frame_upbias": frame_upbias, "frame_downproj": frame_downproj, "frame_downbias": frame_downbias, "code_prenorm": code_prenorm, "code_query": code_query, "code_keys": code_keys, "code_values": code_values, "code_outproj": code_outproj, "code_midnorm": code_midnorm, "code_upproj": code_upproj, "code_upbias": code_upbias, "code_downproj": code_downproj, "code_downbias": code_downbias}


@jax.custom_vjp
def low(v):
    return lax.optimization_barrier(v.astype(jnp.bfloat16)).astype(jnp.float32)

@jax.custom_vjp
def low_back(v):
    return v

def low_keep(v):
    return (low(v), None)

def low_pass(kept, grad):
    return (grad,)

def back_keep(v):
    return (v, None)

def back_low(kept, grad):
    return (low(grad),)
low.defvjp(low_keep, low_pass)
low_back.defvjp(back_keep, back_low)

def gelu_tanh(value):
    return 0.5 * value * (1.0 + jnp.tanh(0.7978845608028654 * (value + 0.044715 * value * value * value)))

def rms_scale(value, gain_vec):
    return value * lax.rsqrt(lax.optimization_barrier(jnp.mean(value * value, axis=-1, keepdims=True)) + 1e-05) * gain_vec

def matmul(left, right):
    return jnp.dot(left, right, precision=lax.Precision.HIGHEST)

def block(x_in, allowed, params, groups):
    prenorm, w_query, w_key, w_value, w_out, midnorm, w_up, b_up, w_down, b_down = params
    row_count = x_in.shape[0]
    width = x_in.shape[1]
    span = row_count // groups
    normed = low(rms_scale(x_in, prenorm))
    query = low(low_back(matmul(normed, w_query))).reshape(groups, span, HEADS, HD)
    key_rows = low(low_back(matmul(normed, w_key))).reshape(groups, span, HEADS, HD)
    value_rows = low(low_back(matmul(normed, w_value))).reshape(groups, span, HEADS, HD)
    scores = jnp.einsum('glhe,gmhe->ghlm', query, key_rows, precision=lax.Precision.HIGHEST)
    scores = low_back(scores * HD ** (-0.5))
    scores = jnp.where(allowed[:, None], scores, -1e+30)
    probs = low(jax.nn.softmax(scores, axis=-1))
    mixed = jnp.einsum('ghlm,gmhe->glhe', probs, value_rows, precision=lax.Precision.HIGHEST)
    mixed = low(low_back(mixed.reshape(row_count, width)))
    hidden = x_in + low_back(matmul(mixed, w_out))
    normed_two = low(rms_scale(hidden, midnorm))
    preact = low_back(matmul(normed_two, w_up) + b_up)
    activated = low(gelu_tanh(preact))
    return hidden + low_back(matmul(activated, w_down) + b_down)

def row_forward(frames, codes, segments, frame_params, code_params):
    place = jnp.arange(FR_DEV)
    frame_allowed = ((segments[:, None] == segments[None, :]) & (place[:, None] >= place[None, :]))[None]
    frame_result = block(frames, frame_allowed, frame_params, 1)
    code_in = (codes + frame_result[:, None, :]).reshape(FR_DEV * CB, D)
    code_place = jnp.arange(CB)
    code_allowed = (code_place[:, None] >= code_place[None, :])[None]
    code_result = block(code_in, code_allowed, code_params, FR_DEV).reshape(FR_DEV, CB, D)
    return (frame_result, code_result)

def reference(frame_input, code_embed, segment_ids, frame_cotangent, code_cotangent, frame_prenorm, frame_query, frame_keys, frame_values, frame_outproj, frame_midnorm, frame_upproj, frame_upbias, frame_downproj, frame_downbias, code_prenorm, code_query, code_keys, code_values, code_outproj, code_midnorm, code_upproj, code_upbias, code_downproj, code_downbias):
    row_total = segment_ids.shape[0]
    frame_weights = tuple((weight_arr.astype(jnp.float32) for weight_arr in (frame_prenorm, frame_query, frame_keys, frame_values, frame_outproj, frame_midnorm, frame_upproj, frame_upbias, frame_downproj, frame_downbias)))
    code_weights = tuple((weight_arr.astype(jnp.float32) for weight_arr in (code_prenorm, code_query, code_keys, code_values, code_outproj, code_midnorm, code_upproj, code_upbias, code_downproj, code_downbias)))

    def forward(frames, codes, frame_params, code_params):

        def one_row(inputs):
            return jax.checkpoint(row_forward)(inputs[0], inputs[1], inputs[2], frame_params, code_params)
        frame_rows, code_rows = lax.map(one_row, (frames.reshape(row_total, FR_DEV, D), codes.reshape(row_total, FR_DEV, CB, D), segment_ids))
        return (frame_rows.reshape(row_total * FR_DEV, D), code_rows.reshape(row_total * FR_DEV, CB, D))
    outputs, pullback = jax.vjp(forward, frame_input.astype(jnp.float32), code_embed.astype(jnp.float32), frame_weights, code_weights)
    grad_frames, grad_codes, frame_grads, code_grads = pullback((frame_cotangent.astype(jnp.float32), code_cotangent.astype(jnp.float32)))
    return (outputs[0].astype(jnp.bfloat16), outputs[1].astype(jnp.bfloat16), grad_frames, grad_codes, frame_grads[0], frame_grads[1], frame_grads[2], frame_grads[3], frame_grads[4], frame_grads[5], frame_grads[6], frame_grads[7], frame_grads[8], frame_grads[9], code_grads[0], code_grads[1], code_grads[2], code_grads[3], code_grads[4], code_grads[5], code_grads[6], code_grads[7], code_grads[8], code_grads[9])
```

```python
import functools

import jax
import jax.numpy as jnp
from jax import lax
from jax.sharding import PartitionSpec as P

D = 1024
HEADS = 16
HD = 64
CB = 3


def gelu_tanh(value):
    return (
        0.5
        * value
        * (1.0 + jnp.tanh(0.7978845608028654 * (value + 0.044715 * value * value * value)))
    )


def rms_scale(value, gain_vec):
    return value * lax.rsqrt(jnp.mean(value * value, axis=-1, keepdims=True) + 1e-05) * gain_vec


def over_rows(left, right):
    return lax.dot_general(
        left, right, (((0,), (0,)), ((), ())), preferred_element_type=jnp.float32
    )


def against(left, right):
    return lax.dot_general(
        left, right, (((1,), (1,)), ((), ())), preferred_element_type=jnp.float32
    )


def masked_scores(query, key_rows, allowed):
    scores = jnp.einsum(
        "glhe,gmhe->ghlm", query, key_rows, preferred_element_type=jnp.float32
    ) * HD ** (-0.5)
    return jnp.where(allowed[:, None], scores, -1e30)


def attend(query, key_rows, value_rows, allowed):
    scores = masked_scores(query, key_rows, allowed)
    highest = jnp.max(scores, axis=-1, keepdims=True)
    expo = jnp.exp(scores - highest)
    totals = jnp.sum(expo, axis=-1, keepdims=True)
    probs = expo / totals
    log_total = highest + jnp.log(totals)
    mixed = jnp.einsum(
        "ghlm,gmhe->glhe",
        probs.astype(jnp.bfloat16),
        value_rows,
        preferred_element_type=jnp.float32,
    )
    return (mixed.astype(jnp.bfloat16), log_total)


def attend_back(query, key_rows, value_rows, allowed, log_total, grad_mixed):
    probs = jnp.exp(masked_scores(query, key_rows, allowed) - log_total)
    grad_probs = jnp.einsum(
        "glhe,gmhe->ghlm", grad_mixed, value_rows, preferred_element_type=jnp.float32
    )
    grad_values = jnp.einsum(
        "ghlm,glhe->gmhe",
        probs.astype(jnp.bfloat16),
        grad_mixed,
        preferred_element_type=jnp.float32,
    )
    inner = jnp.sum(probs * grad_probs, axis=-1, keepdims=True)
    grad_scores = (probs * (grad_probs - inner)).astype(jnp.bfloat16)
    grad_query = jnp.einsum(
        "ghlm,gmhe->glhe", grad_scores, key_rows, preferred_element_type=jnp.float32
    ) * HD ** (-0.5)
    grad_keys = jnp.einsum(
        "ghlm,glhe->gmhe", grad_scores, query, preferred_element_type=jnp.float32
    ) * HD ** (-0.5)
    return (grad_query, grad_keys, grad_values)


def bit_list(sizes):
    found = []
    for axis, size in zip(("gx", "gy"), sizes):
        step = size // 2
        while step >= 1:
            found.append((axis, step, size))
            step //= 2
    return found


def gather_order(sizes, flip):
    names = bit_list(sizes)
    gx_bits = [pos for pos, item in enumerate(names) if item[0] == "gx"]
    gy_bits = [pos for pos, item in enumerate(names) if item[0] == "gy"]
    near = gy_bits[-2:]
    if flip:
        near = near[::-1]
    return gx_bits[:-1] + gy_bits[:-2] + near + gx_bits[-1:]


def swap(value, item):
    axis, step, size = item
    return lax.ppermute(value, axis, [(place, place ^ step) for place in range(size)])


def own_bit(item):
    axis, step, size = item
    return (lax.axis_index(axis) // step) % 2


def spans(done, pos, names):
    high = 2 ** sum(1 for other in done if other < pos)
    low = 2 ** sum(1 for other in done if other > pos)
    return high, low


def gather_step(state, done, pos, names):
    item = names[pos]
    high, low = spans(done, pos, names)
    group, blocks, rows, cols = state.shape
    received = swap(state, item)
    bit = own_bit(item)
    wide = jnp.zeros((group, high, 2, low, rows, cols), state.dtype)
    zero = jnp.zeros((), bit.dtype)
    mine = state.reshape(group, high, 1, low, rows, cols)
    theirs = received.reshape(group, high, 1, low, rows, cols)
    wide = lax.dynamic_update_slice(wide, mine, (zero, zero, bit, zero, zero, zero))
    wide = lax.dynamic_update_slice(wide, theirs, (zero, zero, 1 - bit, zero, zero, zero))
    return wide.reshape(group, blocks * 2, rows, cols), received


def gather_run(state, done, order, names):
    received = None
    for pos in order:
        state, received = gather_step(state, done, pos, names)
        done = done + [pos]
    return state, done, received


def scatter_run(state, order, names, last_type):
    left = sorted(order)
    for index, pos in enumerate(order):
        item = names[pos]
        left = [other for other in left if other != pos]
        high, low = spans(left, pos, names)
        blocks, rows, cols = state.shape
        view = state.reshape(high, 2, low, rows, cols)
        bit = own_bit(item)
        away = lax.dynamic_index_in_dim(view, 1 - bit, 1, keepdims=False)
        kept = lax.dynamic_index_in_dim(view, bit, 1, keepdims=False)
        received = swap(away, item)
        total = kept.astype(jnp.float32) + received.astype(jnp.float32)
        if index < len(order) - 1:
            total = total.astype(state.dtype)
        else:
            total = total.astype(last_type)
        state = total.reshape(blocks // 2, rows, cols)
    return state[0]


def gather_many(shards, sizes, flips, gate):
    names = bit_list(sizes)
    state = jnp.stack(shards)[:, None]
    if gate is not None:
        state, unused = lax.optimization_barrier((state, gate))
    orders = [gather_order(sizes, flip) for flip in (False, True)]
    shared = len(orders[0]) - 3
    state, done, received = gather_run(state, [], orders[0][:shared], names)
    token = received[:1, :1, :1, :1]
    parts = []
    start = 0
    for flip in (False, True):
        count = sum(1 for other in flips if other == flip)
        if count == 0:
            continue
        part = state[start : start + count]
        start += count
        part, part_done, unused = gather_run(part, done, orders[int(flip)][shared:], names)
        for index in range(count):
            whole = part[index]
            parts.append(whole.reshape(-1, whole.shape[-1]))
    return parts, token


def scatter_one(grad, sizes, flip):
    names = bit_list(sizes)
    count = 2 ** len(names)
    order = gather_order(sizes, flip)[::-1]
    return scatter_run(
        grad.reshape(count, grad.shape[0] // count, grad.shape[1]), order, names, jnp.float32
    )


def block_forward(x_in, allowed, gains, weights, groups):
    prenorm, midnorm, b_up, b_down = gains
    w_query, w_key, w_value, w_out, w_up, w_down = weights
    row_count = x_in.shape[0]
    span = row_count // groups
    normed = rms_scale(x_in, prenorm).astype(jnp.bfloat16)
    query = (
        jnp.dot(normed, w_query, preferred_element_type=jnp.float32)
        .astype(jnp.bfloat16)
        .reshape(groups, span, HEADS, HD)
    )
    key_rows = (
        jnp.dot(normed, w_key, preferred_element_type=jnp.float32)
        .astype(jnp.bfloat16)
        .reshape(groups, span, HEADS, HD)
    )
    value_rows = (
        jnp.dot(normed, w_value, preferred_element_type=jnp.float32)
        .astype(jnp.bfloat16)
        .reshape(groups, span, HEADS, HD)
    )
    mixed_heads, log_total = attend(query, key_rows, value_rows, allowed)
    mixed = mixed_heads.reshape(row_count, D)
    hidden = x_in + jnp.dot(mixed, w_out, preferred_element_type=jnp.float32)
    normed_two = rms_scale(hidden, midnorm).astype(jnp.bfloat16)
    preact = jnp.dot(normed_two, w_up, preferred_element_type=jnp.float32) + b_up
    activated = gelu_tanh(preact).astype(jnp.bfloat16)
    result = hidden + (jnp.dot(activated, w_down, preferred_element_type=jnp.float32) + b_down)
    saved = (
        normed,
        query,
        key_rows,
        value_rows,
        log_total,
        mixed,
        hidden,
        normed_two,
        preact,
        activated,
    )
    return (result, saved)


def block_backward(grad_y, x_in, allowed, gains, weights, saved, sizes):
    prenorm, midnorm, b_up, b_down = gains
    w_query, w_key, w_value, w_out, w_up, w_down = weights
    normed, query, key_rows, value_rows, log_total, mixed, hidden, normed_two, preact, activated = (
        saved
    )
    row_count = x_in.shape[0]
    low = jnp.bfloat16
    grad_branch = grad_y.astype(jnp.bfloat16)
    grad_b_down = jnp.sum(grad_branch.astype(jnp.float32), axis=0)
    shard_down = scatter_one(over_rows(activated, grad_branch).astype(low), sizes, True)
    grad_act = against(grad_branch, w_down)
    unused_value, gelu_back = jax.vjp(gelu_tanh, preact)
    grad_pre = gelu_back(grad_act)[0].astype(jnp.bfloat16)
    grad_b_up = jnp.sum(grad_pre.astype(jnp.float32), axis=0)
    shard_up = scatter_one(over_rows(normed_two, grad_pre).astype(low), sizes, False)
    grad_normed_two = against(grad_pre, w_up)
    unused_mid, mid_back = jax.vjp(rms_scale, hidden, midnorm)
    grad_hidden_part, grad_midnorm = mid_back(grad_normed_two)
    grad_hidden = grad_y + grad_hidden_part
    grad_attn = grad_hidden.astype(jnp.bfloat16)
    grad_w_out = over_rows(mixed, grad_attn)
    grad_mixed = against(grad_attn, w_out).astype(jnp.bfloat16)
    grad_query, grad_keys, grad_values = attend_back(
        query, key_rows, value_rows, allowed, log_total, grad_mixed.reshape(query.shape)
    )
    grad_query = grad_query.reshape(row_count, D).astype(jnp.bfloat16)
    grad_keys = grad_keys.reshape(row_count, D).astype(jnp.bfloat16)
    grad_values = grad_values.reshape(row_count, D).astype(jnp.bfloat16)
    pair = jnp.concatenate([grad_query, grad_keys], axis=1)
    shard_pair = scatter_one(over_rows(normed, pair).astype(low), sizes, False)
    grad_w_value = over_rows(normed, grad_values)
    other = jnp.concatenate([grad_w_value.astype(low), grad_w_out.astype(low)], axis=1)
    shard_other = scatter_one(other, sizes, True)
    grad_normed = (
        against(grad_query, w_query) + against(grad_keys, w_key) + against(grad_values, w_value)
    )
    unused_pre, pre_back = jax.vjp(rms_scale, x_in, prenorm)
    grad_x_part, grad_prenorm = pre_back(grad_normed)
    grad_x = grad_hidden + grad_x_part
    shards = (
        shard_pair[:, :D],
        shard_pair[:, D:],
        shard_other[:, :D],
        shard_other[:, D:],
        shard_up,
        shard_down,
    )
    return (grad_x, shards, (grad_prenorm, grad_midnorm, grad_b_up, grad_b_down))


def local(
    sizes,
    frame_input,
    code_embed,
    segment_ids,
    frame_cotangent,
    code_cotangent,
    frame_prenorm,
    frame_query,
    frame_keys,
    frame_values,
    frame_outproj,
    frame_midnorm,
    frame_upproj,
    frame_upbias,
    frame_downproj,
    frame_downbias,
    code_prenorm,
    code_query,
    code_keys,
    code_values,
    code_outproj,
    code_midnorm,
    code_upproj,
    code_upbias,
    code_downproj,
    code_downbias,
):
    frame_count = frame_input.shape[0]
    names = bit_list(sizes)
    devices = 2 ** len(names)
    vectors = (
        frame_prenorm,
        frame_midnorm,
        frame_upbias,
        frame_downbias,
        code_prenorm,
        code_midnorm,
        code_upbias,
        code_downbias,
    )
    widths = [vec.shape[0] for vec in vectors]
    packed = jnp.concatenate(vectors)[None, None, None, :]
    whole, unused, unused_two = gather_run(packed, [], gather_order(sizes, False), names)
    whole = whole.reshape(devices, -1).astype(jnp.float32)
    gains = []
    start = 0
    for width in widths:
        gains.append(whole[:, start : start + width].reshape(devices * width))
        start += width
    order = (False, False, True, True)
    (fq, fk, fv, fo), token = gather_many(
        [frame_query, frame_keys, frame_values, frame_outproj], sizes, order, None
    )
    (fu,), token_up = gather_many([frame_upproj], sizes, (False,), token)
    (fd,), token_down = gather_many([frame_downproj], sizes, (True,), token)
    (cq, ck, cv, co), token = gather_many(
        [code_query, code_keys, code_values, code_outproj], sizes, order, (token_up, token_down)
    )
    (cu,), unused = gather_many([code_upproj], sizes, (False,), token)
    (cd,), unused = gather_many([code_downproj], sizes, (True,), token)
    frame_weights = (fq, fk, fv, fo, fu, fd)
    code_weights = (cq, ck, cv, co, cu, cd)
    frame_gains = tuple(gains[:4])
    code_gains = tuple(gains[4:])
    place = jnp.arange(frame_count)
    segment_row = segment_ids[0]
    frame_allowed = (
        (segment_row[:, None] == segment_row[None, :]) & (place[:, None] >= place[None, :])
    )[None]
    frame_x = frame_input.astype(jnp.float32)
    frame_out, frame_saved = block_forward(frame_x, frame_allowed, frame_gains, frame_weights, 1)
    code_in = (code_embed.astype(jnp.float32) + frame_out[:, None, :]).reshape(frame_count * CB, D)
    code_place = jnp.arange(CB)
    code_allowed = (code_place[:, None] >= code_place[None, :])[None]
    code_out, code_saved = block_forward(
        code_in, code_allowed, code_gains, code_weights, frame_count
    )
    grad_code_in, code_shards, code_vectors = block_backward(
        code_cotangent.astype(jnp.float32).reshape(frame_count * CB, D),
        code_in,
        code_allowed,
        code_gains,
        code_weights,
        code_saved,
        sizes,
    )
    grad_code_rows = grad_code_in.reshape(frame_count, CB, D)
    frame_grad_y = frame_cotangent.astype(jnp.float32) + jnp.sum(grad_code_rows, axis=1)
    grad_frame_in, frame_shards, frame_vectors = block_backward(
        frame_grad_y,
        frame_x,
        frame_allowed,
        frame_gains,
        frame_weights,
        frame_saved,
        sizes,
    )
    terms = jnp.concatenate(
        [
            grad_vec.reshape(devices, -1)
            for grad_vec in tuple(frame_vectors) + tuple(code_vectors)
        ],
        axis=1,
    )[:, None, :]
    sums = scatter_run(terms, gather_order(sizes, False)[::-1], names, jnp.float32)[0]
    vector_shards = []
    start = 0
    for width in widths:
        vector_shards.append(sums[start : start + width])
        start += width

    def arranged(shards, vecs):
        query, keys, values, outproj, upproj, downproj = shards
        prenorm, midnorm, upbias, downbias = vecs
        return (
            prenorm,
            query,
            keys,
            values,
            outproj,
            midnorm,
            upproj,
            upbias,
            downproj,
            downbias,
        )

    return (
        (
            frame_out.astype(jnp.bfloat16),
            code_out.reshape(frame_count, CB, D).astype(jnp.bfloat16),
            grad_frame_in,
            grad_code_rows,
        )
        + arranged(frame_shards, vector_shards[:4])
        + arranged(code_shards, vector_shards[4:])
    )


def solution(mesh):
    in_specs = (
        P(("gx", "gy"), None),
        P(("gx", "gy"), None, None),
        P(("gx", "gy"), None),
        P(("gx", "gy"), None),
        P(("gx", "gy"), None, None),
        P(("gx", "gy")),
        P(("gx", "gy"), None),
        P(("gx", "gy"), None),
        P(("gx", "gy"), None),
        P(("gx", "gy"), None),
        P(("gx", "gy")),
        P(("gx", "gy"), None),
        P(("gx", "gy")),
        P(("gx", "gy"), None),
        P(("gx", "gy")),
        P(("gx", "gy")),
        P(("gx", "gy"), None),
        P(("gx", "gy"), None),
        P(("gx", "gy"), None),
        P(("gx", "gy"), None),
        P(("gx", "gy")),
        P(("gx", "gy"), None),
        P(("gx", "gy")),
        P(("gx", "gy"), None),
        P(("gx", "gy")),
    )
    out_specs = (
        P(("gx", "gy"), None),
        P(("gx", "gy"), None, None),
        P(("gx", "gy"), None),
        P(("gx", "gy"), None, None),
        P(("gx", "gy")),
        P(("gx", "gy"), None),
        P(("gx", "gy"), None),
        P(("gx", "gy"), None),
        P(("gx", "gy"), None),
        P(("gx", "gy")),
        P(("gx", "gy"), None),
        P(("gx", "gy")),
        P(("gx", "gy"), None),
        P(("gx", "gy")),
        P(("gx", "gy")),
        P(("gx", "gy"), None),
        P(("gx", "gy"), None),
        P(("gx", "gy"), None),
        P(("gx", "gy"), None),
        P(("gx", "gy")),
        P(("gx", "gy"), None),
        P(("gx", "gy")),
        P(("gx", "gy"), None),
        P(("gx", "gy")),
    )
    sizes = (mesh.shape["gx"], mesh.shape["gy"])
    return jax.shard_map(
        functools.partial(local, sizes), mesh=mesh, in_specs=in_specs, out_specs=out_specs, check_vma=False)
```

```python
import functools
import math

import jax
import jax.numpy as jnp
from jax import lax
from jax.experimental import pallas as pl
from jax.experimental.pallas import tpu as pltpu
from jax.sharding import PartitionSpec as P

D = 1024
HEADS = 16
HD = 64
CB = 3
LIGHT = pl.CostEstimate(flops=1, bytes_accessed=1, transcendentals=0)


def gelu_tanh(value):
    return (
        0.5
        * value
        * (1.0 + jnp.tanh(0.7978845608028654 * (value + 0.044715 * value * value * value)))
    )


def rms_scale(value, gain_vec):
    return value * lax.rsqrt(jnp.mean(value * value, axis=-1, keepdims=True) + 1e-05) * gain_vec


def over_rows(left, right):
    return lax.dot_general(
        left, right, (((0,), (0,)), ((), ())), preferred_element_type=jnp.float32
    )


def against(left, right):
    return lax.dot_general(
        left, right, (((1,), (1,)), ((), ())), preferred_element_type=jnp.float32
    )


def head_marks():
    lane = lax.broadcasted_iota(jnp.int32, (D, 128), 0) // HD
    head = lax.broadcasted_iota(jnp.int32, (D, 128), 1)
    return (lane == head).astype(jnp.bfloat16)


def head_sums(left, right, marks):
    product = left.astype(jnp.float32) * right.astype(jnp.float32)
    upper = product.astype(jnp.bfloat16)
    lower = (product - upper.astype(jnp.float32)).astype(jnp.bfloat16)
    return jnp.dot(upper, marks, preferred_element_type=jnp.float32) + jnp.dot(
        lower, marks, preferred_element_type=jnp.float32
    )


def spread(heads, marks):
    return lax.dot_general(
        heads, marks, (((1,), (1,)), ((), ())), preferred_element_type=jnp.float32
    )


def token_probs(tokens_q, tokens_k, marks):
    probs = []
    for token in range(CB):
        scores = [
            head_sums(tokens_q[token], tokens_k[other], marks) * HD ** (-0.5)
            for other in range(token + 1)
        ]
        highest = functools.reduce(jnp.maximum, scores)
        expo = [jnp.exp(score - highest) for score in scores]
        total = functools.reduce(jnp.add, expo)
        probs.append([term / total for term in expo])
    return probs


def code_attend_kernel(pair_ref, values_ref, marks_ref, out_ref):
    marks = marks_ref[...]
    query = [pair_ref[token, :, :D] for token in range(CB)]
    keys = [pair_ref[token, :, D:] for token in range(CB)]
    probs = token_probs(query, keys, marks)
    for token in range(CB):
        mixed = None
        for other in range(token + 1):
            value = values_ref[other].astype(jnp.float32)
            term = spread(probs[token][other].astype(jnp.bfloat16), marks) * value
            mixed = term if mixed is None else mixed + term
        out_ref[token] = mixed.astype(jnp.bfloat16)


def code_attend_back_kernel(
    pair_ref, values_ref, grad_ref, marks_ref, out_pair_ref, out_values_ref
):
    marks = marks_ref[...]
    query = [pair_ref[token, :, :D] for token in range(CB)]
    keys = [pair_ref[token, :, D:] for token in range(CB)]
    probs = token_probs(query, keys, marks)
    grad_scores = []
    for token in range(CB):
        grads = [
            head_sums(grad_ref[token], values_ref[other], marks)
            for other in range(token + 1)
        ]
        inner = functools.reduce(
            jnp.add, [prob * grad for prob, grad in zip(probs[token], grads)]
        )
        grad_scores.append(
            [
                (prob * (grad - inner)).astype(jnp.bfloat16)
                for prob, grad in zip(probs[token], grads)
            ]
        )
    scale = HD ** (-0.5)
    grad_keys = [None] * CB
    grad_values = [None] * CB
    for token in range(CB):
        grad_query = None
        for other in range(token + 1):
            wide = spread(grad_scores[token][other], marks)
            term = wide * keys[other].astype(jnp.float32)
            grad_query = term if grad_query is None else grad_query + term
            term = wide * query[token].astype(jnp.float32)
            grad_keys[other] = term if grad_keys[other] is None else grad_keys[other] + term
            wide = spread(probs[token][other].astype(jnp.bfloat16), marks)
            term = wide * grad_ref[token].astype(jnp.float32)
            grad_values[other] = term if grad_values[other] is None else grad_values[other] + term
        out_pair_ref[token, :, :D] = (grad_query * scale).astype(jnp.bfloat16)
    for token in range(CB):
        out_pair_ref[token, :, D:] = (grad_keys[token] * scale).astype(jnp.bfloat16)
        out_values_ref[token] = grad_values[token].astype(jnp.bfloat16)


def token_specs(step, widths):
    return [pl.BlockSpec((CB, step, width), lambda i: (0, i, 0)) for width in widths] + [
        pl.BlockSpec((D, 128), lambda i: (0, 0))
    ]


def code_attend(pair, values):
    frames = values.shape[1]
    step = math.gcd(frames, 64)
    return pl.pallas_call(
        code_attend_kernel,
        grid=(frames // step,),
        in_specs=token_specs(step, (2 * D, D)),
        out_specs=pl.BlockSpec((CB, step, D), lambda i: (0, i, 0)),
        out_shape=jax.ShapeDtypeStruct((CB, frames, D), jnp.bfloat16),
        cost_estimate=LIGHT,
        name="code_attend",
    )(pair, values, head_marks())


def code_attend_back(pair, values, grad_mixed):
    frames = values.shape[1]
    step = math.gcd(frames, 64)
    return pl.pallas_call(
        code_attend_back_kernel,
        grid=(frames // step,),
        in_specs=token_specs(step, (2 * D, D, D)),
        out_specs=[
            pl.BlockSpec((CB, step, 2 * D), lambda i: (0, i, 0)),
            pl.BlockSpec((CB, step, D), lambda i: (0, i, 0)),
        ],
        out_shape=[
            jax.ShapeDtypeStruct((CB, frames, 2 * D), jnp.bfloat16),
            jax.ShapeDtypeStruct((CB, frames, D), jnp.bfloat16),
        ],
        cost_estimate=LIGHT,
        name="code_attend_back",
    )(pair, values, grad_mixed, head_marks())


def frame_mask(column_ref, row_ref):
    frames = column_ref.shape[0]
    shape = (frames, frames)
    earlier = lax.broadcasted_iota(jnp.int32, shape, 0) >= lax.broadcasted_iota(
        jnp.int32, shape, 1
    )
    return earlier & (column_ref[...] == row_ref[...])


def frame_probs(query, keys, allowed):
    scores = against(query, keys) * HD ** (-0.5)
    scores = jnp.where(allowed, scores, -1e30)
    highest = jnp.max(scores, axis=-1, keepdims=True)
    expo = jnp.exp(scores - highest)
    return expo / jnp.sum(expo, axis=-1, keepdims=True)


def half_lanes(value, upper):
    lane = lax.broadcasted_iota(jnp.int32, value.shape, 1)
    chosen = (lane >= HD) if upper else (lane < HD)
    return jnp.where(chosen, value, jnp.zeros_like(value))


def frame_attend_kernel(query_ref, keys_ref, values_ref, column_ref, row_ref, out_ref):
    allowed = frame_mask(column_ref, row_ref)
    mixed = None
    for upper in (False, True):
        probs = frame_probs(half_lanes(query_ref[...], upper), keys_ref[...], allowed)
        term = jnp.dot(
            probs.astype(jnp.bfloat16),
            half_lanes(values_ref[...], upper),
            preferred_element_type=jnp.float32,
        )
        mixed = term if mixed is None else mixed + term
    out_ref[...] = mixed.astype(jnp.bfloat16)


def frame_attend_back_kernel(
    query_ref, keys_ref, values_ref, grad_ref, column_ref, row_ref, out_pair_ref, out_values_ref
):
    allowed = frame_mask(column_ref, row_ref)
    scale = HD ** (-0.5)
    grads = [None, None, None]
    for upper in (False, True):
        query = half_lanes(query_ref[...], upper)
        keys = half_lanes(keys_ref[...], upper)
        grad_out = half_lanes(grad_ref[...], upper)
        probs = frame_probs(query, keys, allowed)
        grad_probs = against(grad_out, values_ref[...])
        inner = jnp.sum(probs * grad_probs, axis=-1, keepdims=True)
        grad_scores = (probs * (grad_probs - inner)).astype(jnp.bfloat16)
        terms = (
            jnp.dot(grad_scores, keys, preferred_element_type=jnp.float32) * scale,
            over_rows(grad_scores, query) * scale,
            over_rows(probs.astype(jnp.bfloat16), grad_out),
        )
        grads = [term if grad is None else grad + term for grad, term in zip(grads, terms)]
    start = pl.multiple_of(pl.program_id(0) * 2 * HD, 2 * HD)
    out_pair_ref[:, pl.ds(start, 2 * HD)] = grads[0].astype(jnp.bfloat16)
    out_pair_ref[:, pl.ds(D + start, 2 * HD)] = grads[1].astype(jnp.bfloat16)
    out_values_ref[...] = grads[2].astype(jnp.bfloat16)


def pair_specs(frames, extra):
    pairs = HEADS // 2
    block = (frames, 2 * HD)
    return (
        [
            pl.BlockSpec(block, lambda j: (0, j)),
            pl.BlockSpec(block, lambda j: (0, j + pairs)),
        ]
        + [pl.BlockSpec(block, lambda j: (0, j))] * extra
        + [
            pl.BlockSpec((frames, 1), lambda j: (0, 0)),
            pl.BlockSpec((1, frames), lambda j: (0, 0)),
        ]
    )


def frame_attend(pair, values, segments):
    frames = values.shape[0]
    return pl.pallas_call(
        frame_attend_kernel,
        grid=(HEADS // 2,),
        in_specs=pair_specs(frames, 1),
        out_specs=pl.BlockSpec((frames, 2 * HD), lambda j: (0, j)),
        out_shape=jax.ShapeDtypeStruct((frames, D), jnp.bfloat16),
        cost_estimate=LIGHT,
        name="frame_attend",
    )(pair, pair, values, segments.reshape(frames, 1), segments.reshape(1, frames))


def frame_attend_back(pair, values, grad_mixed, segments):
    frames = values.shape[0]
    return pl.pallas_call(
        frame_attend_back_kernel,
        grid=(HEADS // 2,),
        in_specs=pair_specs(frames, 2),
        out_specs=[
            pl.BlockSpec((frames, 2 * D), lambda j: (0, 0)),
            pl.BlockSpec((frames, 2 * HD), lambda j: (0, j)),
        ],
        out_shape=[
            jax.ShapeDtypeStruct((frames, 2 * D), jnp.bfloat16),
            jax.ShapeDtypeStruct((frames, D), jnp.bfloat16),
        ],
        cost_estimate=LIGHT,
        name="frame_attend_back",
    )(
        pair,
        pair,
        values,
        grad_mixed,
        segments.reshape(frames, 1),
        segments.reshape(1, frames),
    )


def bit_masks(sizes):
    count = sizes[0] * sizes[1]
    masks = []
    step = count // 2
    while step >= 1:
        masks.append(step)
        step //= 2
    return masks, masks.index(sizes[1])


def swap(value, mask, sizes):
    count = sizes[0] * sizes[1]
    return lax.ppermute(value, ("gx", "gy"), [(place, place ^ mask) for place in range(count)])


def device_index(sizes):
    return lax.axis_index("gx") * sizes[1] + lax.axis_index("gy")


def far_groups(sizes):
    masks, core = bit_masks(sizes)
    far = [mask for place, mask in enumerate(masks[:-2]) if place != core]
    return [far[start : start + 2] for start in range(0, len(far), 2)]


def combined(group):
    found = []
    for index in range(2 ** len(group)):
        mask = 0
        for place, bit in enumerate(group):
            if (index >> (len(group) - 1 - place)) & 1:
                mask |= bit
        found.append(mask)
    return found


def small_index(group, sizes):
    me = device_index(sizes)
    index = jnp.zeros((), jnp.int32)
    for bit in group:
        index = index * 2 + ((me // bit) % 2).astype(jnp.int32)
    return index


def place_far_kernel(place_ref, *refs):
    for index, ref in enumerate(refs[:-1]):
        refs[-1][0, place_ref[0] ^ index] = ref[0]


def placed_far(pieces, place):
    planes, rows, cols = pieces[0].shape
    slots = len(pieces)
    return pl.pallas_call(
        place_far_kernel,
        grid_spec=pltpu.PrefetchScalarGridSpec(
            num_scalar_prefetch=1,
            grid=(planes,),
            in_specs=[pl.BlockSpec((1, rows, cols), lambda i, place_ref: (i, 0, 0))] * slots,
            out_specs=pl.BlockSpec((1, slots, rows, cols), lambda i, place_ref: (i, 0, 0, 0)),
        ),
        out_shape=jax.ShapeDtypeStruct((planes, slots, rows, cols), pieces[0].dtype),
        cost_estimate=LIGHT,
        name="place_far",
    )(place.reshape(1), *pieces)


def place_near_kernel(place_ref, *refs):
    for index, ref in enumerate(refs[:-1]):
        refs[-1][0, place_ref[1] ^ (index // 4), 0, place_ref[0] ^ (index % 4)] = ref[0]


def place_near_tail_kernel(place_ref, *refs):
    cols = refs[-2].shape[-1]
    for index, ref in enumerate(refs[:-2]):
        slot = (0, place_ref[1] ^ (index // 4), 0, place_ref[0] ^ (index % 4))
        refs[-2][slot] = ref[0, :, :cols]
        refs[-1][slot] = ref[0, :, cols:]


def placed_near(pieces, near_place, core_place, group, high, low, tail):
    rows, cols = pieces[0].shape[1:]
    widths = [cols - tail, tail] if tail else [cols]
    offset = group * high * low
    outs = pl.pallas_call(
        place_near_tail_kernel if tail else place_near_kernel,
        grid_spec=pltpu.PrefetchScalarGridSpec(
            num_scalar_prefetch=1,
            grid=(high * low,),
            in_specs=[pl.BlockSpec((1, rows, cols), lambda i, place_ref: (i + offset, 0, 0))] * 8,
            out_specs=[
                pl.BlockSpec(
                    (1, 2, 1, 4, rows, width),
                    lambda i, place_ref: (i // low, 0, i % low, 0, 0, 0),
                )
                for width in widths
            ],
        ),
        out_shape=[
            jax.ShapeDtypeStruct((high, 2, low, 4, rows, width), pieces[0].dtype)
            for width in widths
        ],
        cost_estimate=LIGHT,
        name="place_near",
    )(jnp.stack([near_place, core_place]), *pieces)
    return [out.reshape(high * 2 * low * 4 * rows, out.shape[-1]) for out in outs]


def pinned(*values):
    return lax.optimization_barrier(values)


class Gather:
    def __init__(self, shard, sizes, flip, tail=0):
        self.sizes = sizes
        self.tail = tail
        self.groups, self.rows, self.cols = shard.shape
        self.state = shard
        self.far = far_groups(sizes)
        masks, core = bit_masks(sizes)
        self.near = masks[-2:]
        self.first, self.second = (2, 1) if not flip else (1, 2)
        self.core = masks[core]
        self.high = 2**core
        self.low = 2 ** (len(masks) - core - 3)
        self.pieces = None
        self.received = None
        self.stage = -len(self.far)

    def flown(self, value, mask):
        return swap(value, mask, self.sizes)

    def send(self):
        if self.stage < 0:
            masks = combined(self.far[self.stage])
            self.received = [self.flown(self.state, mask) for mask in masks[1:]]
        elif self.stage == 0:
            mask = combined(self.near)[self.first]
            self.received = [self.flown(self.pieces[0], mask)]
        elif self.stage == 1:
            mask = combined(self.near)[self.second]
            self.received = [self.flown(self.pieces[index], mask) for index in (0, self.first)]
        else:
            self.received = [self.flown(piece, self.core) for piece in self.pieces]

    def take(self):
        if self.stage < 0:
            group = self.far[self.stage]
            wide = placed_far(
                [
                    value.reshape(-1, self.rows, self.cols)
                    for value in [self.state] + list(self.received)
                ],
                small_index(group, self.sizes),
            )
            self.state = wide.reshape(-1, self.rows, self.cols)
            if self.stage == -1:
                self.pieces = [self.state, None, None, None]
        elif self.stage == 0:
            self.pieces[self.first] = self.received[0]
        elif self.stage == 1:
            self.pieces[self.second] = self.received[0]
            self.pieces[3] = self.received[1]
        else:
            near_place = small_index(self.near, self.sizes)
            core_place = small_index([self.core], self.sizes)
            outs = [
                placed_near(
                    self.pieces + list(self.received),
                    near_place,
                    core_place,
                    group,
                    self.high,
                    self.low,
                    self.tail,
                )
                for group in range(self.groups)
            ]
            self.whole = [out[0] for out in outs]
            self.tails = [out[-1] for out in outs]
        self.received = None
        self.stage += 1


def ended(chains, *others):
    flat = [value for chain in chains for value in chain.received]
    held = list(pinned(*flat, *others))
    for chain in chains:
        count = len(chain.received)
        chain.received, held = held[:count], held[count:]
        chain.take()
    return held


def started(chains):
    for chain in chains:
        chain.send()


def half_kernel(side_ref, acts_ref, grad_ref, out_ref):
    out_ref[...] = over_rows(acts_ref[...], grad_ref[...]).astype(jnp.bfloat16)


def half_add_kernel(side_ref, acts_ref, grad_ref, add_ref, out_ref):
    total = over_rows(acts_ref[...], grad_ref[...]) + add_ref[...].astype(jnp.float32)
    out_ref[...] = total.astype(jnp.bfloat16)


def half_product(acts, grad, sizes, received):
    masks, core = bit_masks(sizes)
    rows, inner = acts.shape
    cols = grad.shape[1]
    segment = inner // (2 * 2**core)
    tile = math.gcd(segment, 512)
    parts = segment // tile
    wide = math.gcd(cols, 1024)
    side = small_index([masks[core]], sizes)
    if received is None:
        side = 1 - side

    def acts_at(i, j, side_ref):
        return (0, (i // parts) * 2 * parts + side_ref[0] * parts + i % parts)

    specs = [
        pl.BlockSpec((rows, tile), acts_at),
        pl.BlockSpec((rows, wide), lambda i, j, side_ref: (0, j)),
    ]
    out_spec = pl.BlockSpec((tile, wide), lambda i, j, side_ref: (i, j))
    operands = [acts, grad]
    if received is not None:
        specs.append(out_spec)
        operands.append(received)
    return pl.pallas_call(
        half_kernel if received is None else half_add_kernel,
        grid_spec=pltpu.PrefetchScalarGridSpec(
            num_scalar_prefetch=1,
            grid=(inner // (2 * tile), cols // wide),
            in_specs=specs,
            out_specs=out_spec,
        ),
        out_shape=jax.ShapeDtypeStruct((inner // 2, cols), jnp.bfloat16),
        cost_estimate=LIGHT,
        name="half_away" if received is None else "half_kept",
    )(side.reshape(1), *operands)


class Core:
    def __init__(self, acts, grad, sizes):
        masks, core = bit_masks(sizes)
        self.mask, self.sizes = masks[core], sizes
        self.acts, self.grad = acts, grad
        self.away = [half_product(acts, grad, sizes, None)]
        self.received = None
        self.theirs = None

    def send(self):
        self.received = [swap(self.away[0], self.mask, self.sizes)]

    def take(self):
        self.theirs = self.received[0]
        self.received = None
        self.away = []


class Scatter:
    def __init__(self, states, sizes, flip):
        self.sizes = sizes
        masks, core = bit_masks(sizes)
        self.bits = [mask for place, mask in enumerate(masks) if place != core]
        first, second = masks[-1], masks[-2]
        if flip:
            first, second = second, first
        self.todo = [[first], [second]] + far_groups(sizes)[::-1]
        count = 2 ** len(self.bits)
        self.states = [
            state.reshape(count, state.shape[0] // count, state.shape[1]) for state in states
        ]
        self.received = None
        self.prepare()

    def prepare(self):
        group = self.todo[0]
        first = self.bits.index(group[0])
        self.bits = [bit for bit in self.bits if bit not in group]
        slots = 2 ** len(group)
        high = 2**first
        place = small_index(group, self.sizes)
        self.kept = []
        aways = []
        for state in self.states:
            blocks, rows, cols = state.shape
            view = state.reshape(high, slots, blocks // (high * slots), rows, cols)
            parts = [
                lax.dynamic_index_in_dim(view, place ^ index, 1, keepdims=False).reshape(
                    blocks // slots, rows, cols
                )
                for index in range(slots)
            ]
            self.kept.append(parts[0])
            aways.append(parts[1:])
        self.away = [
            jnp.stack([away[index] for away in aways]) for index in range(slots - 1)
        ]
        self.todo = self.todo[1:]
        self.masks = combined(group)[1:]

    def send(self):
        self.received = [swap(away, mask, self.sizes) for away, mask in zip(self.away, self.masks)]

    def take(self):
        last = not self.todo
        self.states = []
        for index, kept in enumerate(self.kept):
            total = kept.astype(jnp.float32)
            for value in self.received:
                total = total + value[index].astype(jnp.float32)
            self.states.append(total.astype(jnp.float32 if last else jnp.bfloat16))
        self.received = None
        self.away = []
        if not last:
            self.prepare()


def split_kernel(flip, side_ref, acts_ref, grad_ref, add_ref, kept_ref, away_ref):
    total = over_rows(acts_ref[...], grad_ref[...]) + add_ref[...].astype(jnp.float32)
    half, rows, cols = kept_ref.shape
    total = total.astype(jnp.bfloat16)
    parts = [[], []]
    for index in range(2 * half):
        bit = (index // 2) % 2 if flip else index % 2
        parts[bit].append(total[index * rows : (index + 1) * rows])

    @pl.when(side_ref[1] == 0)
    def _():
        for index in range(half):
            kept_ref[index] = parts[0][index]
            away_ref[index] = parts[1][index]

    @pl.when(side_ref[1] != 0)
    def _():
        for index in range(half):
            kept_ref[index] = parts[1][index]
            away_ref[index] = parts[0][index]


def split_product(acts, grad, theirs, sizes, flip, start, cols):
    masks, core = bit_masks(sizes)
    devices = sizes[0] * sizes[1]
    rows, inner = acts.shape
    block = inner // devices
    segment = inner // (2 * 2**core)
    tile = math.gcd(segment, 512)
    parts = segment // tile
    wide = math.gcd(cols, 1024)
    shift = start // wide
    first = masks[-2] if flip else masks[-1]
    sides = jnp.stack([small_index([masks[core]], sizes), small_index([first], sizes)])
    half = tile // (2 * block)
    out_spec = pl.BlockSpec((half, block, wide), lambda i, j, side_ref: (i, 0, j))
    out_shape = jax.ShapeDtypeStruct((devices // 4, block, cols), jnp.bfloat16)
    return pl.pallas_call(
        functools.partial(split_kernel, flip),
        grid_spec=pltpu.PrefetchScalarGridSpec(
            num_scalar_prefetch=1,
            grid=(inner // (2 * tile), cols // wide),
            in_specs=[
                pl.BlockSpec(
                    (rows, tile),
                    lambda i, j, side_ref: (
                        0,
                        (i // parts) * 2 * parts + side_ref[0] * parts + i % parts,
                    ),
                ),
                pl.BlockSpec((rows, wide), lambda i, j, side_ref: (0, j + shift)),
                pl.BlockSpec((tile, wide), lambda i, j, side_ref: (i, j + shift)),
            ],
            out_specs=[out_spec, out_spec],
        ),
        out_shape=[out_shape, out_shape],
        cost_estimate=LIGHT,
        name="split_product",
    )(sides, acts, grad, theirs)


def add_split_kernel(side_ref, kept_ref, kept_add_ref, away_ref, away_add_ref, *outs):
    for out, one, two in ((outs[0], kept_ref, kept_add_ref), (outs[1], away_ref, away_add_ref)):
        total = one[:, 0].astype(jnp.float32) + two[:, 0].astype(jnp.float32)
        out[...] = total.astype(jnp.bfloat16)


def add_split(kept, received, bit):
    blocks, rows, cols = kept.shape
    shape = (blocks // 2, 2, rows, cols)
    kept, received = kept.reshape(shape), received.reshape(shape)
    part = math.gcd(blocks // 2, 4)
    stays = pl.BlockSpec((part, 1, rows, cols), lambda i, side_ref: (i, side_ref[0], 0, 0))
    goes = pl.BlockSpec((part, 1, rows, cols), lambda i, side_ref: (i, 1 - side_ref[0], 0, 0))
    out_spec = pl.BlockSpec((part, rows, cols), lambda i, side_ref: (i, 0, 0))
    out_shape = jax.ShapeDtypeStruct((blocks // 2, rows, cols), kept.dtype)
    return pl.pallas_call(
        add_split_kernel,
        grid_spec=pltpu.PrefetchScalarGridSpec(
            num_scalar_prefetch=1,
            grid=(blocks // (2 * part),),
            in_specs=[stays, stays, goes, goes],
            out_specs=[out_spec, out_spec],
        ),
        out_shape=[out_shape, out_shape],
        cost_estimate=LIGHT,
        name="add_split",
    )(bit.reshape(1), kept, received, kept, received)


def add_far_kernel(count, place_ref, *refs):
    outs = refs[2 * count :]
    for slot, out in enumerate(outs):

        @pl.when(pl.program_id(0) == slot)
        def _(out=out):
            start = 0
            for one, two in zip(refs[:count], refs[count : 2 * count]):
                total = one[0].astype(jnp.float32) + two[0].astype(jnp.float32)
                width = total.shape[-1]
                out[:, start : start + width] = total.astype(jnp.bfloat16)
                start += width


def add_far(kept, received, place, slots):
    rows = kept[0].shape[1]
    width = sum(value.shape[2] for value in kept)
    specs = [
        pl.BlockSpec((1, rows, value.shape[2]), lambda i, place_ref: (place_ref[0] ^ i, 0, 0))
        for value in kept
    ]
    return pl.pallas_call(
        functools.partial(add_far_kernel, len(kept)),
        grid_spec=pltpu.PrefetchScalarGridSpec(
            num_scalar_prefetch=1,
            grid=(slots,),
            in_specs=specs + specs,
            out_specs=[pl.BlockSpec((rows, width), lambda i, place_ref: (0, 0))] * slots,
        ),
        out_shape=[jax.ShapeDtypeStruct((rows, width), kept[0].dtype)] * slots,
        cost_estimate=LIGHT,
        name="add_far",
    )(place.reshape(1), *kept, *received)


class Joint:
    def __init__(self, parts, sizes):
        self.sizes = sizes
        masks, core = bit_masks(sizes)
        self.near = masks[-2:]
        self.far = far_groups(sizes)[0]
        self.flips = [flip for exchange, flip, start, cols in parts]
        pairs = [
            split_product(
                exchange.acts, exchange.grad, exchange.theirs, sizes, flip, start, cols
            )
            for exchange, flip, start, cols in parts
        ]
        self.kept = [pair[0] for pair in pairs]
        self.away = [pair[1] for pair in pairs]
        self.masks = [self.near[0] if flip else self.near[1] for flip in self.flips]
        self.received = None
        self.stage = 0

    def send(self):
        self.received = [swap(away, mask, self.sizes) for away, mask in zip(self.away, self.masks)]

    def take(self):
        received, self.received = self.received, None
        self.stage += 1
        if self.stage == 1:
            self.masks = [self.near[1] if flip else self.near[0] for flip in self.flips]
            pairs = [
                add_split(kept, value, small_index([mask], self.sizes))
                for kept, value, mask in zip(self.kept, received, self.masks)
            ]
            self.kept = [pair[0] for pair in pairs]
            self.away = [pair[1] for pair in pairs]
        elif self.stage == 2:
            self.masks = combined(self.far)[1:]
            outs = add_far(
                self.kept, received, small_index(self.far, self.sizes), 2 ** len(self.far)
            )
            self.kept, self.away = outs[0], list(outs[1:])
        else:
            total = self.kept.astype(jnp.float32)
            for value in received:
                total = total + value.astype(jnp.float32)
            self.total = total
            self.away = []

    def result(self):
        return self.total


class Plain:
    def __init__(self, parts, sizes):
        self.chains = []
        for exchange, flip, start, cols in parts:
            kept = half_product(exchange.acts, exchange.grad, sizes, exchange.theirs)
            self.chains.append(Scatter([kept[:, start : start + cols]], sizes, flip))
        self.received = None

    @property
    def away(self):
        return [away for chain in self.chains for away in chain.away]

    @away.setter
    def away(self, values):
        values = list(values)
        for chain in self.chains:
            count = len(chain.away)
            chain.away, values = values[:count], values[count:]

    def send(self):
        for chain in self.chains:
            chain.send()
        self.received = [value for chain in self.chains for value in chain.received]

    def take(self):
        values, self.received = list(self.received), None
        for chain in self.chains:
            count = len(chain.received)
            chain.received, values = values[:count], values[count:]
            chain.take()

    def result(self):
        return jnp.concatenate([chain.states[0][0] for chain in self.chains], axis=1)


def summed(parts, sizes):
    heights = [exchange.acts.shape[1] // (sizes[0] * sizes[1]) for exchange, *unused in parts]
    if len(far_groups(sizes)) == 1 and all(height % 16 == 0 for height in heights):
        return Joint(parts, sizes)
    return Plain(parts, sizes)


class VectorScatter:
    def __init__(self, terms, sizes):
        self.sizes = sizes
        masks, core = bit_masks(sizes)
        self.bits = masks
        self.todo = [masks[core]] + [mask for mask in masks[::-1] if mask != masks[core]]
        self.state = terms
        self.received = None
        self.prepare()

    def prepare(self):
        bit = self.todo[0]
        high = 2 ** self.bits.index(bit)
        self.bits = [other for other in self.bits if other != bit]
        view = self.state.reshape(high, 2, -1, self.state.shape[-1])
        place = small_index([bit], self.sizes)
        away = lax.dynamic_index_in_dim(view, 1 - place, 1, keepdims=False)
        kept = lax.dynamic_index_in_dim(view, place, 1, keepdims=False)
        self.away = [away.reshape(-1, away.shape[-1])]
        self.kept = kept.reshape(-1, kept.shape[-1])
        self.mask = bit
        self.todo = self.todo[1:]

    def send(self):
        self.received = [swap(self.away[0], self.mask, self.sizes)]

    def take(self):
        self.state = self.kept + self.received[0]
        self.received = None
        self.away = []
        if self.todo:
            self.prepare()


def scatter_round(ending, starting, *others):
    ending = [chain for chain in ending if chain.received is not None]
    others = ended(ending, *others)
    going = [chain for chain in starting if chain.away and chain.received is None]
    flat = [value for chain in going for value in chain.away]
    held = list(pinned(*flat, *others))
    for chain in going:
        count = len(chain.away)
        chain.away, held = held[:count], held[count:]
        chain.send()
    return held


def gelu_and_slope(preact):
    square = preact * preact
    bent = jnp.tanh(preact * (0.7978845608028654 + (0.7978845608028654 * 0.044715) * square))
    half = 0.5 + 0.5 * bent
    value = preact * half
    inner = 0.7978845608028654 + (3 * 0.7978845608028654 * 0.044715) * square
    slope = half + value * (1.0 - bent) * inner
    return value.astype(jnp.bfloat16), slope.astype(jnp.bfloat16)


def times(left, right):
    return jnp.dot(left, right, preferred_element_type=jnp.float32)


def grad_pre_kernel(grad_ref, weight_ref, slope_ref, out_ref, bias_ref):
    weight = weight_ref[...]
    total = None
    for start in range(0, grad_ref.shape[0], 256):
        grad_act = against(grad_ref[start : start + 256], weight)
        slope = slope_ref[start : start + 256].astype(jnp.float32)
        grad_pre = (grad_act * slope).astype(jnp.bfloat16)
        out_ref[start : start + 256] = grad_pre
        term = jnp.sum(grad_pre.astype(jnp.float32), axis=0, keepdims=True)
        total = term if total is None else total + term
    bias_ref[...] = total


def grad_two_kernel(grad_ref, weight_ref, out_ref):
    term = against(grad_ref[...], weight_ref[...])

    @pl.when(pl.program_id(0) == 0)
    def _():
        out_ref[...] = term

    @pl.when(pl.program_id(0) != 0)
    def _():
        out_ref[...] += term


def grad_two_of(grad_pre, w_up):
    rows, hidden = grad_pre.shape
    width = w_up.shape[0]
    tile = 1024
    return pl.pallas_call(
        grad_two_kernel,
        grid=(hidden // tile,),
        in_specs=[
            pl.BlockSpec((rows, tile), lambda i: (0, i)),
            pl.BlockSpec((width, tile), lambda i: (0, i)),
        ],
        out_specs=pl.BlockSpec((rows, width), lambda i: (0, 0)),
        out_shape=jax.ShapeDtypeStruct((rows, width), jnp.float32),
        cost_estimate=LIGHT,
        name="grad_two",
    )(grad_pre, w_up)


def grad_pre_of(grad_low, w_down, slope):
    rows, width = grad_low.shape
    hidden = w_down.shape[0]
    tile = 1024
    grad_pre, bias = pl.pallas_call(
        grad_pre_kernel,
        grid=(hidden // tile,),
        in_specs=[
            pl.BlockSpec((rows, width), lambda i: (0, 0)),
            pl.BlockSpec((tile, width), lambda i: (i, 0)),
            pl.BlockSpec((rows, tile), lambda i: (0, i)),
        ],
        out_specs=[
            pl.BlockSpec((rows, tile), lambda i: (0, i)),
            pl.BlockSpec((1, tile), lambda i: (0, i)),
        ],
        out_shape=[
            jax.ShapeDtypeStruct((rows, hidden), jnp.bfloat16),
            jax.ShapeDtypeStruct((1, hidden), jnp.float32),
        ],
        cost_estimate=LIGHT,
        name="grad_pre",
    )(grad_low, w_down, slope)
    return grad_pre, bias.reshape(hidden)


def local(
    sizes,
    frame_input,
    code_embed,
    segment_ids,
    frame_cotangent,
    code_cotangent,
    frame_prenorm,
    frame_query,
    frame_keys,
    frame_values,
    frame_outproj,
    frame_midnorm,
    frame_upproj,
    frame_upbias,
    frame_downproj,
    frame_downbias,
    code_prenorm,
    code_query,
    code_keys,
    code_values,
    code_outproj,
    code_midnorm,
    code_upproj,
    code_upbias,
    code_downproj,
    code_downbias,
):
    low = jnp.bfloat16
    frames = frame_input.shape[0]
    devices = sizes[0] * sizes[1]
    vectors = (
        frame_prenorm,
        frame_midnorm,
        frame_upbias,
        frame_downbias,
        code_prenorm,
        code_midnorm,
        code_upbias,
        code_downbias,
    )
    widths = [vec.shape[0] for vec in vectors]

    def weight(shard, flip):
        return Gather(shard, sizes, flip)

    f_a = weight(jnp.concatenate([frame_query, frame_keys], axis=1)[None], False)
    shard_rows = frame_values.shape[0]
    packed = jnp.concatenate([vec[None] for vec in vectors], axis=1)
    packed = jnp.pad(packed, ((0, 0), (0, shard_rows * 128 - packed.shape[1])))
    packed = packed.reshape(shard_rows, 128)
    f_b = Gather(
        jnp.stack(
            [
                jnp.concatenate([frame_values, packed], axis=1),
                jnp.concatenate([frame_outproj, packed], axis=1),
            ]
        ),
        sizes,
        True,
        128,
    )
    f_u = weight(frame_upproj[None], False)
    f_d = weight(frame_downproj[None], True)
    c_a = weight(jnp.concatenate([code_query, code_keys], axis=1)[None], False)
    c_b = weight(jnp.stack([code_values, code_outproj]), True)
    c_u = weight(code_upproj[None], False)
    c_d = weight(code_downproj[None], True)
    f_attn, f_ff, c_attn, c_ff = [f_a, f_b], [f_u, f_d], [c_a, c_b], [c_u, c_d]

    for unused in range(len(f_a.far) - 1):
        for chains in (f_attn, f_ff, c_attn, c_ff):
            started(chains)
            ended(chains)
    started(f_attn)
    ended(f_attn)
    started(f_attn + f_ff)
    ended(f_attn)
    started(f_attn)
    ended(f_attn + f_ff)
    started(f_attn + f_ff + c_attn)
    ended(f_attn + f_ff + c_attn)
    started(f_ff)
    whole = f_b.tails[0].reshape(devices, -1)[:, : sum(widths)].astype(jnp.float32)
    gains = []
    start = 0
    for width in widths:
        gains.append(whole[:, start : start + width].reshape(devices * width))
        start += width
    frame_gains = tuple(gains[:4])
    code_gains = tuple(gains[4:])
    frame_x = frame_input.astype(jnp.float32)
    f_normed = rms_scale(frame_x, frame_gains[0]).astype(low)
    f_pair = f_a.whole[0]
    f_value, f_out = f_b.whole

    segments = segment_ids[0]
    f_qk = times(f_normed, f_pair).astype(low)
    f_v = times(f_normed, f_value).astype(low)
    f_mixed = frame_attend(f_qk, f_v, segments)
    f_hidden = frame_x + times(f_mixed, f_out)
    f_normed_two = rms_scale(f_hidden, frame_gains[1]).astype(low)
    f_hidden, f_normed_two = ended(f_ff, f_hidden, f_normed_two)
    started(f_ff + c_attn + c_ff)
    code_rows = jnp.swapaxes(code_embed, 0, 1)
    grad_code_y = jnp.swapaxes(code_cotangent, 0, 1)
    code_rows, grad_code_y = ended(f_ff + c_attn, code_rows, grad_code_y)
    started(c_attn)
    (f_up,) = f_u.whole
    (f_down,) = f_d.whole
    f_act, f_slope = gelu_and_slope(times(f_normed_two, f_up) + frame_gains[2])
    rows = CB * frames
    grad_code_y = grad_code_y.reshape(rows, D)
    f_act, f_slope = ended(c_attn + c_ff, f_act, f_slope)
    started(c_attn + c_ff)
    frame_y = f_hidden + (times(f_act, f_down) + frame_gains[3])

    code_x = (code_rows.astype(jnp.float32) + frame_y[None]).reshape(rows, D)
    c_normed = rms_scale(code_x, code_gains[0]).astype(low)
    c_normed, code_x = ended(c_attn + c_ff, c_normed, code_x)
    started(c_ff)
    c_pair = c_a.whole[0]
    c_value, c_out = c_b.whole

    def tokens_of(value):
        return value.reshape(CB, frames, value.shape[-1])

    c_qk = times(c_normed, c_pair).astype(low)
    c_v = times(c_normed, c_value).astype(low)
    c_qk, c_v = ended(c_ff, c_qk, c_v)
    started(c_ff)
    c_mixed = code_attend(tokens_of(c_qk), tokens_of(c_v)).reshape(rows, D)
    c_hidden = code_x + times(c_mixed, c_out)
    c_normed_two = rms_scale(c_hidden, code_gains[1]).astype(low)
    c_hidden, c_normed_two = ended([c_u], c_hidden, c_normed_two)
    (c_up,) = c_u.whole
    c_act, c_slope = gelu_and_slope(times(c_normed_two, c_up) + code_gains[2])
    c_act, c_slope = ended([c_d], c_act, c_slope)
    (c_down,) = c_d.whole

    def both(exchange):
        half = exchange.grad.shape[1] // 2
        return [summed([(exchange, True, 0, half), (exchange, False, half, half)], sizes)]

    def attention_sums(pair, value, outproj):
        parts = [(pair, False, 0, 2 * D), (value, True, 0, D), (outproj, True, 0, D)]
        return [summed(parts, sizes)]

    def norm_back(grad_out, inputs, gain):
        unused, back = jax.vjp(rms_scale, inputs, gain)
        return back(grad_out)

    grad_low = grad_code_y
    c_d_core = Core(c_act, grad_low, sizes)
    c_slope, grad_low = scatter_round([], [c_d_core], c_slope, grad_low)
    c_grad_b_down = jnp.sum(grad_low.astype(jnp.float32), axis=0)
    (c_grad_b_down,) = ended([c_d_core], c_grad_b_down)
    c_d_chain = both(c_d_core)
    c_slope, grad_low = scatter_round([], c_d_chain, c_slope, grad_low)
    grad_pre, c_grad_b_up = grad_pre_of(grad_low, c_down, c_slope)
    c_u_core = Core(c_normed_two, grad_pre, sizes)
    (grad_pre,) = scatter_round(c_d_chain, c_d_chain + [c_u_core], grad_pre)
    grad_two = grad_two_of(grad_pre, c_up)
    (grad_two,) = scatter_round(c_d_chain + [c_u_core], c_d_chain, grad_two)
    c_u_chain = both(c_u_core)
    grad_part, c_grad_mid = norm_back(grad_two, c_hidden, code_gains[1])
    grad_hidden = grad_low.astype(jnp.float32) + grad_part
    grad_attn = grad_hidden.astype(low)
    grad_attn, grad_hidden = scatter_round(c_d_chain, c_u_chain, grad_attn, grad_hidden)
    c_o_core = Core(c_mixed, grad_attn, sizes)
    grad_mixed = against(grad_attn, c_out).astype(low)
    grad_pair, grad_values = code_attend_back(
        tokens_of(c_qk), tokens_of(c_v), tokens_of(grad_mixed)
    )
    grad_pair = grad_pair.reshape(rows, 2 * D)
    grad_values = grad_values.reshape(rows, D)
    grad_pair, grad_values = scatter_round(
        c_u_chain, c_u_chain + [c_o_core], grad_pair, grad_values
    )
    c_p_core = Core(c_normed, grad_pair, sizes)
    c_v_core = Core(c_normed, grad_values, sizes)
    grad_pair, grad_values = scatter_round(
        c_u_chain + [c_o_core], c_u_chain + [c_p_core, c_v_core], grad_pair, grad_values
    )
    grad_normed = against(grad_pair, c_pair) + against(grad_values, c_value)
    grad_part, c_grad_pre = norm_back(grad_normed, code_x, code_gains[0])
    grad_code_x = grad_hidden + grad_part
    grad_frame_y = frame_cotangent.astype(jnp.float32) + jnp.sum(tokens_of(grad_code_x), axis=0)
    grad_code_x, grad_frame_y = ended(
        c_u_chain + [c_p_core, c_v_core], grad_code_x, grad_frame_y
    )
    c_ab = attention_sums(c_p_core, c_v_core, c_o_core)
    (grad_frame_y,) = scatter_round([], c_ab, grad_frame_y)

    grad_low = grad_frame_y.astype(low)
    f_d_core = Core(f_act, grad_low, sizes)
    grad_pre, f_grad_b_up = grad_pre_of(grad_low, f_down, f_slope)
    f_u_core = Core(f_normed_two, grad_pre, sizes)
    (grad_pre,) = scatter_round(c_ab, c_ab + [f_d_core, f_u_core], grad_pre)
    grad_two = grad_two_of(grad_pre, f_up)
    grad_part, f_grad_mid = norm_back(grad_two, f_hidden, frame_gains[1])
    grad_hidden = grad_frame_y + grad_part
    grad_attn = grad_hidden.astype(low)
    grad_attn, grad_hidden = scatter_round(
        c_ab + [f_d_core, f_u_core], c_ab, grad_attn, grad_hidden
    )
    f_d_chain = both(f_d_core)
    grad_attn, grad_hidden = scatter_round(c_ab, f_d_chain, grad_attn, grad_hidden)
    f_u_chain = both(f_u_core)
    f_o_core = Core(f_mixed, grad_attn, sizes)
    grad_mixed = against(grad_attn, f_out).astype(low)
    grad_pair, grad_values = frame_attend_back(f_qk, f_v, grad_mixed, segments)
    grad_pair, grad_values = scatter_round(
        f_d_chain, f_d_chain + f_u_chain + [f_o_core], grad_pair, grad_values
    )
    f_p_core = Core(f_normed, grad_pair, sizes)
    f_v_core = Core(f_normed, grad_values, sizes)
    grad_normed = against(grad_pair, f_pair) + against(grad_values, f_value)
    grad_part, f_grad_pre = norm_back(grad_normed, frame_x, frame_gains[0])
    grad_frame_x = grad_hidden + grad_part
    (grad_frame_x,) = scatter_round(
        f_d_chain + f_u_chain + [f_o_core],
        f_d_chain + f_u_chain + [f_p_core, f_v_core],
        grad_frame_x,
    )
    f_grad_b_down = jnp.sum(grad_low.astype(jnp.float32), axis=0)
    (f_grad_b_down,) = ended(f_u_chain + [f_p_core, f_v_core], f_grad_b_down)
    f_ab = attention_sums(f_p_core, f_v_core, f_o_core)
    terms = jnp.concatenate(
        [
            term.reshape(devices, -1)
            for term in (
                f_grad_pre,
                f_grad_mid,
                f_grad_b_up,
                f_grad_b_down,
                c_grad_pre,
                c_grad_mid,
                c_grad_b_up,
                c_grad_b_down,
            )
        ],
        axis=1,
    )
    row = VectorScatter(terms, sizes)
    grad_frame_x, c_act = scatter_round(f_d_chain, f_ab + f_u_chain + [row], grad_frame_x, c_act)
    code_y = c_hidden + (times(c_act, c_down) + code_gains[3])
    frame_output = frame_y.astype(low)
    (code_y,) = scatter_round(f_ab + [row], f_ab + [row], code_y)
    code_output = jnp.swapaxes(tokens_of(code_y.astype(low)), 0, 1)
    (code_output,) = scatter_round(f_ab + f_u_chain + [row], f_ab + [row], code_output)
    code_embed_grad = jnp.swapaxes(tokens_of(grad_code_x), 0, 1)
    (code_embed_grad,) = scatter_round(f_ab + [row], [row], code_embed_grad)
    everything = c_d_chain + c_u_chain + c_ab + f_d_chain + f_u_chain + f_ab + [row]
    while True:
        started([chain for chain in everything if chain.away and chain.received is None])
        going = [chain for chain in everything if chain.received is not None]
        if not going:
            break
        ended(going)
    sums = row.state[0]
    pieces = []
    start = 0
    for width in widths:
        pieces.append(sums[start : start + width])
        start += width

    def arranged(attn_sums, up_sums, down_sums, vecs):
        total = attn_sums[0].result()
        prenorm, midnorm, upbias, downbias = vecs
        return (
            prenorm,
            total[:, :D],
            total[:, D : 2 * D],
            total[:, 2 * D : 3 * D],
            total[:, 3 * D :],
            midnorm,
            up_sums[0].result(),
            upbias,
            down_sums[0].result(),
            downbias,
        )

    code_outs = arranged(c_ab, c_u_chain, c_d_chain, pieces[4:])
    frame_outs = arranged(f_ab, f_u_chain, f_d_chain, pieces[:4])
    return (frame_output, code_output, grad_frame_x, code_embed_grad) + frame_outs + code_outs


def solution(mesh):
    in_specs = (
        P(("gx", "gy"), None),
        P(("gx", "gy"), None, None),
        P(("gx", "gy"), None),
        P(("gx", "gy"), None),
        P(("gx", "gy"), None, None),
        P(("gx", "gy")),
        P(("gx", "gy"), None),
        P(("gx", "gy"), None),
        P(("gx", "gy"), None),
        P(("gx", "gy"), None),
        P(("gx", "gy")),
        P(("gx", "gy"), None),
        P(("gx", "gy")),
        P(("gx", "gy"), None),
        P(("gx", "gy")),
        P(("gx", "gy")),
        P(("gx", "gy"), None),
        P(("gx", "gy"), None),
        P(("gx", "gy"), None),
        P(("gx", "gy"), None),
        P(("gx", "gy")),
        P(("gx", "gy"), None),
        P(("gx", "gy")),
        P(("gx", "gy"), None),
        P(("gx", "gy")),
    )
    out_specs = (
        P(("gx", "gy"), None),
        P(("gx", "gy"), None, None),
        P(("gx", "gy"), None),
        P(("gx", "gy"), None, None),
        P(("gx", "gy")),
        P(("gx", "gy"), None),
        P(("gx", "gy"), None),
        P(("gx", "gy"), None),
        P(("gx", "gy"), None),
        P(("gx", "gy")),
        P(("gx", "gy"), None),
        P(("gx", "gy")),
        P(("gx", "gy"), None),
        P(("gx", "gy")),
        P(("gx", "gy")),
        P(("gx", "gy"), None),
        P(("gx", "gy"), None),
        P(("gx", "gy"), None),
        P(("gx", "gy"), None),
        P(("gx", "gy")),
        P(("gx", "gy"), None),
        P(("gx", "gy")),
        P(("gx", "gy"), None),
        P(("gx", "gy")),
    )
    sizes = (mesh.shape["gx"], mesh.shape["gy"])
    return jax.shard_map(
        functools.partial(local, sizes), mesh=mesh, in_specs=in_specs, out_specs=out_specs, check_vma=False)
```

```python
import functools
import math

import jax
import jax.numpy as jnp
from jax import lax
from jax.experimental import pallas as pl
from jax.experimental.pallas import tpu as pltpu
from jax.sharding import PartitionSpec as P

D = 1024
HEADS = 16
HD = 64
CB = 3
LIGHT = pl.CostEstimate(flops=1, bytes_accessed=1, transcendentals=0)


def gelu_tanh(value):
    return (
        0.5
        * value
        * (1.0 + jnp.tanh(0.7978845608028654 * (value + 0.044715 * value * value * value)))
    )


def rms_scale(value, gain_vec):
    return value * lax.rsqrt(jnp.mean(value * value, axis=-1, keepdims=True) + 1e-05) * gain_vec


def over_rows(left, right):
    return lax.dot_general(
        left, right, (((0,), (0,)), ((), ())), preferred_element_type=jnp.float32
    )


def against(left, right):
    return lax.dot_general(
        left, right, (((1,), (1,)), ((), ())), preferred_element_type=jnp.float32
    )


def head_marks():
    lane = lax.broadcasted_iota(jnp.int32, (D, 128), 0) // HD
    head = lax.broadcasted_iota(jnp.int32, (D, 128), 1)
    return (lane == head).astype(jnp.bfloat16)


def head_sums(left, right, marks):
    product = left.astype(jnp.float32) * right.astype(jnp.float32)
    upper = product.astype(jnp.bfloat16)
    lower = (product - upper.astype(jnp.float32)).astype(jnp.bfloat16)
    return jnp.dot(upper, marks, preferred_element_type=jnp.float32) + jnp.dot(
        lower, marks, preferred_element_type=jnp.float32
    )


def spread(heads, marks):
    return lax.dot_general(
        heads, marks, (((1,), (1,)), ((), ())), preferred_element_type=jnp.float32
    )


def token_probs(tokens_q, tokens_k, marks):
    probs = []
    for token in range(CB):
        scores = [
            head_sums(tokens_q[token], tokens_k[other], marks) * HD ** (-0.5)
            for other in range(token + 1)
        ]
        highest = functools.reduce(jnp.maximum, scores)
        expo = [jnp.exp(score - highest) for score in scores]
        total = functools.reduce(jnp.add, expo)
        probs.append([term / total for term in expo])
    return probs


def code_attend_kernel(pair_ref, values_ref, marks_ref, out_ref):
    marks = marks_ref[...]
    query = [pair_ref[token, :, :D] for token in range(CB)]
    keys = [pair_ref[token, :, D:] for token in range(CB)]
    probs = token_probs(query, keys, marks)
    for token in range(CB):
        mixed = None
        for other in range(token + 1):
            value = values_ref[other].astype(jnp.float32)
            term = spread(probs[token][other].astype(jnp.bfloat16), marks) * value
            mixed = term if mixed is None else mixed + term
        out_ref[token] = mixed.astype(jnp.bfloat16)


def code_attend_back_kernel(
    pair_ref, values_ref, grad_ref, marks_ref, out_pair_ref, out_values_ref
):
    marks = marks_ref[...]
    query = [pair_ref[token, :, :D] for token in range(CB)]
    keys = [pair_ref[token, :, D:] for token in range(CB)]
    probs = token_probs(query, keys, marks)
    grad_scores = []
    for token in range(CB):
        grads = [
            head_sums(grad_ref[token], values_ref[other], marks)
            for other in range(token + 1)
        ]
        inner = functools.reduce(
            jnp.add, [prob * grad for prob, grad in zip(probs[token], grads)]
        )
        grad_scores.append(
            [
                (prob * (grad - inner)).astype(jnp.bfloat16)
                for prob, grad in zip(probs[token], grads)
            ]
        )
    scale = HD ** (-0.5)
    grad_keys = [None] * CB
    grad_values = [None] * CB
    for token in range(CB):
        grad_query = None
        for other in range(token + 1):
            wide = spread(grad_scores[token][other], marks)
            term = wide * keys[other].astype(jnp.float32)
            grad_query = term if grad_query is None else grad_query + term
            term = wide * query[token].astype(jnp.float32)
            grad_keys[other] = term if grad_keys[other] is None else grad_keys[other] + term
            wide = spread(probs[token][other].astype(jnp.bfloat16), marks)
            term = wide * grad_ref[token].astype(jnp.float32)
            grad_values[other] = term if grad_values[other] is None else grad_values[other] + term
        out_pair_ref[token, :, :D] = (grad_query * scale).astype(jnp.bfloat16)
    for token in range(CB):
        out_pair_ref[token, :, D:] = (grad_keys[token] * scale).astype(jnp.bfloat16)
        out_values_ref[token] = grad_values[token].astype(jnp.bfloat16)


def token_specs(step, widths):
    return [pl.BlockSpec((CB, step, width), lambda i: (0, i, 0)) for width in widths] + [
        pl.BlockSpec((D, 128), lambda i: (0, 0))
    ]


def code_attend(pair, values):
    frames = values.shape[1]
    step = math.gcd(frames, 64)
    return pl.pallas_call(
        code_attend_kernel,
        grid=(frames // step,),
        in_specs=token_specs(step, (2 * D, D)),
        out_specs=pl.BlockSpec((CB, step, D), lambda i: (0, i, 0)),
        out_shape=jax.ShapeDtypeStruct((CB, frames, D), jnp.bfloat16),
        cost_estimate=LIGHT,
        name="code_attend",
    )(pair, values, head_marks())


def code_attend_back(pair, values, grad_mixed):
    frames = values.shape[1]
    step = math.gcd(frames, 64)
    return pl.pallas_call(
        code_attend_back_kernel,
        grid=(frames // step,),
        in_specs=token_specs(step, (2 * D, D, D)),
        out_specs=[
            pl.BlockSpec((CB, step, 2 * D), lambda i: (0, i, 0)),
            pl.BlockSpec((CB, step, D), lambda i: (0, i, 0)),
        ],
        out_shape=[
            jax.ShapeDtypeStruct((CB, frames, 2 * D), jnp.bfloat16),
            jax.ShapeDtypeStruct((CB, frames, D), jnp.bfloat16),
        ],
        cost_estimate=LIGHT,
        name="code_attend_back",
    )(pair, values, grad_mixed, head_marks())


def frame_mask(column_ref, row_ref):
    frames = column_ref.shape[0]
    shape = (frames, frames)
    earlier = lax.broadcasted_iota(jnp.int32, shape, 0) >= lax.broadcasted_iota(
        jnp.int32, shape, 1
    )
    return earlier & (column_ref[...] == row_ref[...])


def frame_probs(query, keys, allowed):
    scores = against(query, keys) * HD ** (-0.5)
    scores = jnp.where(allowed, scores, -1e30)
    highest = jnp.max(scores, axis=-1, keepdims=True)
    expo = jnp.exp(scores - highest)
    return expo / jnp.sum(expo, axis=-1, keepdims=True)


def half_lanes(value, upper):
    lane = lax.broadcasted_iota(jnp.int32, value.shape, 1)
    chosen = (lane >= HD) if upper else (lane < HD)
    return jnp.where(chosen, value, jnp.zeros_like(value))


def frame_attend_kernel(query_ref, keys_ref, values_ref, column_ref, row_ref, out_ref):
    allowed = frame_mask(column_ref, row_ref)
    mixed = None
    for upper in (False, True):
        probs = frame_probs(half_lanes(query_ref[...], upper), keys_ref[...], allowed)
        term = jnp.dot(
            probs.astype(jnp.bfloat16),
            half_lanes(values_ref[...], upper),
            preferred_element_type=jnp.float32,
        )
        mixed = term if mixed is None else mixed + term
    out_ref[...] = mixed.astype(jnp.bfloat16)


def frame_attend_back_kernel(
    query_ref, keys_ref, values_ref, grad_ref, column_ref, row_ref, out_pair_ref, out_values_ref
):
    allowed = frame_mask(column_ref, row_ref)
    scale = HD ** (-0.5)
    grads = [None, None, None]
    for upper in (False, True):
        query = half_lanes(query_ref[...], upper)
        keys = half_lanes(keys_ref[...], upper)
        grad_out = half_lanes(grad_ref[...], upper)
        probs = frame_probs(query, keys, allowed)
        grad_probs = against(grad_out, values_ref[...])
        inner = jnp.sum(probs * grad_probs, axis=-1, keepdims=True)
        grad_scores = (probs * (grad_probs - inner)).astype(jnp.bfloat16)
        terms = (
            jnp.dot(grad_scores, keys, preferred_element_type=jnp.float32) * scale,
            over_rows(grad_scores, query) * scale,
            over_rows(probs.astype(jnp.bfloat16), grad_out),
        )
        grads = [term if grad is None else grad + term for grad, term in zip(grads, terms)]
    start = pl.multiple_of(pl.program_id(0) * 2 * HD, 2 * HD)
    out_pair_ref[:, pl.ds(start, 2 * HD)] = grads[0].astype(jnp.bfloat16)
    out_pair_ref[:, pl.ds(D + start, 2 * HD)] = grads[1].astype(jnp.bfloat16)
    out_values_ref[...] = grads[2].astype(jnp.bfloat16)


def pair_specs(frames, extra):
    pairs = HEADS // 2
    block = (frames, 2 * HD)
    return (
        [
            pl.BlockSpec(block, lambda j: (0, j)),
            pl.BlockSpec(block, lambda j: (0, j + pairs)),
        ]
        + [pl.BlockSpec(block, lambda j: (0, j))] * extra
        + [
            pl.BlockSpec((frames, 1), lambda j: (0, 0)),
            pl.BlockSpec((1, frames), lambda j: (0, 0)),
        ]
    )


def frame_attend(pair, values, segments):
    frames = values.shape[0]
    return pl.pallas_call(
        frame_attend_kernel,
        grid=(HEADS // 2,),
        in_specs=pair_specs(frames, 1),
        out_specs=pl.BlockSpec((frames, 2 * HD), lambda j: (0, j)),
        out_shape=jax.ShapeDtypeStruct((frames, D), jnp.bfloat16),
        cost_estimate=LIGHT,
        name="frame_attend",
    )(pair, pair, values, segments.reshape(frames, 1), segments.reshape(1, frames))


def frame_attend_back(pair, values, grad_mixed, segments):
    frames = values.shape[0]
    return pl.pallas_call(
        frame_attend_back_kernel,
        grid=(HEADS // 2,),
        in_specs=pair_specs(frames, 2),
        out_specs=[
            pl.BlockSpec((frames, 2 * D), lambda j: (0, 0)),
            pl.BlockSpec((frames, 2 * HD), lambda j: (0, j)),
        ],
        out_shape=[
            jax.ShapeDtypeStruct((frames, 2 * D), jnp.bfloat16),
            jax.ShapeDtypeStruct((frames, D), jnp.bfloat16),
        ],
        cost_estimate=LIGHT,
        name="frame_attend_back",
    )(
        pair,
        pair,
        values,
        grad_mixed,
        segments.reshape(frames, 1),
        segments.reshape(1, frames),
    )


def bit_masks(sizes):
    count = sizes[0] * sizes[1]
    masks = []
    step = count // 2
    while step >= 1:
        masks.append(step)
        step //= 2
    return masks, masks.index(sizes[1])


def swap(value, mask, sizes):
    count = sizes[0] * sizes[1]
    return lax.ppermute(value, ("gx", "gy"), [(place, place ^ mask) for place in range(count)])


def device_index(sizes):
    return lax.axis_index("gx") * sizes[1] + lax.axis_index("gy")


def far_groups(sizes):
    masks, core = bit_masks(sizes)
    far = [mask for place, mask in enumerate(masks[:-2]) if place != core]
    return [far[start : start + 2] for start in range(0, len(far), 2)]


def combined(group):
    found = []
    for index in range(2 ** len(group)):
        mask = 0
        for place, bit in enumerate(group):
            if (index >> (len(group) - 1 - place)) & 1:
                mask |= bit
        found.append(mask)
    return found


def small_index(group, sizes):
    me = device_index(sizes)
    index = jnp.zeros((), jnp.int32)
    for bit in group:
        index = index * 2 + ((me // bit) % 2).astype(jnp.int32)
    return index


def spans(done, pos):
    high = 2 ** sum(1 for other in done if other < pos)
    low = 2 ** sum(1 for other in done if other > pos)
    return high, low


def merge_kernel(bit_ref, mine_ref, theirs_ref, *outs):
    def put(first, second):
        start = 0
        for out in outs:
            width = out.shape[-1]
            out[0, 0] = first[0, :, start : start + width]
            out[0, 1] = second[0, :, start : start + width]
            start += width

    @pl.when(bit_ref[0] == 0)
    def _():
        put(mine_ref, theirs_ref)

    @pl.when(bit_ref[0] != 0)
    def _():
        put(theirs_ref, mine_ref)


def merged(mine, theirs, bit, splits):
    planes, rows, cols = mine.shape
    part = rows
    while part % 2 == 0 and part * cols > 512 * 1024:
        part //= 2
    read = pl.BlockSpec((1, part, cols), lambda i, j, bit_ref: (i, j, 0))
    return pl.pallas_call(
        merge_kernel,
        grid_spec=pltpu.PrefetchScalarGridSpec(
            num_scalar_prefetch=1,
            grid=(planes, rows // part),
            in_specs=[read, read],
            out_specs=[
                pl.BlockSpec((1, 2, part, width), lambda i, j, bit_ref: (i, 0, j, 0))
                for width in splits
            ],
        ),
        out_shape=[
            jax.ShapeDtypeStruct((planes, 2, rows, width), mine.dtype) for width in splits
        ],
        cost_estimate=LIGHT,
        name="merge",
    )(bit.reshape(1), mine, theirs)


def place_far_kernel(place_ref, *refs):
    for index, ref in enumerate(refs[:-1]):
        refs[-1][0, place_ref[0] ^ index] = ref[0]


def placed_far(pieces, place):
    planes, rows, cols = pieces[0].shape
    slots = len(pieces)
    return pl.pallas_call(
        place_far_kernel,
        grid_spec=pltpu.PrefetchScalarGridSpec(
            num_scalar_prefetch=1,
            grid=(planes,),
            in_specs=[pl.BlockSpec((1, rows, cols), lambda i, place_ref: (i, 0, 0))] * slots,
            out_specs=pl.BlockSpec((1, slots, rows, cols), lambda i, place_ref: (i, 0, 0, 0)),
        ),
        out_shape=jax.ShapeDtypeStruct((planes, slots, rows, cols), pieces[0].dtype),
        cost_estimate=LIGHT,
        name="place_far",
    )(place.reshape(1), *pieces)


def pinned(*values):
    return lax.optimization_barrier(values)


def gather_order(sizes, flip):
    masks, core = bit_masks(sizes)
    count = len(masks)
    far = [place for place in range(count - 2) if place != core]
    near = [count - 1, count - 2] if flip else [count - 2, count - 1]
    return far + near + [core]


class Gather:
    def __init__(self, shards, sizes, flips, splits):
        self.sizes = sizes
        self.flips, self.splits = flips, splits
        masks, core = bit_masks(sizes)
        self.masks, self.core = masks, core
        self.far = far_groups(sizes)
        self.states = [shards]
        self.received = None
        self.stage = -len(self.far)

    def near_masks(self, second):
        return [self.masks[-1 if flip != second else -2] for flip in self.flips]

    def send(self):
        if self.stage < 0:
            masks = combined(self.far[self.stage])[1:]
            self.received = [swap(self.states[0], mask, self.sizes) for mask in masks]
        elif self.stage < 2:
            masks = self.near_masks(self.stage == 1)
            self.received = [
                swap(state, mask, self.sizes) for state, mask in zip(self.states, masks)
            ]
        else:
            mask = self.masks[self.core]
            self.received = [swap(state, mask, self.sizes) for state in self.states]

    def take(self):
        received, self.received = list(self.received), None
        if self.stage < 0:
            state = self.states[0]
            groups, rows, cols = state.shape[0], state.shape[-2], state.shape[-1]
            group = self.far[self.stage]
            pieces = [value.reshape(-1, rows, cols) for value in [state] + received]
            wide = placed_far(pieces, small_index(group, self.sizes))
            self.states = [wide.reshape(groups, -1, rows, cols)]
            if self.stage == -1:
                self.states = [self.states[0][place] for place in range(groups)]
        elif self.stage < 2:
            states = []
            masks = self.near_masks(self.stage == 1)
            for state, value, mask, flip in zip(self.states, received, masks, self.flips):
                blocks, rows, cols = state.shape
                joined = 2 if flip and self.stage == 1 else 1
                shape = (blocks // joined, joined * rows, cols)
                bit = small_index([mask], self.sizes)
                (out,) = merged(state.reshape(shape), value.reshape(shape), bit, [cols])
                states.append(out.reshape(2 * blocks, rows, cols))
            self.states = states
        else:
            self.whole = []
            for state, value, splits in zip(self.states, received, self.splits):
                blocks, rows, cols = state.shape
                high = 2**self.core
                shape = (high, blocks // high * rows, cols)
                bit = small_index([self.masks[self.core]], self.sizes)
                outs = merged(state.reshape(shape), value.reshape(shape), bit, splits)
                self.whole.append([out.reshape(-1, out.shape[-1]) for out in outs])
        self.stage += 1


def ended(chains, *others):
    flat = [value for chain in chains for value in chain.received]
    held = list(pinned(*flat, *others))
    for chain in chains:
        count = len(chain.received)
        chain.received, held = held[:count], held[count:]
        chain.take()
    return held


def started(chains):
    for chain in chains:
        chain.send()


def half_kernel(side_ref, acts_ref, grad_ref, out_ref):
    out_ref[...] = over_rows(acts_ref[...], grad_ref[...]).astype(jnp.bfloat16)


def half_add_kernel(side_ref, acts_ref, grad_ref, add_ref, out_ref):
    total = over_rows(acts_ref[...], grad_ref[...]) + add_ref[...].astype(jnp.float32)
    out_ref[...] = total.astype(jnp.bfloat16)


def half_product(acts, grad, sizes, received):
    masks, core = bit_masks(sizes)
    rows, inner = acts.shape
    cols = grad.shape[1]
    segment = inner // (2 * 2**core)
    tile = math.gcd(segment, 512)
    parts = segment // tile
    wide = math.gcd(cols, 1024)
    side = small_index([masks[core]], sizes)
    if received is None:
        side = 1 - side

    def acts_at(i, j, side_ref):
        return (0, (i // parts) * 2 * parts + side_ref[0] * parts + i % parts)

    specs = [
        pl.BlockSpec((rows, tile), acts_at),
        pl.BlockSpec((rows, wide), lambda i, j, side_ref: (0, j)),
    ]
    out_spec = pl.BlockSpec((tile, wide), lambda i, j, side_ref: (i, j))
    operands = [acts, grad]
    if received is not None:
        specs.append(out_spec)
        operands.append(received)
    return pl.pallas_call(
        half_kernel if received is None else half_add_kernel,
        grid_spec=pltpu.PrefetchScalarGridSpec(
            num_scalar_prefetch=1,
            grid=(inner // (2 * tile), cols // wide),
            in_specs=specs,
            out_specs=out_spec,
        ),
        out_shape=jax.ShapeDtypeStruct((inner // 2, cols), jnp.bfloat16),
        cost_estimate=LIGHT,
        name="half_away" if received is None else "half_kept",
    )(side.reshape(1), *operands)


class Core:
    def __init__(self, acts, grad, sizes):
        masks, core = bit_masks(sizes)
        self.mask, self.sizes = masks[core], sizes
        self.acts, self.grad = acts, grad
        self.away = [half_product(acts, grad, sizes, None)]
        self.received = None
        self.theirs = None

    def send(self):
        self.received = [swap(self.away[0], self.mask, self.sizes)]

    def take(self):
        self.theirs = self.received[0]
        self.received = None
        self.away = []


class Scatter:
    def __init__(self, states, sizes, flip):
        self.sizes = sizes
        masks, core = bit_masks(sizes)
        self.bits = [mask for place, mask in enumerate(masks) if place != core]
        first, second = masks[-1], masks[-2]
        if flip:
            first, second = second, first
        self.todo = [[first], [second]] + far_groups(sizes)[::-1]
        count = 2 ** len(self.bits)
        self.states = [
            state.reshape(count, state.shape[0] // count, state.shape[1]) for state in states
        ]
        self.received = None
        self.prepare()

    def prepare(self):
        group = self.todo[0]
        first = self.bits.index(group[0])
        self.bits = [bit for bit in self.bits if bit not in group]
        slots = 2 ** len(group)
        high = 2**first
        place = small_index(group, self.sizes)
        self.kept = []
        aways = []
        for state in self.states:
            blocks, rows, cols = state.shape
            view = state.reshape(high, slots, blocks // (high * slots), rows, cols)
            parts = [
                lax.dynamic_index_in_dim(view, place ^ index, 1, keepdims=False).reshape(
                    blocks // slots, rows, cols
                )
                for index in range(slots)
            ]
            self.kept.append(parts[0])
            aways.append(parts[1:])
        self.away = [
            jnp.stack([away[index] for away in aways]) for index in range(slots - 1)
        ]
        self.todo = self.todo[1:]
        self.masks = combined(group)[1:]

    def send(self):
        self.received = [swap(away, mask, self.sizes) for away, mask in zip(self.away, self.masks)]

    def take(self):
        last = not self.todo
        self.states = []
        for index, kept in enumerate(self.kept):
            total = kept.astype(jnp.float32)
            for value in self.received:
                total = total + value[index].astype(jnp.float32)
            self.states.append(total.astype(jnp.float32 if last else jnp.bfloat16))
        self.received = None
        self.away = []
        if not last:
            self.prepare()


def split_kernel(flips, side_ref, acts_ref, *refs):
    count = len(flips)
    acts = acts_ref[...]
    for place, flip in enumerate(flips):
        grad_ref, add_ref = refs[2 * place], refs[2 * place + 1]
        kept_ref, away_ref = refs[2 * (count + place)], refs[2 * (count + place) + 1]
        total = over_rows(acts, grad_ref[...]) + add_ref[...].astype(jnp.float32)
        total = total.astype(jnp.bfloat16)
        half, rows, cols = kept_ref.shape
        parts = [[], []]
        for index in range(2 * half):
            bit = (index // 2) % 2 if flip else index % 2
            parts[bit].append(total[index * rows : (index + 1) * rows])

        def put(first, second, kept_ref=kept_ref, away_ref=away_ref, half=half):
            for index in range(half):
                kept_ref[index] = first[index]
                away_ref[index] = second[index]

        @pl.when(side_ref[1 + place] == 0)
        def _(put=put, parts=parts):
            put(parts[0], parts[1])

        @pl.when(side_ref[1 + place] != 0)
        def _(put=put, parts=parts):
            put(parts[1], parts[0])


def split_product(acts, grad, theirs, sizes, flips):
    masks, core = bit_masks(sizes)
    devices = sizes[0] * sizes[1]
    rows, inner = acts.shape
    count = len(flips)
    cols = grad.shape[1] // count
    block = inner // devices
    segment = inner // (2 * 2**core)
    tile = math.gcd(segment, 512)
    parts = segment // tile
    wide = math.gcd(cols, 1024 // count)
    steps = cols // wide
    firsts = [masks[-2] if flip else masks[-1] for flip in flips]
    sides = jnp.stack([small_index([mask], sizes) for mask in [masks[core]] + firsts])
    half = tile // (2 * block)
    out_spec = pl.BlockSpec((half, block, wide), lambda i, j, side_ref: (i, 0, j))
    out_shape = jax.ShapeDtypeStruct((devices // 4, block, cols), jnp.bfloat16)
    specs = [
        pl.BlockSpec(
            (rows, tile),
            lambda i, j, side_ref: (
                0,
                (i // parts) * 2 * parts + side_ref[0] * parts + i % parts,
            ),
        )
    ]
    for place in range(count):
        shift = place * steps
        specs.append(pl.BlockSpec((rows, wide), lambda i, j, side_ref, s=shift: (0, j + s)))
        specs.append(pl.BlockSpec((tile, wide), lambda i, j, side_ref, s=shift: (i, j + s)))
    return pl.pallas_call(
        functools.partial(split_kernel, flips),
        grid_spec=pltpu.PrefetchScalarGridSpec(
            num_scalar_prefetch=1,
            grid=(inner // (2 * tile), steps),
            in_specs=specs,
            out_specs=[out_spec] * (2 * count),
        ),
        out_shape=[out_shape] * (2 * count),
        cost_estimate=LIGHT,
        name="split_product",
    )(sides, acts, *([grad, theirs] * count))


def add_split_kernel(side_ref, *refs):
    count = len(refs) // 6
    for place in range(count):
        ins = refs[4 * place : 4 * place + 4]
        outs = refs[4 * count + 2 * place : 4 * count + 2 * place + 2]
        for out, one, two in zip(outs, ins[::2], ins[1::2]):
            out[...] = one[:, 0] + two[:, 0]


def add_split(kepts, values, bits):
    blocks = kepts[0].shape[0]
    part = math.gcd(blocks // 2, 4)
    specs, operands, out_specs, out_shapes = [], [], [], []
    for place, (kept, value) in enumerate(zip(kepts, values)):
        unused, rows, cols = kept.shape
        shape = (blocks // 2, 2, rows, cols)
        block = (part, 1, rows, cols)
        stays = pl.BlockSpec(block, lambda i, side_ref, p=place: (i, side_ref[p], 0, 0))
        goes = pl.BlockSpec(block, lambda i, side_ref, p=place: (i, 1 - side_ref[p], 0, 0))
        specs.extend([stays, stays, goes, goes])
        operands.extend([kept.reshape(shape), value.reshape(shape)] * 2)
        out_specs.extend([pl.BlockSpec((part, rows, cols), lambda i, side_ref: (i, 0, 0))] * 2)
        out_shapes.extend([jax.ShapeDtypeStruct((blocks // 2, rows, cols), kept.dtype)] * 2)
    outs = pl.pallas_call(
        add_split_kernel,
        grid_spec=pltpu.PrefetchScalarGridSpec(
            num_scalar_prefetch=1,
            grid=(blocks // (2 * part),),
            in_specs=specs,
            out_specs=out_specs,
        ),
        out_shape=out_shapes,
        cost_estimate=LIGHT,
        name="add_split",
    )(jnp.stack(bits), *operands)
    return list(outs[::2]), list(outs[1::2])


def add_join_kernel(count, place_ref, *refs):
    for slot, out in enumerate(refs[2 * count :]):

        @pl.when(pl.program_id(1) == slot)
        def _(out=out):
            start = 0
            for one, two in zip(refs[:count], refs[count : 2 * count]):
                total = one[0] + two[0]
                width = total.shape[-1]
                out[0, :, start : start + width] = total
                start += width


def add_join(kept, received, bit):
    blocks, rows, unused = kept[0].shape
    width = sum(value.shape[2] for value in kept)
    specs = [
        pl.BlockSpec(
            (1, rows, value.shape[2]), lambda i, j, side_ref: (2 * i + (side_ref[0] ^ j), 0, 0)
        )
        for value in kept
    ]
    return pl.pallas_call(
        functools.partial(add_join_kernel, len(kept)),
        grid_spec=pltpu.PrefetchScalarGridSpec(
            num_scalar_prefetch=1,
            grid=(blocks // 2, 2),
            in_specs=specs + specs,
            out_specs=[pl.BlockSpec((1, rows, width), lambda i, j, side_ref: (i, 0, 0))] * 2,
        ),
        out_shape=[jax.ShapeDtypeStruct((blocks // 2, rows, width), kept[0].dtype)] * 2,
        cost_estimate=LIGHT,
        name="add_join",
    )(bit.reshape(1), *kept, *received)


class Joint:
    def __init__(self, parts, sizes):
        self.sizes = sizes
        masks, core = bit_masks(sizes)
        self.near = masks[-2:]
        self.far = far_groups(sizes)[0]
        self.flips, self.kept, self.away = [], [], []
        for exchange, flips in parts:
            outs = split_product(exchange.acts, exchange.grad, exchange.theirs, sizes, flips)
            self.kept.extend(outs[::2])
            self.away.extend(outs[1::2])
            self.flips.extend(flips)
        self.masks = [self.near[0] if flip else self.near[1] for flip in self.flips]
        self.received = None
        self.stage = 0

    def send(self):
        self.received = [swap(away, mask, self.sizes) for away, mask in zip(self.away, self.masks)]

    def take(self):
        received, self.received = self.received, None
        self.stage += 1
        if self.stage == 1:
            self.masks = [self.near[1] if flip else self.near[0] for flip in self.flips]
            bits = [small_index([mask], self.sizes) for mask in self.masks]
            self.kept, self.away = add_split(self.kept, received, bits)
        elif self.stage == 2:
            self.masks = [self.far[1]]
            kept, away = add_join(self.kept, received, small_index(self.masks, self.sizes))
            self.kept, self.away = [kept], [away]
        elif self.stage == 3:
            self.masks = [self.far[0]]
            bits = [small_index(self.masks, self.sizes)]
            self.kept, self.away = add_split(self.kept, received, bits)
        else:
            self.total = self.kept[0][0].astype(jnp.float32) + received[0][0].astype(jnp.float32)
            self.away = []

    def result(self):
        return self.total


class Plain:
    def __init__(self, parts, sizes):
        self.chains = []
        for exchange, flips in parts:
            kept = half_product(exchange.acts, exchange.grad, sizes, exchange.theirs)
            self.chains.append(Scatter([kept], sizes, flips[0]))
        self.received = None

    @property
    def away(self):
        return [away for chain in self.chains for away in chain.away]

    @away.setter
    def away(self, values):
        values = list(values)
        for chain in self.chains:
            count = len(chain.away)
            chain.away, values = values[:count], values[count:]

    def send(self):
        for chain in self.chains:
            chain.send()
        self.received = [value for chain in self.chains for value in chain.received]

    def take(self):
        values, self.received = list(self.received), None
        for chain in self.chains:
            count = len(chain.received)
            chain.received, values = values[:count], values[count:]
            chain.take()

    def result(self):
        return jnp.concatenate([chain.states[0][0] for chain in self.chains], axis=1)


def summed(parts, sizes):
    heights = [exchange.acts.shape[1] // (sizes[0] * sizes[1]) for exchange, unused in parts]
    groups = far_groups(sizes)
    fits = all(height % 16 == 0 for height in heights)
    if len(groups) == 1 and len(groups[0]) == 2 and fits:
        return Joint(parts, sizes)
    return Plain(parts, sizes)


class VectorScatter:
    def __init__(self, terms, sizes):
        self.sizes = sizes
        masks, core = bit_masks(sizes)
        self.bits = masks
        self.todo = [masks[core]] + [mask for mask in masks[::-1] if mask != masks[core]]
        self.state = terms
        self.received = None
        self.prepare()

    def prepare(self):
        bit = self.todo[0]
        high = 2 ** self.bits.index(bit)
        self.bits = [other for other in self.bits if other != bit]
        view = self.state.reshape(high, 2, -1, self.state.shape[-1])
        place = small_index([bit], self.sizes)
        away = lax.dynamic_index_in_dim(view, 1 - place, 1, keepdims=False)
        kept = lax.dynamic_index_in_dim(view, place, 1, keepdims=False)
        self.away = [away.reshape(-1, away.shape[-1])]
        self.kept = kept.reshape(-1, kept.shape[-1])
        self.mask = bit
        self.todo = self.todo[1:]

    def send(self):
        self.received = [swap(self.away[0], self.mask, self.sizes)]

    def take(self):
        self.state = self.kept + self.received[0]
        self.received = None
        self.away = []
        if self.todo:
            self.prepare()


def scatter_round(ending, starting, *others):
    ending = [chain for chain in ending if chain.received is not None]
    others = ended(ending, *others)
    going = [chain for chain in starting if chain.away and chain.received is None]
    flat = [value for chain in going for value in chain.away]
    held = list(pinned(*flat, *others))
    for chain in going:
        count = len(chain.away)
        chain.away, held = held[:count], held[count:]
        chain.send()
    return held


def gelu_and_slope(preact):
    square = preact * preact
    bent = jnp.tanh(preact * (0.7978845608028654 + (0.7978845608028654 * 0.044715) * square))
    half = 0.5 + 0.5 * bent
    value = preact * half
    inner = 0.7978845608028654 + (3 * 0.7978845608028654 * 0.044715) * square
    slope = half + value * (1.0 - bent) * inner
    return value.astype(jnp.bfloat16), slope.astype(jnp.bfloat16)


def times(left, right):
    return jnp.dot(left, right, preferred_element_type=jnp.float32)


def grad_pre_kernel(grad_ref, weight_ref, slope_ref, out_ref, bias_ref):
    weight = weight_ref[...]
    total = None
    for start in range(0, grad_ref.shape[0], 256):
        grad_act = against(grad_ref[start : start + 256], weight)
        slope = slope_ref[start : start + 256].astype(jnp.float32)
        grad_pre = (grad_act * slope).astype(jnp.bfloat16)
        out_ref[start : start + 256] = grad_pre
        term = jnp.sum(grad_pre.astype(jnp.float32), axis=0, keepdims=True)
        total = term if total is None else total + term
    bias_ref[...] = total


def grad_two_kernel(grad_ref, weight_ref, out_ref):
    term = against(grad_ref[...], weight_ref[...])

    @pl.when(pl.program_id(0) == 0)
    def _():
        out_ref[...] = term

    @pl.when(pl.program_id(0) != 0)
    def _():
        out_ref[...] += term


def grad_two_of(grad_pre, w_up):
    rows, hidden = grad_pre.shape
    width = w_up.shape[0]
    tile = 1024
    return pl.pallas_call(
        grad_two_kernel,
        grid=(hidden // tile,),
        in_specs=[
            pl.BlockSpec((rows, tile), lambda i: (0, i)),
            pl.BlockSpec((width, tile), lambda i: (0, i)),
        ],
        out_specs=pl.BlockSpec((rows, width), lambda i: (0, 0)),
        out_shape=jax.ShapeDtypeStruct((rows, width), jnp.float32),
        cost_estimate=LIGHT,
        name="grad_two",
    )(grad_pre, w_up)


def grad_pre_of(grad_low, w_down, slope):
    rows, width = grad_low.shape
    hidden = w_down.shape[0]
    tile = 1024
    grad_pre, bias = pl.pallas_call(
        grad_pre_kernel,
        grid=(hidden // tile,),
        in_specs=[
            pl.BlockSpec((rows, width), lambda i: (0, 0)),
            pl.BlockSpec((tile, width), lambda i: (i, 0)),
            pl.BlockSpec((rows, tile), lambda i: (0, i)),
        ],
        out_specs=[
            pl.BlockSpec((rows, tile), lambda i: (0, i)),
            pl.BlockSpec((1, tile), lambda i: (0, i)),
        ],
        out_shape=[
            jax.ShapeDtypeStruct((rows, hidden), jnp.bfloat16),
            jax.ShapeDtypeStruct((1, hidden), jnp.float32),
        ],
        cost_estimate=LIGHT,
        name="grad_pre",
    )(grad_low, w_down, slope)
    return grad_pre, bias.reshape(hidden)


def local(
    sizes,
    frame_input,
    code_embed,
    segment_ids,
    frame_cotangent,
    code_cotangent,
    frame_prenorm,
    frame_query,
    frame_keys,
    frame_values,
    frame_outproj,
    frame_midnorm,
    frame_upproj,
    frame_upbias,
    frame_downproj,
    frame_downbias,
    code_prenorm,
    code_query,
    code_keys,
    code_values,
    code_outproj,
    code_midnorm,
    code_upproj,
    code_upbias,
    code_downproj,
    code_downbias,
):
    low = jnp.bfloat16
    frames = frame_input.shape[0]
    devices = sizes[0] * sizes[1]
    vectors = (
        frame_prenorm,
        frame_midnorm,
        frame_upbias,
        frame_downbias,
        code_prenorm,
        code_midnorm,
        code_upbias,
        code_downbias,
    )
    widths = [vec.shape[0] for vec in vectors]

    shard_rows = frame_values.shape[0]
    packed = jnp.concatenate([vec[None] for vec in vectors], axis=1)
    packed = jnp.pad(packed, ((0, 0), (0, shard_rows * 128 - packed.shape[1])))
    packed = packed.reshape(shard_rows, 128)
    f_ab = Gather(
        jnp.stack(
            [
                jnp.concatenate([frame_query, frame_keys, packed], axis=1),
                jnp.concatenate([frame_values, frame_outproj, packed], axis=1),
            ]
        ),
        sizes,
        (False, True),
        ([2 * D, 128], [D, D, 128]),
    )
    c_ab = Gather(
        jnp.stack(
            [
                jnp.concatenate([code_query, code_keys], axis=1),
                jnp.concatenate([code_values, code_outproj], axis=1),
            ]
        ),
        sizes,
        (False, True),
        ([2 * D], [D, D]),
    )

    def gathered(shard):
        return lax.all_gather(shard, ("gx", "gy"), axis=0, tiled=True)

    f_up, f_down = gathered(frame_upproj), gathered(frame_downproj)
    c_up = gathered(code_upproj)
    c_d = Gather(code_downproj[None], sizes, (True,), ([D],))
    for unused in range(len(f_ab.far) - 1):
        started([f_ab])
        ended([f_ab])
        started([c_ab])
        ended([c_ab])
        started([c_d])
        ended([c_d])
    started([f_ab])
    ended([f_ab])
    started([f_ab])
    code_rows = jnp.swapaxes(code_embed, 0, 1)
    grad_code_y = jnp.swapaxes(code_cotangent, 0, 1)
    code_rows, grad_code_y = ended([f_ab], code_rows, grad_code_y)
    started([f_ab, c_ab])
    ended([f_ab, c_ab])
    started([f_ab, c_ab])
    ended([f_ab, c_ab])
    f_pair = f_ab.whole[0][0]
    f_value, f_out, tail = f_ab.whole[1]
    whole = tail.reshape(devices, -1)[:, : sum(widths)].astype(jnp.float32)
    gains = []
    start = 0
    for width in widths:
        gains.append(whole[:, start : start + width].reshape(devices * width))
        start += width
    frame_gains = tuple(gains[:4])
    code_gains = tuple(gains[4:])
    frame_x = frame_input.astype(jnp.float32)
    f_normed = rms_scale(frame_x, frame_gains[0]).astype(low)
    started([c_ab, c_d])
    segments = segment_ids[0]
    f_qk = times(f_normed, f_pair).astype(low)
    f_v = times(f_normed, f_value).astype(low)
    f_mixed = frame_attend(f_qk, f_v, segments)
    f_qk, f_v, f_mixed = ended([c_ab, c_d], f_qk, f_v, f_mixed)
    started([c_ab, c_d])
    f_hidden = frame_x + times(f_mixed, f_out)
    f_normed_two = rms_scale(f_hidden, frame_gains[1]).astype(low)
    f_hidden, f_normed_two = ended([c_ab, c_d], f_hidden, f_normed_two)
    started([c_d])
    f_act, f_slope = gelu_and_slope(times(f_normed_two, f_up) + frame_gains[2])
    rows = CB * frames
    grad_code_y = grad_code_y.reshape(rows, D)
    frame_y = f_hidden + (times(f_act, f_down) + frame_gains[3])

    def tokens_of(value):
        return value.reshape(CB, frames, value.shape[-1])

    code_x = (code_rows.astype(jnp.float32) + frame_y[None]).reshape(rows, D)
    c_normed = rms_scale(code_x, code_gains[0]).astype(low)
    c_pair = c_ab.whole[0][0]
    c_value, c_out = c_ab.whole[1]
    c_qk = times(c_normed, c_pair).astype(low)
    c_v = times(c_normed, c_value).astype(low)
    c_mixed = code_attend(tokens_of(c_qk), tokens_of(c_v)).reshape(rows, D)
    c_hidden = code_x + times(c_mixed, c_out)
    (c_hidden,) = ended([c_d], c_hidden)
    started([c_d])
    c_normed_two = rms_scale(c_hidden, code_gains[1]).astype(low)
    (c_normed_two,) = ended([c_d], c_normed_two)
    ((c_down,),) = c_d.whole
    c_act, c_slope = gelu_and_slope(times(c_normed_two, c_up) + code_gains[2])

    def both(exchange):
        return [summed([(exchange, (True, False))], sizes)]

    def attention_sums(pair, value, outproj):
        parts = [(pair, (False,)), (value, (True,)), (outproj, (True,))]
        return [summed(parts, sizes)]

    def norm_back(grad_out, inputs, gain):
        unused, back = jax.vjp(rms_scale, inputs, gain)
        return back(grad_out)

    grad_low = grad_code_y
    c_d_core = Core(c_act, grad_low, sizes)
    c_slope, grad_low = scatter_round([], [c_d_core], c_slope, grad_low)
    c_grad_b_down = jnp.sum(grad_low.astype(jnp.float32), axis=0)
    (c_grad_b_down,) = ended([c_d_core], c_grad_b_down)
    c_d_chain = both(c_d_core)
    c_slope, grad_low = scatter_round([], c_d_chain, c_slope, grad_low)
    grad_pre, c_grad_b_up = grad_pre_of(grad_low, c_down, c_slope)
    c_u_core = Core(c_normed_two, grad_pre, sizes)
    (grad_pre,) = scatter_round(c_d_chain, c_d_chain + [c_u_core], grad_pre)
    grad_two = grad_two_of(grad_pre, c_up)
    (grad_two,) = scatter_round(c_d_chain + [c_u_core], c_d_chain, grad_two)
    c_u_chain = both(c_u_core)
    grad_part, c_grad_mid = norm_back(grad_two, c_hidden, code_gains[1])
    grad_hidden = grad_low.astype(jnp.float32) + grad_part
    grad_attn = grad_hidden.astype(low)
    grad_attn, grad_hidden = scatter_round(
        c_d_chain, c_d_chain + c_u_chain, grad_attn, grad_hidden
    )
    c_o_core = Core(c_mixed, grad_attn, sizes)
    grad_mixed = against(grad_attn, c_out).astype(low)
    grad_pair, grad_values = code_attend_back(
        tokens_of(c_qk), tokens_of(c_v), tokens_of(grad_mixed)
    )
    grad_pair = grad_pair.reshape(rows, 2 * D)
    grad_values = grad_values.reshape(rows, D)
    grad_pair, grad_values = scatter_round(
        c_d_chain + c_u_chain, c_u_chain + [c_o_core], grad_pair, grad_values
    )
    c_p_core = Core(c_normed, grad_pair, sizes)
    c_v_core = Core(c_normed, grad_values, sizes)
    grad_pair, grad_values = scatter_round(
        c_u_chain + [c_o_core], c_u_chain + [c_p_core, c_v_core], grad_pair, grad_values
    )
    grad_normed = against(grad_pair, c_pair) + against(grad_values, c_value)
    grad_part, c_grad_pre = norm_back(grad_normed, code_x, code_gains[0])
    grad_code_x = grad_hidden + grad_part
    grad_frame_y = frame_cotangent.astype(jnp.float32) + jnp.sum(tokens_of(grad_code_x), axis=0)
    grad_code_x, grad_frame_y = scatter_round(
        c_u_chain + [c_p_core, c_v_core], c_u_chain, grad_code_x, grad_frame_y
    )
    c_sums = attention_sums(c_p_core, c_v_core, c_o_core)
    (grad_frame_y,) = scatter_round(c_u_chain, c_sums, grad_frame_y)

    grad_low = grad_frame_y.astype(low)
    f_d_core = Core(f_act, grad_low, sizes)
    grad_pre, f_grad_b_up = grad_pre_of(grad_low, f_down, f_slope)
    f_u_core = Core(f_normed_two, grad_pre, sizes)
    (grad_pre,) = scatter_round(c_sums, c_sums + [f_d_core, f_u_core], grad_pre)
    grad_two = grad_two_of(grad_pre, f_up)
    grad_part, f_grad_mid = norm_back(grad_two, f_hidden, frame_gains[1])
    grad_hidden = grad_frame_y + grad_part
    grad_attn = grad_hidden.astype(low)
    grad_attn, grad_hidden = scatter_round(
        c_sums + [f_d_core, f_u_core], c_sums, grad_attn, grad_hidden
    )
    f_d_chain = both(f_d_core)
    grad_attn, grad_hidden = scatter_round(
        c_sums, c_sums + f_d_chain, grad_attn, grad_hidden
    )
    f_u_chain = both(f_u_core)
    f_o_core = Core(f_mixed, grad_attn, sizes)
    grad_mixed = against(grad_attn, f_out).astype(low)
    grad_pair, grad_values = frame_attend_back(f_qk, f_v, grad_mixed, segments)
    grad_pair, grad_values, c_act = scatter_round(
        c_sums + f_d_chain, f_d_chain + f_u_chain + [f_o_core], grad_pair, grad_values, c_act
    )
    f_p_core = Core(f_normed, grad_pair, sizes)
    f_v_core = Core(f_normed, grad_values, sizes)
    code_y = c_hidden + (times(c_act, c_down) + code_gains[3])
    code_y, grad_pair, grad_values = scatter_round(
        f_d_chain + f_u_chain + [f_o_core],
        f_d_chain + f_u_chain + [f_p_core, f_v_core],
        code_y,
        grad_pair,
        grad_values,
    )
    grad_normed = against(grad_pair, f_pair) + against(grad_values, f_value)
    grad_part, f_grad_pre = norm_back(grad_normed, frame_x, frame_gains[0])
    grad_frame_x = grad_hidden + grad_part
    f_grad_b_down = jnp.sum(grad_low.astype(jnp.float32), axis=0)
    terms = jnp.concatenate(
        [
            term.reshape(devices, -1)
            for term in (
                f_grad_pre,
                f_grad_mid,
                f_grad_b_up,
                f_grad_b_down,
                c_grad_pre,
                c_grad_mid,
                c_grad_b_up,
                c_grad_b_down,
            )
        ],
        axis=1,
    )
    row = VectorScatter(terms, sizes)
    (grad_frame_x,) = scatter_round(
        f_d_chain + f_u_chain + [f_p_core, f_v_core],
        f_d_chain + f_u_chain + [row],
        grad_frame_x,
    )
    f_sums = attention_sums(f_p_core, f_v_core, f_o_core)
    (code_y,) = scatter_round(
        f_d_chain + f_u_chain + [row], f_d_chain + f_u_chain + f_sums + [row], code_y
    )
    frame_output = frame_y.astype(low)
    code_output = jnp.swapaxes(tokens_of(code_y.astype(low)), 0, 1)
    (code_output,) = scatter_round(f_u_chain + f_sums + [row], f_sums + [row], code_output)
    code_embed_grad = jnp.swapaxes(tokens_of(grad_code_x), 0, 1)
    (code_embed_grad,) = scatter_round(f_sums + [row], f_sums + [row], code_embed_grad)
    everything = c_d_chain + c_u_chain + c_sums + f_d_chain + f_u_chain + f_sums + [row]
    while True:
        started([chain for chain in everything if chain.away and chain.received is None])
        going = [chain for chain in everything if chain.received is not None]
        if not going:
            break
        ended(going)
    sums = row.state[0]
    pieces = []
    start = 0
    for width in widths:
        pieces.append(sums[start : start + width])
        start += width

    def arranged(attn_sums, up_sums, down_sums, vecs):
        total = attn_sums[0].result()
        prenorm, midnorm, upbias, downbias = vecs
        return (
            prenorm,
            total[:, :D],
            total[:, D : 2 * D],
            total[:, 2 * D : 3 * D],
            total[:, 3 * D :],
            midnorm,
            up_sums,
            upbias,
            down_sums,
            downbias,
        )

    code_outs = arranged(c_sums, c_u_chain[0].result(), c_d_chain[0].result(), pieces[4:])
    frame_outs = arranged(
        f_sums, f_u_chain[0].result(), f_d_chain[0].result(), pieces[:4]
    )
    return (frame_output, code_output, grad_frame_x, code_embed_grad) + frame_outs + code_outs


def solution(mesh):
    in_specs = (
        P(("gx", "gy"), None),
        P(("gx", "gy"), None, None),
        P(("gx", "gy"), None),
        P(("gx", "gy"), None),
        P(("gx", "gy"), None, None),
        P(("gx", "gy")),
        P(("gx", "gy"), None),
        P(("gx", "gy"), None),
        P(("gx", "gy"), None),
        P(("gx", "gy"), None),
        P(("gx", "gy")),
        P(("gx", "gy"), None),
        P(("gx", "gy")),
        P(("gx", "gy"), None),
        P(("gx", "gy")),
        P(("gx", "gy")),
        P(("gx", "gy"), None),
        P(("gx", "gy"), None),
        P(("gx", "gy"), None),
        P(("gx", "gy"), None),
        P(("gx", "gy")),
        P(("gx", "gy"), None),
        P(("gx", "gy")),
        P(("gx", "gy"), None),
        P(("gx", "gy")),
    )
    out_specs = (
        P(("gx", "gy"), None),
        P(("gx", "gy"), None, None),
        P(("gx", "gy"), None),
        P(("gx", "gy"), None, None),
        P(("gx", "gy")),
        P(("gx", "gy"), None),
        P(("gx", "gy"), None),
        P(("gx", "gy"), None),
        P(("gx", "gy"), None),
        P(("gx", "gy")),
        P(("gx", "gy"), None),
        P(("gx", "gy")),
        P(("gx", "gy"), None),
        P(("gx", "gy")),
        P(("gx", "gy")),
        P(("gx", "gy"), None),
        P(("gx", "gy"), None),
        P(("gx", "gy"), None),
        P(("gx", "gy"), None),
        P(("gx", "gy")),
        P(("gx", "gy"), None),
        P(("gx", "gy")),
        P(("gx", "gy"), None),
        P(("gx", "gy")),
    )
    sizes = (mesh.shape["gx"], mesh.shape["gy"])
    return jax.shard_map(
        functools.partial(local, sizes), mesh=mesh, in_specs=in_specs, out_specs=out_specs, check_vma=False)
```

```python
import functools
import math

import jax
import jax.numpy as jnp
from jax import lax
from jax.experimental import pallas as pl
from jax.experimental.pallas import tpu as pltpu
from jax.sharding import PartitionSpec as P

D = 1024
HEADS = 16
HD = 64
CB = 3
LIGHT = pl.CostEstimate(flops=1, bytes_accessed=1, transcendentals=0)


def gelu_tanh(value):
    return (
        0.5
        * value
        * (1.0 + jnp.tanh(0.7978845608028654 * (value + 0.044715 * value * value * value)))
    )


def rms_scale(value, gain_vec):
    return value * lax.rsqrt(jnp.mean(value * value, axis=-1, keepdims=True) + 1e-05) * gain_vec


def over_rows(left, right):
    return lax.dot_general(
        left, right, (((0,), (0,)), ((), ())), preferred_element_type=jnp.float32
    )


def against(left, right):
    return lax.dot_general(
        left, right, (((1,), (1,)), ((), ())), preferred_element_type=jnp.float32
    )


def head_marks():
    lane = lax.broadcasted_iota(jnp.int32, (D, 128), 0) // HD
    head = lax.broadcasted_iota(jnp.int32, (D, 128), 1)
    return (lane == head).astype(jnp.bfloat16)


def head_sums(left, right, marks):
    product = left.astype(jnp.float32) * right.astype(jnp.float32)
    upper = product.astype(jnp.bfloat16)
    lower = (product - upper.astype(jnp.float32)).astype(jnp.bfloat16)
    return jnp.dot(upper, marks, preferred_element_type=jnp.float32) + jnp.dot(
        lower, marks, preferred_element_type=jnp.float32
    )


def spread(heads, marks):
    return lax.dot_general(
        heads, marks, (((1,), (1,)), ((), ())), preferred_element_type=jnp.float32
    )


def token_probs(tokens_q, tokens_k, marks):
    probs = []
    for token in range(CB):
        scores = [
            head_sums(tokens_q[token], tokens_k[other], marks) * HD ** (-0.5)
            for other in range(token + 1)
        ]
        highest = functools.reduce(jnp.maximum, scores)
        expo = [jnp.exp(score - highest) for score in scores]
        total = functools.reduce(jnp.add, expo)
        probs.append([term / total for term in expo])
    return probs


def code_attend_kernel(pair_ref, values_ref, marks_ref, out_ref):
    marks = marks_ref[...]
    query = [pair_ref[token, :, :D] for token in range(CB)]
    keys = [pair_ref[token, :, D:] for token in range(CB)]
    probs = token_probs(query, keys, marks)
    for token in range(CB):
        mixed = None
        for other in range(token + 1):
            value = values_ref[other].astype(jnp.float32)
            term = spread(probs[token][other].astype(jnp.bfloat16), marks) * value
            mixed = term if mixed is None else mixed + term
        out_ref[token] = mixed.astype(jnp.bfloat16)


def code_attend_back_kernel(
    pair_ref, values_ref, grad_ref, marks_ref, out_pair_ref, out_values_ref
):
    marks = marks_ref[...]
    query = [pair_ref[token, :, :D] for token in range(CB)]
    keys = [pair_ref[token, :, D:] for token in range(CB)]
    probs = token_probs(query, keys, marks)
    grad_scores = []
    for token in range(CB):
        grads = [
            head_sums(grad_ref[token], values_ref[other], marks)
            for other in range(token + 1)
        ]
        inner = functools.reduce(
            jnp.add, [prob * grad for prob, grad in zip(probs[token], grads)]
        )
        grad_scores.append(
            [
                (prob * (grad - inner)).astype(jnp.bfloat16)
                for prob, grad in zip(probs[token], grads)
            ]
        )
    scale = HD ** (-0.5)
    grad_keys = [None] * CB
    grad_values = [None] * CB
    for token in range(CB):
        grad_query = None
        for other in range(token + 1):
            wide = spread(grad_scores[token][other], marks)
            term = wide * keys[other].astype(jnp.float32)
            grad_query = term if grad_query is None else grad_query + term
            term = wide * query[token].astype(jnp.float32)
            grad_keys[other] = term if grad_keys[other] is None else grad_keys[other] + term
            wide = spread(probs[token][other].astype(jnp.bfloat16), marks)
            term = wide * grad_ref[token].astype(jnp.float32)
            grad_values[other] = term if grad_values[other] is None else grad_values[other] + term
        out_pair_ref[token, :, :D] = (grad_query * scale).astype(jnp.bfloat16)
    for token in range(CB):
        out_pair_ref[token, :, D:] = (grad_keys[token] * scale).astype(jnp.bfloat16)
        out_values_ref[token] = grad_values[token].astype(jnp.bfloat16)


def token_specs(step, widths):
    return [pl.BlockSpec((CB, step, width), lambda i: (0, i, 0)) for width in widths] + [
        pl.BlockSpec((D, 128), lambda i: (0, 0))
    ]


def code_attend(pair, values):
    frames = values.shape[1]
    step = math.gcd(frames, 64)
    return pl.pallas_call(
        code_attend_kernel,
        grid=(frames // step,),
        in_specs=token_specs(step, (2 * D, D)),
        out_specs=pl.BlockSpec((CB, step, D), lambda i: (0, i, 0)),
        out_shape=jax.ShapeDtypeStruct((CB, frames, D), jnp.bfloat16),
        cost_estimate=LIGHT,
        name="code_attend",
    )(pair, values, head_marks())


def code_attend_back(pair, values, grad_mixed):
    frames = values.shape[1]
    step = math.gcd(frames, 64)
    return pl.pallas_call(
        code_attend_back_kernel,
        grid=(frames // step,),
        in_specs=token_specs(step, (2 * D, D, D)),
        out_specs=[
            pl.BlockSpec((CB, step, 2 * D), lambda i: (0, i, 0)),
            pl.BlockSpec((CB, step, D), lambda i: (0, i, 0)),
        ],
        out_shape=[
            jax.ShapeDtypeStruct((CB, frames, 2 * D), jnp.bfloat16),
            jax.ShapeDtypeStruct((CB, frames, D), jnp.bfloat16),
        ],
        cost_estimate=LIGHT,
        name="code_attend_back",
    )(pair, values, grad_mixed, head_marks())


def frame_mask(column_ref, row_ref):
    frames = column_ref.shape[0]
    shape = (frames, frames)
    earlier = lax.broadcasted_iota(jnp.int32, shape, 0) >= lax.broadcasted_iota(
        jnp.int32, shape, 1
    )
    return earlier & (column_ref[...] == row_ref[...])


def frame_probs(query, keys, allowed):
    scores = against(query, keys) * HD ** (-0.5)
    scores = jnp.where(allowed, scores, -1e30)
    highest = jnp.max(scores, axis=-1, keepdims=True)
    expo = jnp.exp(scores - highest)
    return expo / jnp.sum(expo, axis=-1, keepdims=True)


def half_lanes(value, upper):
    lane = lax.broadcasted_iota(jnp.int32, value.shape, 1)
    chosen = (lane >= HD) if upper else (lane < HD)
    return jnp.where(chosen, value, jnp.zeros_like(value))


def frame_attend_kernel(query_ref, keys_ref, values_ref, column_ref, row_ref, out_ref):
    allowed = frame_mask(column_ref, row_ref)
    mixed = None
    for upper in (False, True):
        probs = frame_probs(half_lanes(query_ref[...], upper), keys_ref[...], allowed)
        term = jnp.dot(
            probs.astype(jnp.bfloat16),
            half_lanes(values_ref[...], upper),
            preferred_element_type=jnp.float32,
        )
        mixed = term if mixed is None else mixed + term
    out_ref[...] = mixed.astype(jnp.bfloat16)


def frame_attend_back_kernel(
    query_ref, keys_ref, values_ref, grad_ref, column_ref, row_ref, out_pair_ref, out_values_ref
):
    allowed = frame_mask(column_ref, row_ref)
    scale = HD ** (-0.5)
    grads = [None, None, None]
    for upper in (False, True):
        query = half_lanes(query_ref[...], upper)
        keys = half_lanes(keys_ref[...], upper)
        grad_out = half_lanes(grad_ref[...], upper)
        probs = frame_probs(query, keys, allowed)
        grad_probs = against(grad_out, values_ref[...])
        inner = jnp.sum(probs * grad_probs, axis=-1, keepdims=True)
        grad_scores = (probs * (grad_probs - inner)).astype(jnp.bfloat16)
        terms = (
            jnp.dot(grad_scores, keys, preferred_element_type=jnp.float32) * scale,
            over_rows(grad_scores, query) * scale,
            over_rows(probs.astype(jnp.bfloat16), grad_out),
        )
        grads = [term if grad is None else grad + term for grad, term in zip(grads, terms)]
    start = pl.multiple_of(pl.program_id(0) * 2 * HD, 2 * HD)
    out_pair_ref[:, pl.ds(start, 2 * HD)] = grads[0].astype(jnp.bfloat16)
    out_pair_ref[:, pl.ds(D + start, 2 * HD)] = grads[1].astype(jnp.bfloat16)
    out_values_ref[...] = grads[2].astype(jnp.bfloat16)


def pair_specs(frames, extra):
    pairs = HEADS // 2
    block = (frames, 2 * HD)
    return (
        [
            pl.BlockSpec(block, lambda j: (0, j)),
            pl.BlockSpec(block, lambda j: (0, j + pairs)),
        ]
        + [pl.BlockSpec(block, lambda j: (0, j))] * extra
        + [
            pl.BlockSpec((frames, 1), lambda j: (0, 0)),
            pl.BlockSpec((1, frames), lambda j: (0, 0)),
        ]
    )


def frame_attend(pair, values, segments):
    frames = values.shape[0]
    return pl.pallas_call(
        frame_attend_kernel,
        grid=(HEADS // 2,),
        in_specs=pair_specs(frames, 1),
        out_specs=pl.BlockSpec((frames, 2 * HD), lambda j: (0, j)),
        out_shape=jax.ShapeDtypeStruct((frames, D), jnp.bfloat16),
        cost_estimate=LIGHT,
        name="frame_attend",
    )(pair, pair, values, segments.reshape(frames, 1), segments.reshape(1, frames))


def frame_attend_back(pair, values, grad_mixed, segments):
    frames = values.shape[0]
    return pl.pallas_call(
        frame_attend_back_kernel,
        grid=(HEADS // 2,),
        in_specs=pair_specs(frames, 2),
        out_specs=[
            pl.BlockSpec((frames, 2 * D), lambda j: (0, 0)),
            pl.BlockSpec((frames, 2 * HD), lambda j: (0, j)),
        ],
        out_shape=[
            jax.ShapeDtypeStruct((frames, 2 * D), jnp.bfloat16),
            jax.ShapeDtypeStruct((frames, D), jnp.bfloat16),
        ],
        cost_estimate=LIGHT,
        name="frame_attend_back",
    )(
        pair,
        pair,
        values,
        grad_mixed,
        segments.reshape(frames, 1),
        segments.reshape(1, frames),
    )


def bit_masks(sizes):
    count = sizes[0] * sizes[1]
    masks = []
    step = count // 2
    while step >= 1:
        masks.append(step)
        step //= 2
    return masks, masks.index(sizes[1])


def swap(value, mask, sizes):
    count = sizes[0] * sizes[1]
    return lax.ppermute(value, ("gx", "gy"), [(place, place ^ mask) for place in range(count)])


def device_index(sizes):
    return lax.axis_index("gx") * sizes[1] + lax.axis_index("gy")


def far_groups(sizes):
    masks, core = bit_masks(sizes)
    far = [mask for place, mask in enumerate(masks[:-2]) if place != core]
    return [far[start : start + 2] for start in range(0, len(far), 2)]


def combined(group):
    found = []
    for index in range(2 ** len(group)):
        mask = 0
        for place, bit in enumerate(group):
            if (index >> (len(group) - 1 - place)) & 1:
                mask |= bit
        found.append(mask)
    return found


def small_index(group, sizes):
    me = device_index(sizes)
    index = jnp.zeros((), jnp.int32)
    for bit in group:
        index = index * 2 + ((me // bit) % 2).astype(jnp.int32)
    return index


def spans(done, pos):
    high = 2 ** sum(1 for other in done if other < pos)
    low = 2 ** sum(1 for other in done if other > pos)
    return high, low


def merge_kernel(bit_ref, mine_ref, theirs_ref, *outs):
    def put(first, second):
        start = 0
        for out in outs:
            width = out.shape[-1]
            out[0, 0] = first[0, :, start : start + width]
            out[0, 1] = second[0, :, start : start + width]
            start += width

    @pl.when(bit_ref[0] == 0)
    def _():
        put(mine_ref, theirs_ref)

    @pl.when(bit_ref[0] != 0)
    def _():
        put(theirs_ref, mine_ref)


def merged(mine, theirs, bit, splits):
    planes, rows, cols = mine.shape
    part = rows
    while part % 2 == 0 and part * cols > 512 * 1024:
        part //= 2
    read = pl.BlockSpec((1, part, cols), lambda i, j, bit_ref: (i, j, 0))
    return pl.pallas_call(
        merge_kernel,
        grid_spec=pltpu.PrefetchScalarGridSpec(
            num_scalar_prefetch=1,
            grid=(planes, rows // part),
            in_specs=[read, read],
            out_specs=[
                pl.BlockSpec((1, 2, part, width), lambda i, j, bit_ref: (i, 0, j, 0))
                for width in splits
            ],
        ),
        out_shape=[
            jax.ShapeDtypeStruct((planes, 2, rows, width), mine.dtype) for width in splits
        ],
        cost_estimate=LIGHT,
        name="merge",
    )(bit.reshape(1), mine, theirs)


def place_far_kernel(place_ref, *refs):
    for index, ref in enumerate(refs[:-1]):
        refs[-1][0, place_ref[0] ^ index] = ref[0]


def placed_far(pieces, place):
    planes, rows, cols = pieces[0].shape
    slots = len(pieces)
    return pl.pallas_call(
        place_far_kernel,
        grid_spec=pltpu.PrefetchScalarGridSpec(
            num_scalar_prefetch=1,
            grid=(planes,),
            in_specs=[pl.BlockSpec((1, rows, cols), lambda i, place_ref: (i, 0, 0))] * slots,
            out_specs=pl.BlockSpec((1, slots, rows, cols), lambda i, place_ref: (i, 0, 0, 0)),
        ),
        out_shape=jax.ShapeDtypeStruct((planes, slots, rows, cols), pieces[0].dtype),
        cost_estimate=LIGHT,
        name="place_far",
    )(place.reshape(1), *pieces)


def pinned(*values):
    return lax.optimization_barrier(values)


def gather_order(sizes, flip):
    masks, core = bit_masks(sizes)
    count = len(masks)
    far = [place for place in range(count - 2) if place != core]
    near = [count - 1, count - 2] if flip else [count - 2, count - 1]
    return far + near + [core]


class Gather:
    def __init__(self, shards, sizes, flips, splits):
        self.sizes = sizes
        self.flips, self.splits = flips, splits
        masks, core = bit_masks(sizes)
        self.masks, self.core = masks, core
        self.far = far_groups(sizes)
        self.states = [shards]
        self.received = None
        self.stage = -len(self.far)

    def near_masks(self, second):
        return [self.masks[-1 if flip != second else -2] for flip in self.flips]

    def send(self):
        if self.stage < 0:
            masks = combined(self.far[self.stage])[1:]
            self.received = [swap(self.states[0], mask, self.sizes) for mask in masks]
        elif self.stage < 2:
            masks = self.near_masks(self.stage == 1)
            self.received = [
                swap(state, mask, self.sizes) for state, mask in zip(self.states, masks)
            ]
        else:
            mask = self.masks[self.core]
            self.received = [swap(state, mask, self.sizes) for state in self.states]

    def take(self):
        received, self.received = list(self.received), None
        if self.stage < 0:
            state = self.states[0]
            groups, rows, cols = state.shape[0], state.shape[-2], state.shape[-1]
            group = self.far[self.stage]
            pieces = [value.reshape(-1, rows, cols) for value in [state] + received]
            wide = placed_far(pieces, small_index(group, self.sizes))
            self.states = [wide.reshape(groups, -1, rows, cols)]
            if self.stage == -1:
                self.states = [self.states[0][place] for place in range(groups)]
        elif self.stage < 2:
            states = []
            masks = self.near_masks(self.stage == 1)
            for state, value, mask, flip in zip(self.states, received, masks, self.flips):
                blocks, rows, cols = state.shape
                joined = 2 if flip and self.stage == 1 else 1
                shape = (blocks // joined, joined * rows, cols)
                bit = small_index([mask], self.sizes)
                (out,) = merged(state.reshape(shape), value.reshape(shape), bit, [cols])
                states.append(out.reshape(2 * blocks, rows, cols))
            self.states = states
        else:
            self.whole = []
            for state, value, splits in zip(self.states, received, self.splits):
                blocks, rows, cols = state.shape
                high = 2**self.core
                shape = (high, blocks // high * rows, cols)
                bit = small_index([self.masks[self.core]], self.sizes)
                outs = merged(state.reshape(shape), value.reshape(shape), bit, splits)
                self.whole.append([out.reshape(-1, out.shape[-1]) for out in outs])
        self.stage += 1


def ended(chains, *others):
    flat = [value for chain in chains for value in chain.received]
    held = list(pinned(*flat, *others))
    for chain in chains:
        count = len(chain.received)
        chain.received, held = held[:count], held[count:]
        chain.take()
    return held


def started(chains):
    for chain in chains:
        chain.send()


def half_kernel(side_ref, acts_ref, grad_ref, out_ref):
    out_ref[...] = over_rows(acts_ref[...], grad_ref[...]).astype(jnp.bfloat16)


def half_add_kernel(side_ref, acts_ref, grad_ref, add_ref, out_ref):
    total = over_rows(acts_ref[...], grad_ref[...]) + add_ref[...].astype(jnp.float32)
    out_ref[...] = total.astype(jnp.bfloat16)


def half_product(acts, grad, sizes, received):
    masks, core = bit_masks(sizes)
    rows, inner = acts.shape
    cols = grad.shape[1]
    segment = inner // (2 * 2**core)
    tile = math.gcd(segment, 512)
    parts = segment // tile
    wide = math.gcd(cols, 1024)
    side = small_index([masks[core]], sizes)
    if received is None:
        side = 1 - side

    def acts_at(i, j, side_ref):
        return (0, (i // parts) * 2 * parts + side_ref[0] * parts + i % parts)

    specs = [
        pl.BlockSpec((rows, tile), acts_at),
        pl.BlockSpec((rows, wide), lambda i, j, side_ref: (0, j)),
    ]
    out_spec = pl.BlockSpec((tile, wide), lambda i, j, side_ref: (i, j))
    operands = [acts, grad]
    if received is not None:
        specs.append(out_spec)
        operands.append(received)
    return pl.pallas_call(
        half_kernel if received is None else half_add_kernel,
        grid_spec=pltpu.PrefetchScalarGridSpec(
            num_scalar_prefetch=1,
            grid=(inner // (2 * tile), cols // wide),
            in_specs=specs,
            out_specs=out_spec,
        ),
        out_shape=jax.ShapeDtypeStruct((inner // 2, cols), jnp.bfloat16),
        cost_estimate=LIGHT,
        name="half_away" if received is None else "half_kept",
    )(side.reshape(1), *operands)


class Core:
    def __init__(self, acts, grad, sizes):
        masks, core = bit_masks(sizes)
        self.mask, self.sizes = masks[core], sizes
        self.acts, self.grad = acts, grad
        self.away = [half_product(acts, grad, sizes, None)]
        self.received = None
        self.theirs = None

    def send(self):
        self.received = [swap(self.away[0], self.mask, self.sizes)]

    def take(self):
        self.theirs = self.received[0]
        self.received = None
        self.away = []


class Scatter:
    def __init__(self, states, sizes, flip):
        self.sizes = sizes
        masks, core = bit_masks(sizes)
        self.bits = [mask for place, mask in enumerate(masks) if place != core]
        first, second = masks[-1], masks[-2]
        if flip:
            first, second = second, first
        self.todo = [[first], [second]] + far_groups(sizes)[::-1]
        count = 2 ** len(self.bits)
        self.states = [
            state.reshape(count, state.shape[0] // count, state.shape[1]) for state in states
        ]
        self.received = None
        self.prepare()

    def prepare(self):
        group = self.todo[0]
        first = self.bits.index(group[0])
        self.bits = [bit for bit in self.bits if bit not in group]
        slots = 2 ** len(group)
        high = 2**first
        place = small_index(group, self.sizes)
        self.kept = []
        aways = []
        for state in self.states:
            blocks, rows, cols = state.shape
            view = state.reshape(high, slots, blocks // (high * slots), rows, cols)
            parts = [
                lax.dynamic_index_in_dim(view, place ^ index, 1, keepdims=False).reshape(
                    blocks // slots, rows, cols
                )
                for index in range(slots)
            ]
            self.kept.append(parts[0])
            aways.append(parts[1:])
        self.away = [
            jnp.stack([away[index] for away in aways]) for index in range(slots - 1)
        ]
        self.todo = self.todo[1:]
        self.masks = combined(group)[1:]

    def send(self):
        self.received = [swap(away, mask, self.sizes) for away, mask in zip(self.away, self.masks)]

    def take(self):
        last = not self.todo
        self.states = []
        for index, kept in enumerate(self.kept):
            total = kept.astype(jnp.float32)
            for value in self.received:
                total = total + value[index].astype(jnp.float32)
            self.states.append(total.astype(jnp.float32 if last else jnp.bfloat16))
        self.received = None
        self.away = []
        if not last:
            self.prepare()


def split_kernel(flips, side_ref, acts_ref, *refs):
    count = len(flips)
    acts = acts_ref[...]
    for place, flip in enumerate(flips):
        grad_ref, add_ref = refs[2 * place], refs[2 * place + 1]
        kept_ref, away_ref = refs[2 * (count + place)], refs[2 * (count + place) + 1]
        total = over_rows(acts, grad_ref[...]) + add_ref[...].astype(jnp.float32)
        total = total.astype(jnp.bfloat16)
        half, rows, cols = kept_ref.shape
        parts = [[], []]
        for index in range(2 * half):
            bit = (index // 2) % 2 if flip else index % 2
            parts[bit].append(total[index * rows : (index + 1) * rows])

        def put(first, second, kept_ref=kept_ref, away_ref=away_ref, half=half):
            for index in range(half):
                kept_ref[index] = first[index]
                away_ref[index] = second[index]

        @pl.when(side_ref[1 + place] == 0)
        def _(put=put, parts=parts):
            put(parts[0], parts[1])

        @pl.when(side_ref[1 + place] != 0)
        def _(put=put, parts=parts):
            put(parts[1], parts[0])


def split_product(acts, grad, theirs, sizes, flips):
    masks, core = bit_masks(sizes)
    devices = sizes[0] * sizes[1]
    rows, inner = acts.shape
    count = len(flips)
    cols = grad.shape[1] // count
    block = inner // devices
    segment = inner // (2 * 2**core)
    tile = math.gcd(segment, 512)
    parts = segment // tile
    wide = math.gcd(cols, 1024 // count)
    steps = cols // wide
    firsts = [masks[-2] if flip else masks[-1] for flip in flips]
    sides = jnp.stack([small_index([mask], sizes) for mask in [masks[core]] + firsts])
    half = tile // (2 * block)
    out_spec = pl.BlockSpec((half, block, wide), lambda i, j, side_ref: (i, 0, j))
    out_shape = jax.ShapeDtypeStruct((devices // 4, block, cols), jnp.bfloat16)
    specs = [
        pl.BlockSpec(
            (rows, tile),
            lambda i, j, side_ref: (
                0,
                (i // parts) * 2 * parts + side_ref[0] * parts + i % parts,
            ),
        )
    ]
    for place in range(count):
        shift = place * steps
        specs.append(pl.BlockSpec((rows, wide), lambda i, j, side_ref, s=shift: (0, j + s)))
        specs.append(pl.BlockSpec((tile, wide), lambda i, j, side_ref, s=shift: (i, j + s)))
    return pl.pallas_call(
        functools.partial(split_kernel, flips),
        grid_spec=pltpu.PrefetchScalarGridSpec(
            num_scalar_prefetch=1,
            grid=(inner // (2 * tile), steps),
            in_specs=specs,
            out_specs=[out_spec] * (2 * count),
        ),
        out_shape=[out_shape] * (2 * count),
        cost_estimate=LIGHT,
        name="split_product",
    )(sides, acts, *([grad, theirs] * count))


def add_split_kernel(side_ref, *refs):
    count = len(refs) // 6
    for place in range(count):
        ins = refs[4 * place : 4 * place + 4]
        outs = refs[4 * count + 2 * place : 4 * count + 2 * place + 2]
        for out, one, two in zip(outs, ins[::2], ins[1::2]):
            out[...] = one[:, 0] + two[:, 0]


def add_split(kepts, values, bits):
    blocks = kepts[0].shape[0]
    part = math.gcd(blocks // 2, 2)
    specs, operands, out_specs, out_shapes = [], [], [], []
    for place, (kept, value) in enumerate(zip(kepts, values)):
        unused, rows, cols = kept.shape
        shape = (blocks // 2, 2, rows, cols)
        block = (part, 1, rows, cols)
        stays = pl.BlockSpec(block, lambda i, side_ref, p=place: (i, side_ref[p], 0, 0))
        goes = pl.BlockSpec(block, lambda i, side_ref, p=place: (i, 1 - side_ref[p], 0, 0))
        specs.extend([stays, stays, goes, goes])
        operands.extend([kept.reshape(shape), value.reshape(shape)] * 2)
        out_specs.extend([pl.BlockSpec((part, rows, cols), lambda i, side_ref: (i, 0, 0))] * 2)
        out_shapes.extend([jax.ShapeDtypeStruct((blocks // 2, rows, cols), kept.dtype)] * 2)
    outs = pl.pallas_call(
        add_split_kernel,
        grid_spec=pltpu.PrefetchScalarGridSpec(
            num_scalar_prefetch=1,
            grid=(blocks // (2 * part),),
            in_specs=specs,
            out_specs=out_specs,
        ),
        out_shape=out_shapes,
        cost_estimate=LIGHT,
        name="add_split",
    )(jnp.stack(bits), *operands)
    return list(outs[::2]), list(outs[1::2])


def add_join_kernel(count, place_ref, *refs):
    for slot, out in enumerate(refs[2 * count :]):

        @pl.when(pl.program_id(1) == slot)
        def _(out=out):
            start = 0
            for one, two in zip(refs[:count], refs[count : 2 * count]):
                total = one[0] + two[0]
                width = total.shape[-1]
                out[0, :, start : start + width] = total
                start += width


def add_join(kept, received, bit):
    blocks, rows, unused = kept[0].shape
    width = sum(value.shape[2] for value in kept)
    specs = [
        pl.BlockSpec(
            (1, rows, value.shape[2]), lambda i, j, side_ref: (2 * i + (side_ref[0] ^ j), 0, 0)
        )
        for value in kept
    ]
    return pl.pallas_call(
        functools.partial(add_join_kernel, len(kept)),
        grid_spec=pltpu.PrefetchScalarGridSpec(
            num_scalar_prefetch=1,
            grid=(blocks // 2, 2),
            in_specs=specs + specs,
            out_specs=[pl.BlockSpec((1, rows, width), lambda i, j, side_ref: (i, 0, 0))] * 2,
        ),
        out_shape=[jax.ShapeDtypeStruct((blocks // 2, rows, width), kept[0].dtype)] * 2,
        cost_estimate=LIGHT,
        name="add_join",
    )(bit.reshape(1), *kept, *received)


class Joint:
    def __init__(self, parts, sizes):
        self.sizes = sizes
        masks, core = bit_masks(sizes)
        self.near = masks[-2:]
        self.far = far_groups(sizes)[0]
        self.flips, self.kept, self.away = [], [], []
        for exchange, flips in parts:
            outs = split_product(exchange.acts, exchange.grad, exchange.theirs, sizes, flips)
            self.kept.extend(outs[::2])
            self.away.extend(outs[1::2])
            self.flips.extend(flips)
        self.masks = [self.near[0] if flip else self.near[1] for flip in self.flips]
        self.received = None
        self.stage = 0

    def send(self):
        self.received = [swap(away, mask, self.sizes) for away, mask in zip(self.away, self.masks)]

    def take(self):
        received, self.received = self.received, None
        self.stage += 1
        if self.stage == 1:
            self.masks = [self.near[1] if flip else self.near[0] for flip in self.flips]
            bits = [small_index([mask], self.sizes) for mask in self.masks]
            self.kept, self.away = add_split(self.kept, received, bits)
        elif self.stage == 2:
            self.masks = [self.far[1]]
            kept, away = add_join(self.kept, received, small_index(self.masks, self.sizes))
            self.kept, self.away = [kept], [away]
        elif self.stage == 3:
            self.masks = [self.far[0]]
            bits = [small_index(self.masks, self.sizes)]
            self.kept, self.away = add_split(self.kept, received, bits)
        else:
            self.total = self.kept[0][0].astype(jnp.float32) + received[0][0].astype(jnp.float32)
            self.away = []

    def result(self):
        return self.total


class Plain:
    def __init__(self, parts, sizes):
        self.chains = []
        for exchange, flips in parts:
            kept = half_product(exchange.acts, exchange.grad, sizes, exchange.theirs)
            self.chains.append(Scatter([kept], sizes, flips[0]))
        self.received = None

    @property
    def away(self):
        return [away for chain in self.chains for away in chain.away]

    @away.setter
    def away(self, values):
        values = list(values)
        for chain in self.chains:
            count = len(chain.away)
            chain.away, values = values[:count], values[count:]

    def send(self):
        for chain in self.chains:
            chain.send()
        self.received = [value for chain in self.chains for value in chain.received]

    def take(self):
        values, self.received = list(self.received), None
        for chain in self.chains:
            count = len(chain.received)
            chain.received, values = values[:count], values[count:]
            chain.take()

    def result(self):
        return jnp.concatenate([chain.states[0][0] for chain in self.chains], axis=1)


def summed(parts, sizes):
    heights = [exchange.acts.shape[1] // (sizes[0] * sizes[1]) for exchange, unused in parts]
    groups = far_groups(sizes)
    fits = all(height % 16 == 0 for height in heights)
    if len(groups) == 1 and len(groups[0]) == 2 and fits:
        return Joint(parts, sizes)
    return Plain(parts, sizes)


class VectorScatter:
    def __init__(self, terms, sizes):
        self.sizes = sizes
        masks, core = bit_masks(sizes)
        self.bits = masks
        self.todo = [masks[core]] + [mask for mask in masks[::-1] if mask != masks[core]]
        self.state = terms
        self.received = None
        self.prepare()

    def prepare(self):
        bit = self.todo[0]
        high = 2 ** self.bits.index(bit)
        self.bits = [other for other in self.bits if other != bit]
        view = self.state.reshape(high, 2, -1, self.state.shape[-1])
        place = small_index([bit], self.sizes)
        away = lax.dynamic_index_in_dim(view, 1 - place, 1, keepdims=False)
        kept = lax.dynamic_index_in_dim(view, place, 1, keepdims=False)
        self.away = [away.reshape(-1, away.shape[-1])]
        self.kept = kept.reshape(-1, kept.shape[-1])
        self.mask = bit
        self.todo = self.todo[1:]

    def send(self):
        self.received = [swap(self.away[0], self.mask, self.sizes)]

    def take(self):
        self.state = self.kept + self.received[0]
        self.received = None
        self.away = []
        if self.todo:
            self.prepare()


def scatter_round(ending, starting, *others):
    ending = [chain for chain in ending if chain.received is not None]
    others = ended(ending, *others)
    going = [chain for chain in starting if chain.away and chain.received is None]
    flat = [value for chain in going for value in chain.away]
    held = list(pinned(*flat, *others))
    for chain in going:
        count = len(chain.away)
        chain.away, held = held[:count], held[count:]
        chain.send()
    return held


def gelu_and_slope(preact):
    square = preact * preact
    bent = jnp.tanh(preact * (0.7978845608028654 + (0.7978845608028654 * 0.044715) * square))
    half = 0.5 + 0.5 * bent
    value = preact * half
    inner = 0.7978845608028654 + (3 * 0.7978845608028654 * 0.044715) * square
    slope = half + value * (1.0 - bent) * inner
    return value.astype(jnp.bfloat16), slope.astype(jnp.bfloat16)


def times(left, right):
    return jnp.dot(left, right, preferred_element_type=jnp.float32)


def grad_pre_kernel(grad_ref, weight_ref, slope_ref, out_ref, bias_ref):
    weight = weight_ref[...]
    total = None
    for start in range(0, grad_ref.shape[0], 256):
        grad_act = against(grad_ref[start : start + 256], weight)
        slope = slope_ref[start : start + 256].astype(jnp.float32)
        grad_pre = (grad_act * slope).astype(jnp.bfloat16)
        out_ref[start : start + 256] = grad_pre
        term = jnp.sum(grad_pre.astype(jnp.float32), axis=0, keepdims=True)
        total = term if total is None else total + term
    bias_ref[...] = total


def grad_two_kernel(grad_ref, weight_ref, out_ref):
    term = against(grad_ref[...], weight_ref[...])

    @pl.when(pl.program_id(0) == 0)
    def _():
        out_ref[...] = term

    @pl.when(pl.program_id(0) != 0)
    def _():
        out_ref[...] += term


def grad_two_of(grad_pre, w_up):
    rows, hidden = grad_pre.shape
    width = w_up.shape[0]
    tile = 1024
    return pl.pallas_call(
        grad_two_kernel,
        grid=(hidden // tile,),
        in_specs=[
            pl.BlockSpec((rows, tile), lambda i: (0, i)),
            pl.BlockSpec((width, tile), lambda i: (0, i)),
        ],
        out_specs=pl.BlockSpec((rows, width), lambda i: (0, 0)),
        out_shape=jax.ShapeDtypeStruct((rows, width), jnp.float32),
        cost_estimate=LIGHT,
        name="grad_two",
    )(grad_pre, w_up)


def grad_pre_of(grad_low, w_down, slope):
    rows, width = grad_low.shape
    hidden = w_down.shape[0]
    tile = 1024
    grad_pre, bias = pl.pallas_call(
        grad_pre_kernel,
        grid=(hidden // tile,),
        in_specs=[
            pl.BlockSpec((rows, width), lambda i: (0, 0)),
            pl.BlockSpec((tile, width), lambda i: (i, 0)),
            pl.BlockSpec((rows, tile), lambda i: (0, i)),
        ],
        out_specs=[
            pl.BlockSpec((rows, tile), lambda i: (0, i)),
            pl.BlockSpec((1, tile), lambda i: (0, i)),
        ],
        out_shape=[
            jax.ShapeDtypeStruct((rows, hidden), jnp.bfloat16),
            jax.ShapeDtypeStruct((1, hidden), jnp.float32),
        ],
        cost_estimate=LIGHT,
        name="grad_pre",
    )(grad_low, w_down, slope)
    return grad_pre, bias.reshape(hidden)


def local(
    sizes,
    frame_input,
    code_embed,
    segment_ids,
    frame_cotangent,
    code_cotangent,
    frame_prenorm,
    frame_query,
    frame_keys,
    frame_values,
    frame_outproj,
    frame_midnorm,
    frame_upproj,
    frame_upbias,
    frame_downproj,
    frame_downbias,
    code_prenorm,
    code_query,
    code_keys,
    code_values,
    code_outproj,
    code_midnorm,
    code_upproj,
    code_upbias,
    code_downproj,
    code_downbias,
):
    low = jnp.bfloat16
    frames = frame_input.shape[0]
    devices = sizes[0] * sizes[1]
    vectors = (
        frame_prenorm,
        frame_midnorm,
        frame_upbias,
        frame_downbias,
        code_prenorm,
        code_midnorm,
        code_upbias,
        code_downbias,
    )
    widths = [vec.shape[0] for vec in vectors]

    shard_rows = frame_values.shape[0]
    packed = jnp.concatenate([vec[None] for vec in vectors], axis=1)
    packed = jnp.pad(packed, ((0, 0), (0, shard_rows * 128 - packed.shape[1])))
    packed = packed.reshape(shard_rows, 128)
    f_ab = Gather(
        jnp.stack(
            [
                jnp.concatenate([frame_query, frame_keys, packed], axis=1),
                jnp.concatenate([frame_values, frame_outproj, packed], axis=1),
            ]
        ),
        sizes,
        (False, True),
        ([2 * D, 128], [D, D, 128]),
    )
    c_ab = Gather(
        jnp.stack(
            [
                jnp.concatenate([code_query, code_keys], axis=1),
                jnp.concatenate([code_values, code_outproj], axis=1),
            ]
        ),
        sizes,
        (False, True),
        ([2 * D], [D, D]),
    )

    def gathered(shard):
        return lax.all_gather(shard, ("gx", "gy"), axis=0, tiled=True)

    f_up, f_down = gathered(frame_upproj), gathered(frame_downproj)
    c_up = gathered(code_upproj)
    c_d = Gather(code_downproj[None], sizes, (True,), ([D],))
    for unused in range(len(f_ab.far) - 1):
        started([f_ab])
        ended([f_ab])
        started([c_ab])
        ended([c_ab])
        started([c_d])
        ended([c_d])
    started([f_ab])
    ended([f_ab])
    started([f_ab])
    code_rows = jnp.swapaxes(code_embed, 0, 1)
    grad_code_y = jnp.swapaxes(code_cotangent, 0, 1)
    code_rows, grad_code_y = ended([f_ab], code_rows, grad_code_y)
    started([f_ab, c_ab])
    ended([f_ab, c_ab])
    started([f_ab, c_ab])
    ended([f_ab, c_ab])
    f_pair = f_ab.whole[0][0]
    f_value, f_out, tail = f_ab.whole[1]
    whole = tail.reshape(devices, -1)[:, : sum(widths)].astype(jnp.float32)
    gains = []
    start = 0
    for width in widths:
        gains.append(whole[:, start : start + width].reshape(devices * width))
        start += width
    frame_gains = tuple(gains[:4])
    code_gains = tuple(gains[4:])
    frame_x = frame_input.astype(jnp.float32)
    f_normed = rms_scale(frame_x, frame_gains[0]).astype(low)
    started([c_ab, c_d])
    segments = segment_ids[0]
    f_qk = times(f_normed, f_pair).astype(low)
    f_v = times(f_normed, f_value).astype(low)
    f_mixed = frame_attend(f_qk, f_v, segments)
    f_qk, f_v, f_mixed = ended([c_ab, c_d], f_qk, f_v, f_mixed)
    started([c_ab, c_d])
    f_hidden = frame_x + times(f_mixed, f_out)
    f_normed_two = rms_scale(f_hidden, frame_gains[1]).astype(low)
    f_hidden, f_normed_two = ended([c_ab, c_d], f_hidden, f_normed_two)
    started([c_d])
    f_act, f_slope = gelu_and_slope(times(f_normed_two, f_up) + frame_gains[2])
    rows = CB * frames
    grad_code_y = grad_code_y.reshape(rows, D)
    frame_y = f_hidden + (times(f_act, f_down) + frame_gains[3])

    def tokens_of(value):
        return value.reshape(CB, frames, value.shape[-1])

    code_x = (code_rows.astype(jnp.float32) + frame_y[None]).reshape(rows, D)
    c_normed = rms_scale(code_x, code_gains[0]).astype(low)
    c_pair = c_ab.whole[0][0]
    c_value, c_out = c_ab.whole[1]
    c_qk = times(c_normed, c_pair).astype(low)
    c_v = times(c_normed, c_value).astype(low)
    c_mixed = code_attend(tokens_of(c_qk), tokens_of(c_v)).reshape(rows, D)
    c_hidden = code_x + times(c_mixed, c_out)
    (c_hidden,) = ended([c_d], c_hidden)
    started([c_d])
    c_normed_two = rms_scale(c_hidden, code_gains[1]).astype(low)
    c_act, c_slope = gelu_and_slope(times(c_normed_two, c_up) + code_gains[2])
    c_act, c_slope = ended([c_d], c_act, c_slope)
    ((c_down,),) = c_d.whole

    def both(exchange):
        return [summed([(exchange, (True, False))], sizes)]

    def attention_sums(pair, value, outproj):
        parts = [(pair, (False,)), (value, (True,)), (outproj, (True,))]
        return [summed(parts, sizes)]

    def norm_back(grad_out, inputs, gain):
        unused, back = jax.vjp(rms_scale, inputs, gain)
        return back(grad_out)

    grad_low = grad_code_y
    c_d_core = Core(c_act, grad_low, sizes)
    c_slope, grad_low = scatter_round([], [c_d_core], c_slope, grad_low)
    c_grad_b_down = jnp.sum(grad_low.astype(jnp.float32), axis=0)
    (c_grad_b_down,) = ended([c_d_core], c_grad_b_down)
    c_d_chain = both(c_d_core)
    c_slope, grad_low = scatter_round([], c_d_chain, c_slope, grad_low)
    grad_pre, c_grad_b_up = grad_pre_of(grad_low, c_down, c_slope)
    c_u_core = Core(c_normed_two, grad_pre, sizes)
    (grad_pre,) = scatter_round(c_d_chain, c_d_chain + [c_u_core], grad_pre)
    grad_two = grad_two_of(grad_pre, c_up)
    (grad_two,) = scatter_round(c_d_chain + [c_u_core], c_d_chain, grad_two)
    c_u_chain = both(c_u_core)
    grad_part, c_grad_mid = norm_back(grad_two, c_hidden, code_gains[1])
    grad_hidden = grad_low.astype(jnp.float32) + grad_part
    grad_attn = grad_hidden.astype(low)
    grad_attn, grad_hidden = scatter_round(
        c_d_chain, c_d_chain + c_u_chain, grad_attn, grad_hidden
    )
    c_o_core = Core(c_mixed, grad_attn, sizes)
    grad_mixed = against(grad_attn, c_out).astype(low)
    grad_pair, grad_values = code_attend_back(
        tokens_of(c_qk), tokens_of(c_v), tokens_of(grad_mixed)
    )
    grad_pair = grad_pair.reshape(rows, 2 * D)
    grad_values = grad_values.reshape(rows, D)
    grad_pair, grad_values = scatter_round(
        c_d_chain + c_u_chain, c_u_chain + [c_o_core], grad_pair, grad_values
    )
    c_p_core = Core(c_normed, grad_pair, sizes)
    c_v_core = Core(c_normed, grad_values, sizes)
    grad_pair, grad_values = scatter_round(
        c_u_chain + [c_o_core], c_u_chain + [c_p_core, c_v_core], grad_pair, grad_values
    )
    grad_normed = against(grad_pair, c_pair) + against(grad_values, c_value)
    grad_part, c_grad_pre = norm_back(grad_normed, code_x, code_gains[0])
    grad_code_x = grad_hidden + grad_part
    grad_frame_y = frame_cotangent.astype(jnp.float32) + jnp.sum(tokens_of(grad_code_x), axis=0)
    grad_code_x, grad_frame_y = scatter_round(
        c_u_chain + [c_p_core, c_v_core], c_u_chain, grad_code_x, grad_frame_y
    )
    c_sums = attention_sums(c_p_core, c_v_core, c_o_core)
    (grad_frame_y,) = scatter_round(c_u_chain, c_sums, grad_frame_y)

    grad_low = grad_frame_y.astype(low)
    f_d_core = Core(f_act, grad_low, sizes)
    grad_pre, f_grad_b_up = grad_pre_of(grad_low, f_down, f_slope)
    f_u_core = Core(f_normed_two, grad_pre, sizes)
    (grad_pre,) = scatter_round(c_sums, c_sums + [f_d_core, f_u_core], grad_pre)
    grad_two = grad_two_of(grad_pre, f_up)
    grad_part, f_grad_mid = norm_back(grad_two, f_hidden, frame_gains[1])
    grad_hidden = grad_frame_y + grad_part
    grad_attn = grad_hidden.astype(low)
    grad_attn, grad_hidden = scatter_round(
        c_sums + [f_d_core, f_u_core], c_sums, grad_attn, grad_hidden
    )
    f_d_chain = both(f_d_core)
    grad_attn, grad_hidden = scatter_round(
        c_sums, c_sums + f_d_chain, grad_attn, grad_hidden
    )
    f_u_chain = both(f_u_core)
    f_o_core = Core(f_mixed, grad_attn, sizes)
    grad_mixed = against(grad_attn, f_out).astype(low)
    grad_pair, grad_values = frame_attend_back(f_qk, f_v, grad_mixed, segments)
    grad_pair, grad_values, c_act = scatter_round(
        c_sums + f_d_chain, f_d_chain + f_u_chain + [f_o_core], grad_pair, grad_values, c_act
    )
    f_p_core = Core(f_normed, grad_pair, sizes)
    f_v_core = Core(f_normed, grad_values, sizes)
    code_y = c_hidden + (times(c_act, c_down) + code_gains[3])
    code_y, grad_pair, grad_values = scatter_round(
        f_d_chain + f_u_chain + [f_o_core],
        f_d_chain + f_u_chain + [f_p_core, f_v_core],
        code_y,
        grad_pair,
        grad_values,
    )
    grad_normed = against(grad_pair, f_pair) + against(grad_values, f_value)
    grad_part, f_grad_pre = norm_back(grad_normed, frame_x, frame_gains[0])
    grad_frame_x = grad_hidden + grad_part
    f_grad_b_down = jnp.sum(grad_low.astype(jnp.float32), axis=0)
    terms = jnp.concatenate(
        [
            term.reshape(devices, -1)
            for term in (
                f_grad_pre,
                f_grad_mid,
                f_grad_b_up,
                f_grad_b_down,
                c_grad_pre,
                c_grad_mid,
                c_grad_b_up,
                c_grad_b_down,
            )
        ],
        axis=1,
    )
    row = VectorScatter(terms, sizes)
    (grad_frame_x,) = scatter_round(
        f_d_chain + f_u_chain + [f_p_core, f_v_core],
        f_d_chain + f_u_chain + [row],
        grad_frame_x,
    )
    f_sums = attention_sums(f_p_core, f_v_core, f_o_core)
    (code_y,) = scatter_round(
        f_d_chain + f_u_chain + [row], f_d_chain + f_u_chain + f_sums + [row], code_y
    )
    frame_output = frame_y.astype(low)
    code_output = jnp.swapaxes(tokens_of(code_y.astype(low)), 0, 1)
    (code_output,) = scatter_round(f_u_chain + f_sums + [row], f_sums + [row], code_output)
    code_embed_grad = jnp.swapaxes(tokens_of(grad_code_x), 0, 1)
    (code_embed_grad,) = scatter_round(f_sums + [row], f_sums + [row], code_embed_grad)
    everything = c_d_chain + c_u_chain + c_sums + f_d_chain + f_u_chain + f_sums + [row]
    while True:
        started([chain for chain in everything if chain.away and chain.received is None])
        going = [chain for chain in everything if chain.received is not None]
        if not going:
            break
        ended(going)
    sums = row.state[0]
    pieces = []
    start = 0
    for width in widths:
        pieces.append(sums[start : start + width])
        start += width

    def arranged(attn_sums, up_sums, down_sums, vecs):
        total = attn_sums[0].result()
        prenorm, midnorm, upbias, downbias = vecs
        return (
            prenorm,
            total[:, :D],
            total[:, D : 2 * D],
            total[:, 2 * D : 3 * D],
            total[:, 3 * D :],
            midnorm,
            up_sums,
            upbias,
            down_sums,
            downbias,
        )

    code_outs = arranged(c_sums, c_u_chain[0].result(), c_d_chain[0].result(), pieces[4:])
    frame_outs = arranged(
        f_sums, f_u_chain[0].result(), f_d_chain[0].result(), pieces[:4]
    )
    return (frame_output, code_output, grad_frame_x, code_embed_grad) + frame_outs + code_outs


def solution(mesh):
    in_specs = (
        P(("gx", "gy"), None),
        P(("gx", "gy"), None, None),
        P(("gx", "gy"), None),
        P(("gx", "gy"), None),
        P(("gx", "gy"), None, None),
        P(("gx", "gy")),
        P(("gx", "gy"), None),
        P(("gx", "gy"), None),
        P(("gx", "gy"), None),
        P(("gx", "gy"), None),
        P(("gx", "gy")),
        P(("gx", "gy"), None),
        P(("gx", "gy")),
        P(("gx", "gy"), None),
        P(("gx", "gy")),
        P(("gx", "gy")),
        P(("gx", "gy"), None),
        P(("gx", "gy"), None),
        P(("gx", "gy"), None),
        P(("gx", "gy"), None),
        P(("gx", "gy")),
        P(("gx", "gy"), None),
        P(("gx", "gy")),
        P(("gx", "gy"), None),
        P(("gx", "gy")),
    )
    out_specs = (
        P(("gx", "gy"), None),
        P(("gx", "gy"), None, None),
        P(("gx", "gy"), None),
        P(("gx", "gy"), None, None),
        P(("gx", "gy")),
        P(("gx", "gy"), None),
        P(("gx", "gy"), None),
        P(("gx", "gy"), None),
        P(("gx", "gy"), None),
        P(("gx", "gy")),
        P(("gx", "gy"), None),
        P(("gx", "gy")),
        P(("gx", "gy"), None),
        P(("gx", "gy")),
        P(("gx", "gy")),
        P(("gx", "gy"), None),
        P(("gx", "gy"), None),
        P(("gx", "gy"), None),
        P(("gx", "gy"), None),
        P(("gx", "gy")),
        P(("gx", "gy"), None),
        P(("gx", "gy")),
        P(("gx", "gy"), None),
        P(("gx", "gy")),
    )
    sizes = (mesh.shape["gx"], mesh.shape["gy"])
    return jax.shard_map(
        functools.partial(local, sizes), mesh=mesh, in_specs=in_specs, out_specs=out_specs, check_vma=False)
```

```python
import functools
import math

import jax
import jax.numpy as jnp
from jax import lax
from jax.experimental import pallas as pl
from jax.experimental.pallas import tpu as pltpu
from jax.sharding import PartitionSpec as P

D = 1024
HEADS = 16
HD = 64
CB = 3
LIGHT = pl.CostEstimate(flops=1, bytes_accessed=1, transcendentals=0)


def gelu_tanh(value):
    return (
        0.5
        * value
        * (1.0 + jnp.tanh(0.7978845608028654 * (value + 0.044715 * value * value * value)))
    )


def rms_scale(value, gain_vec):
    return value * lax.rsqrt(jnp.mean(value * value, axis=-1, keepdims=True) + 1e-05) * gain_vec


def over_rows(left, right):
    return lax.dot_general(
        left, right, (((0,), (0,)), ((), ())), preferred_element_type=jnp.float32
    )


def against(left, right):
    return lax.dot_general(
        left, right, (((1,), (1,)), ((), ())), preferred_element_type=jnp.float32
    )


def head_marks():
    lane = lax.broadcasted_iota(jnp.int32, (D, 128), 0) // HD
    head = lax.broadcasted_iota(jnp.int32, (D, 128), 1)
    return (lane == head).astype(jnp.bfloat16)


def head_sums(left, right, marks):
    product = left.astype(jnp.float32) * right.astype(jnp.float32)
    upper = product.astype(jnp.bfloat16)
    lower = (product - upper.astype(jnp.float32)).astype(jnp.bfloat16)
    return jnp.dot(upper, marks, preferred_element_type=jnp.float32) + jnp.dot(
        lower, marks, preferred_element_type=jnp.float32
    )


def spread(heads, marks):
    return lax.dot_general(
        heads, marks, (((1,), (1,)), ((), ())), preferred_element_type=jnp.float32
    )


def token_probs(tokens_q, tokens_k, marks):
    probs = []
    for token in range(CB):
        scores = [
            head_sums(tokens_q[token], tokens_k[other], marks) * HD ** (-0.5)
            for other in range(token + 1)
        ]
        highest = functools.reduce(jnp.maximum, scores)
        expo = [jnp.exp(score - highest) for score in scores]
        total = functools.reduce(jnp.add, expo)
        probs.append([term / total for term in expo])
    return probs


def code_attend_kernel(pair_ref, values_ref, marks_ref, out_ref):
    marks = marks_ref[...]
    query = [pair_ref[token, :, :D] for token in range(CB)]
    keys = [pair_ref[token, :, D:] for token in range(CB)]
    probs = token_probs(query, keys, marks)
    for token in range(CB):
        mixed = None
        for other in range(token + 1):
            value = values_ref[other].astype(jnp.float32)
            term = spread(probs[token][other].astype(jnp.bfloat16), marks) * value
            mixed = term if mixed is None else mixed + term
        out_ref[token] = mixed.astype(jnp.bfloat16)


def code_attend_back_kernel(
    pair_ref, values_ref, grad_ref, marks_ref, out_pair_ref, out_values_ref
):
    marks = marks_ref[...]
    query = [pair_ref[token, :, :D] for token in range(CB)]
    keys = [pair_ref[token, :, D:] for token in range(CB)]
    probs = token_probs(query, keys, marks)
    grad_scores = []
    for token in range(CB):
        grads = [
            head_sums(grad_ref[token], values_ref[other], marks)
            for other in range(token + 1)
        ]
        inner = functools.reduce(
            jnp.add, [prob * grad for prob, grad in zip(probs[token], grads)]
        )
        grad_scores.append(
            [
                (prob * (grad - inner)).astype(jnp.bfloat16)
                for prob, grad in zip(probs[token], grads)
            ]
        )
    scale = HD ** (-0.5)
    grad_keys = [None] * CB
    grad_values = [None] * CB
    for token in range(CB):
        grad_query = None
        for other in range(token + 1):
            wide = spread(grad_scores[token][other], marks)
            term = wide * keys[other].astype(jnp.float32)
            grad_query = term if grad_query is None else grad_query + term
            term = wide * query[token].astype(jnp.float32)
            grad_keys[other] = term if grad_keys[other] is None else grad_keys[other] + term
            wide = spread(probs[token][other].astype(jnp.bfloat16), marks)
            term = wide * grad_ref[token].astype(jnp.float32)
            grad_values[other] = term if grad_values[other] is None else grad_values[other] + term
        out_pair_ref[token, :, :D] = (grad_query * scale).astype(jnp.bfloat16)
    for token in range(CB):
        out_pair_ref[token, :, D:] = (grad_keys[token] * scale).astype(jnp.bfloat16)
        out_values_ref[token] = grad_values[token].astype(jnp.bfloat16)


def token_specs(step, widths):
    return [pl.BlockSpec((CB, step, width), lambda i: (0, i, 0)) for width in widths] + [
        pl.BlockSpec((D, 128), lambda i: (0, 0))
    ]


def code_attend(pair, values):
    frames = values.shape[1]
    step = math.gcd(frames, 64)
    return pl.pallas_call(
        code_attend_kernel,
        grid=(frames // step,),
        in_specs=token_specs(step, (2 * D, D)),
        out_specs=pl.BlockSpec((CB, step, D), lambda i: (0, i, 0)),
        out_shape=jax.ShapeDtypeStruct((CB, frames, D), jnp.bfloat16),
        cost_estimate=LIGHT,
        name="code_attend",
    )(pair, values, head_marks())


def code_attend_back(pair, values, grad_mixed):
    frames = values.shape[1]
    step = math.gcd(frames, 64)
    return pl.pallas_call(
        code_attend_back_kernel,
        grid=(frames // step,),
        in_specs=token_specs(step, (2 * D, D, D)),
        out_specs=[
            pl.BlockSpec((CB, step, 2 * D), lambda i: (0, i, 0)),
            pl.BlockSpec((CB, step, D), lambda i: (0, i, 0)),
        ],
        out_shape=[
            jax.ShapeDtypeStruct((CB, frames, 2 * D), jnp.bfloat16),
            jax.ShapeDtypeStruct((CB, frames, D), jnp.bfloat16),
        ],
        cost_estimate=LIGHT,
        name="code_attend_back",
    )(pair, values, grad_mixed, head_marks())


def frame_mask(column_ref, row_ref):
    frames = column_ref.shape[0]
    shape = (frames, frames)
    earlier = lax.broadcasted_iota(jnp.int32, shape, 0) >= lax.broadcasted_iota(
        jnp.int32, shape, 1
    )
    return earlier & (column_ref[...] == row_ref[...])


def frame_probs(query, keys, allowed):
    scores = against(query, keys) * HD ** (-0.5)
    scores = jnp.where(allowed, scores, -1e30)
    highest = jnp.max(scores, axis=-1, keepdims=True)
    expo = jnp.exp(scores - highest)
    return expo / jnp.sum(expo, axis=-1, keepdims=True)


def half_lanes(value, upper):
    lane = lax.broadcasted_iota(jnp.int32, value.shape, 1)
    chosen = (lane >= HD) if upper else (lane < HD)
    return jnp.where(chosen, value, jnp.zeros_like(value))


def frame_attend_kernel(query_ref, keys_ref, values_ref, column_ref, row_ref, out_ref):
    allowed = frame_mask(column_ref, row_ref)
    mixed = None
    for upper in (False, True):
        probs = frame_probs(half_lanes(query_ref[...], upper), keys_ref[...], allowed)
        term = jnp.dot(
            probs.astype(jnp.bfloat16),
            half_lanes(values_ref[...], upper),
            preferred_element_type=jnp.float32,
        )
        mixed = term if mixed is None else mixed + term
    out_ref[...] = mixed.astype(jnp.bfloat16)


def frame_attend_back_kernel(
    query_ref, keys_ref, values_ref, grad_ref, column_ref, row_ref, out_pair_ref, out_values_ref
):
    allowed = frame_mask(column_ref, row_ref)
    scale = HD ** (-0.5)
    grads = [None, None, None]
    for upper in (False, True):
        query = half_lanes(query_ref[...], upper)
        keys = half_lanes(keys_ref[...], upper)
        grad_out = half_lanes(grad_ref[...], upper)
        probs = frame_probs(query, keys, allowed)
        grad_probs = against(grad_out, values_ref[...])
        inner = jnp.sum(probs * grad_probs, axis=-1, keepdims=True)
        grad_scores = (probs * (grad_probs - inner)).astype(jnp.bfloat16)
        terms = (
            jnp.dot(grad_scores, keys, preferred_element_type=jnp.float32) * scale,
            over_rows(grad_scores, query) * scale,
            over_rows(probs.astype(jnp.bfloat16), grad_out),
        )
        grads = [term if grad is None else grad + term for grad, term in zip(grads, terms)]
    start = pl.multiple_of(pl.program_id(0) * 2 * HD, 2 * HD)
    out_pair_ref[:, pl.ds(start, 2 * HD)] = grads[0].astype(jnp.bfloat16)
    out_pair_ref[:, pl.ds(D + start, 2 * HD)] = grads[1].astype(jnp.bfloat16)
    out_values_ref[...] = grads[2].astype(jnp.bfloat16)


def pair_specs(frames, extra):
    pairs = HEADS // 2
    block = (frames, 2 * HD)
    return (
        [
            pl.BlockSpec(block, lambda j: (0, j)),
            pl.BlockSpec(block, lambda j: (0, j + pairs)),
        ]
        + [pl.BlockSpec(block, lambda j: (0, j))] * extra
        + [
            pl.BlockSpec((frames, 1), lambda j: (0, 0)),
            pl.BlockSpec((1, frames), lambda j: (0, 0)),
        ]
    )


def frame_attend(pair, values, segments):
    frames = values.shape[0]
    return pl.pallas_call(
        frame_attend_kernel,
        grid=(HEADS // 2,),
        in_specs=pair_specs(frames, 1),
        out_specs=pl.BlockSpec((frames, 2 * HD), lambda j: (0, j)),
        out_shape=jax.ShapeDtypeStruct((frames, D), jnp.bfloat16),
        cost_estimate=LIGHT,
        name="frame_attend",
    )(pair, pair, values, segments.reshape(frames, 1), segments.reshape(1, frames))


def frame_attend_back(pair, values, grad_mixed, segments):
    frames = values.shape[0]
    return pl.pallas_call(
        frame_attend_back_kernel,
        grid=(HEADS // 2,),
        in_specs=pair_specs(frames, 2),
        out_specs=[
            pl.BlockSpec((frames, 2 * D), lambda j: (0, 0)),
            pl.BlockSpec((frames, 2 * HD), lambda j: (0, j)),
        ],
        out_shape=[
            jax.ShapeDtypeStruct((frames, 2 * D), jnp.bfloat16),
            jax.ShapeDtypeStruct((frames, D), jnp.bfloat16),
        ],
        cost_estimate=LIGHT,
        name="frame_attend_back",
    )(
        pair,
        pair,
        values,
        grad_mixed,
        segments.reshape(frames, 1),
        segments.reshape(1, frames),
    )


def bit_masks(sizes):
    count = sizes[0] * sizes[1]
    masks = []
    step = count // 2
    while step >= 1:
        masks.append(step)
        step //= 2
    return masks, masks.index(sizes[1])


def swap(value, mask, sizes):
    count = sizes[0] * sizes[1]
    return lax.ppermute(value, ("gx", "gy"), [(place, place ^ mask) for place in range(count)])


def device_index(sizes):
    return lax.axis_index("gx") * sizes[1] + lax.axis_index("gy")


def far_groups(sizes):
    masks, core = bit_masks(sizes)
    far = [mask for place, mask in enumerate(masks[:-2]) if place != core]
    return [far[start : start + 2] for start in range(0, len(far), 2)]


def combined(group):
    found = []
    for index in range(2 ** len(group)):
        mask = 0
        for place, bit in enumerate(group):
            if (index >> (len(group) - 1 - place)) & 1:
                mask |= bit
        found.append(mask)
    return found


def small_index(group, sizes):
    me = device_index(sizes)
    index = jnp.zeros((), jnp.int32)
    for bit in group:
        index = index * 2 + ((me // bit) % 2).astype(jnp.int32)
    return index


def spans(done, pos):
    high = 2 ** sum(1 for other in done if other < pos)
    low = 2 ** sum(1 for other in done if other > pos)
    return high, low


def merge_kernel(bit_ref, mine_ref, theirs_ref, *outs):
    def put(first, second):
        start = 0
        for out in outs:
            width = out.shape[-1]
            out[0, 0] = first[0, :, start : start + width]
            out[0, 1] = second[0, :, start : start + width]
            start += width

    @pl.when(bit_ref[0] == 0)
    def _():
        put(mine_ref, theirs_ref)

    @pl.when(bit_ref[0] != 0)
    def _():
        put(theirs_ref, mine_ref)


def merged(mine, theirs, bit, splits):
    planes, rows, cols = mine.shape
    part = rows
    while part % 2 == 0 and part * cols > 512 * 1024:
        part //= 2
    read = pl.BlockSpec((1, part, cols), lambda i, j, bit_ref: (i, j, 0))
    return pl.pallas_call(
        merge_kernel,
        grid_spec=pltpu.PrefetchScalarGridSpec(
            num_scalar_prefetch=1,
            grid=(planes, rows // part),
            in_specs=[read, read],
            out_specs=[
                pl.BlockSpec((1, 2, part, width), lambda i, j, bit_ref: (i, 0, j, 0))
                for width in splits
            ],
        ),
        out_shape=[
            jax.ShapeDtypeStruct((planes, 2, rows, width), mine.dtype) for width in splits
        ],
        cost_estimate=LIGHT,
        name="merge",
    )(bit.reshape(1), mine, theirs)


def place_far_kernel(place_ref, *refs):
    for index, ref in enumerate(refs[:-1]):
        refs[-1][0, place_ref[0] ^ index] = ref[0]


def placed_far(pieces, place):
    planes, rows, cols = pieces[0].shape
    slots = len(pieces)
    return pl.pallas_call(
        place_far_kernel,
        grid_spec=pltpu.PrefetchScalarGridSpec(
            num_scalar_prefetch=1,
            grid=(planes,),
            in_specs=[pl.BlockSpec((1, rows, cols), lambda i, place_ref: (i, 0, 0))] * slots,
            out_specs=pl.BlockSpec((1, slots, rows, cols), lambda i, place_ref: (i, 0, 0, 0)),
        ),
        out_shape=jax.ShapeDtypeStruct((planes, slots, rows, cols), pieces[0].dtype),
        cost_estimate=LIGHT,
        name="place_far",
    )(place.reshape(1), *pieces)


def pinned(*values):
    return lax.optimization_barrier(values)


def gather_order(sizes, flip):
    masks, core = bit_masks(sizes)
    count = len(masks)
    far = [place for place in range(count - 2) if place != core]
    near = [count - 1, count - 2] if flip else [count - 2, count - 1]
    return far + near + [core]


class Gather:
    def __init__(self, shards, sizes, flips, splits):
        self.sizes = sizes
        self.flips, self.splits = flips, splits
        masks, core = bit_masks(sizes)
        self.masks, self.core = masks, core
        self.far = far_groups(sizes)
        self.states = [shards]
        self.received = None
        self.stage = -len(self.far)

    def near_masks(self, second):
        return [self.masks[-1 if flip != second else -2] for flip in self.flips]

    def send(self):
        if self.stage < 0:
            masks = combined(self.far[self.stage])[1:]
            self.received = [swap(self.states[0], mask, self.sizes) for mask in masks]
        elif self.stage < 2:
            masks = self.near_masks(self.stage == 1)
            self.received = [
                swap(state, mask, self.sizes) for state, mask in zip(self.states, masks)
            ]
        else:
            mask = self.masks[self.core]
            self.received = [swap(state, mask, self.sizes) for state in self.states]

    def take(self):
        received, self.received = list(self.received), None
        if self.stage < 0:
            state = self.states[0]
            groups, rows, cols = state.shape[0], state.shape[-2], state.shape[-1]
            group = self.far[self.stage]
            pieces = [value.reshape(-1, rows, cols) for value in [state] + received]
            wide = placed_far(pieces, small_index(group, self.sizes))
            self.states = [wide.reshape(groups, -1, rows, cols)]
            if self.stage == -1:
                self.states = [self.states[0][place] for place in range(groups)]
        elif self.stage < 2:
            states = []
            masks = self.near_masks(self.stage == 1)
            for state, value, mask, flip in zip(self.states, received, masks, self.flips):
                blocks, rows, cols = state.shape
                joined = 2 if flip and self.stage == 1 else 1
                shape = (blocks // joined, joined * rows, cols)
                bit = small_index([mask], self.sizes)
                (out,) = merged(state.reshape(shape), value.reshape(shape), bit, [cols])
                states.append(out.reshape(2 * blocks, rows, cols))
            self.states = states
        else:
            self.whole = []
            for state, value, splits in zip(self.states, received, self.splits):
                blocks, rows, cols = state.shape
                high = 2**self.core
                shape = (high, blocks // high * rows, cols)
                bit = small_index([self.masks[self.core]], self.sizes)
                outs = merged(state.reshape(shape), value.reshape(shape), bit, splits)
                self.whole.append([out.reshape(-1, out.shape[-1]) for out in outs])
        self.stage += 1


def ended(chains, *others):
    flat = [value for chain in chains for value in chain.received]
    held = list(pinned(*flat, *others))
    for chain in chains:
        count = len(chain.received)
        chain.received, held = held[:count], held[count:]
        chain.take()
    return held


def started(chains):
    for chain in chains:
        chain.send()


def half_kernel(side_ref, acts_ref, grad_ref, out_ref):
    out_ref[...] = over_rows(acts_ref[...], grad_ref[...]).astype(jnp.bfloat16)


def half_add_kernel(side_ref, acts_ref, grad_ref, add_ref, out_ref):
    total = over_rows(acts_ref[...], grad_ref[...]) + add_ref[...].astype(jnp.float32)
    out_ref[...] = total.astype(jnp.bfloat16)


def half_product(acts, grad, sizes, received):
    masks, core = bit_masks(sizes)
    rows, inner = acts.shape
    cols = grad.shape[1]
    segment = inner // (2 * 2**core)
    tile = math.gcd(segment, 512)
    parts = segment // tile
    wide = math.gcd(cols, 1024)
    side = small_index([masks[core]], sizes)
    if received is None:
        side = 1 - side

    def acts_at(i, j, side_ref):
        return (0, (i // parts) * 2 * parts + side_ref[0] * parts + i % parts)

    specs = [
        pl.BlockSpec((rows, tile), acts_at),
        pl.BlockSpec((rows, wide), lambda i, j, side_ref: (0, j)),
    ]
    out_spec = pl.BlockSpec((tile, wide), lambda i, j, side_ref: (i, j))
    operands = [acts, grad]
    if received is not None:
        specs.append(out_spec)
        operands.append(received)
    return pl.pallas_call(
        half_kernel if received is None else half_add_kernel,
        grid_spec=pltpu.PrefetchScalarGridSpec(
            num_scalar_prefetch=1,
            grid=(inner // (2 * tile), cols // wide),
            in_specs=specs,
            out_specs=out_spec,
        ),
        out_shape=jax.ShapeDtypeStruct((inner // 2, cols), jnp.bfloat16),
        cost_estimate=LIGHT,
        name="half_away" if received is None else "half_kept",
    )(side.reshape(1), *operands)


class Core:
    def __init__(self, acts, grad, sizes):
        masks, core = bit_masks(sizes)
        self.mask, self.sizes = masks[core], sizes
        self.acts, self.grad = acts, grad
        self.away = [half_product(acts, grad, sizes, None)]
        self.received = None
        self.theirs = None

    def send(self):
        self.received = [swap(self.away[0], self.mask, self.sizes)]

    def take(self):
        self.theirs = self.received[0]
        self.received = None
        self.away = []


class Scatter:
    def __init__(self, states, sizes, flip):
        self.sizes = sizes
        masks, core = bit_masks(sizes)
        self.bits = [mask for place, mask in enumerate(masks) if place != core]
        first, second = masks[-1], masks[-2]
        if flip:
            first, second = second, first
        self.todo = [[first], [second]] + far_groups(sizes)[::-1]
        count = 2 ** len(self.bits)
        self.states = [
            state.reshape(count, state.shape[0] // count, state.shape[1]) for state in states
        ]
        self.received = None
        self.prepare()

    def prepare(self):
        group = self.todo[0]
        first = self.bits.index(group[0])
        self.bits = [bit for bit in self.bits if bit not in group]
        slots = 2 ** len(group)
        high = 2**first
        place = small_index(group, self.sizes)
        self.kept = []
        aways = []
        for state in self.states:
            blocks, rows, cols = state.shape
            view = state.reshape(high, slots, blocks // (high * slots), rows, cols)
            parts = [
                lax.dynamic_index_in_dim(view, place ^ index, 1, keepdims=False).reshape(
                    blocks // slots, rows, cols
                )
                for index in range(slots)
            ]
            self.kept.append(parts[0])
            aways.append(parts[1:])
        self.away = [
            jnp.stack([away[index] for away in aways]) for index in range(slots - 1)
        ]
        self.todo = self.todo[1:]
        self.masks = combined(group)[1:]

    def send(self):
        self.received = [swap(away, mask, self.sizes) for away, mask in zip(self.away, self.masks)]

    def take(self):
        last = not self.todo
        self.states = []
        for index, kept in enumerate(self.kept):
            total = kept.astype(jnp.float32)
            for value in self.received:
                total = total + value[index].astype(jnp.float32)
            self.states.append(total.astype(jnp.float32 if last else jnp.bfloat16))
        self.received = None
        self.away = []
        if not last:
            self.prepare()


def split_kernel(flips, side_ref, acts_ref, *refs):
    count = len(flips)
    acts = acts_ref[...]
    for place, flip in enumerate(flips):
        grad_ref, add_ref = refs[2 * place], refs[2 * place + 1]
        kept_ref, away_ref = refs[2 * (count + place)], refs[2 * (count + place) + 1]
        total = over_rows(acts, grad_ref[...]) + add_ref[...].astype(jnp.float32)
        total = total.astype(jnp.bfloat16)
        half, rows, cols = kept_ref.shape
        parts = [[], []]
        for index in range(2 * half):
            bit = (index // 2) % 2 if flip else index % 2
            parts[bit].append(total[index * rows : (index + 1) * rows])

        def put(first, second, kept_ref=kept_ref, away_ref=away_ref, half=half):
            for index in range(half):
                kept_ref[index] = first[index]
                away_ref[index] = second[index]

        @pl.when(side_ref[1 + place] == 0)
        def _(put=put, parts=parts):
            put(parts[0], parts[1])

        @pl.when(side_ref[1 + place] != 0)
        def _(put=put, parts=parts):
            put(parts[1], parts[0])


def split_product(acts, grad, theirs, sizes, flips):
    masks, core = bit_masks(sizes)
    devices = sizes[0] * sizes[1]
    rows, inner = acts.shape
    count = len(flips)
    cols = grad.shape[1] // count
    block = inner // devices
    segment = inner // (2 * 2**core)
    tile = math.gcd(segment, 512)
    parts = segment // tile
    wide = math.gcd(cols, 1024 // count)
    steps = cols // wide
    firsts = [masks[-2] if flip else masks[-1] for flip in flips]
    sides = jnp.stack([small_index([mask], sizes) for mask in [masks[core]] + firsts])
    half = tile // (2 * block)
    out_spec = pl.BlockSpec((half, block, wide), lambda i, j, side_ref: (i, 0, j))
    out_shape = jax.ShapeDtypeStruct((devices // 4, block, cols), jnp.bfloat16)
    specs = [
        pl.BlockSpec(
            (rows, tile),
            lambda i, j, side_ref: (
                0,
                (i // parts) * 2 * parts + side_ref[0] * parts + i % parts,
            ),
        )
    ]
    for place in range(count):
        shift = place * steps
        specs.append(pl.BlockSpec((rows, wide), lambda i, j, side_ref, s=shift: (0, j + s)))
        specs.append(pl.BlockSpec((tile, wide), lambda i, j, side_ref, s=shift: (i, j + s)))
    return pl.pallas_call(
        functools.partial(split_kernel, flips),
        grid_spec=pltpu.PrefetchScalarGridSpec(
            num_scalar_prefetch=1,
            grid=(inner // (2 * tile), steps),
            in_specs=specs,
            out_specs=[out_spec] * (2 * count),
        ),
        out_shape=[out_shape] * (2 * count),
        cost_estimate=LIGHT,
        name="split_product",
    )(sides, acts, *([grad, theirs] * count))


def add_split_kernel(side_ref, *refs):
    count = len(refs) // 6
    for place in range(count):
        ins = refs[4 * place : 4 * place + 4]
        outs = refs[4 * count + 2 * place : 4 * count + 2 * place + 2]
        for out, one, two in zip(outs, ins[::2], ins[1::2]):
            out[...] = one[:, 0] + two[:, 0]


def add_split(kepts, values, bits):
    blocks = kepts[0].shape[0]
    part = math.gcd(blocks // 2, 2)
    specs, operands, out_specs, out_shapes = [], [], [], []
    for place, (kept, value) in enumerate(zip(kepts, values)):
        unused, rows, cols = kept.shape
        shape = (blocks // 2, 2, rows, cols)
        block = (part, 1, rows, cols)
        stays = pl.BlockSpec(block, lambda i, side_ref, p=place: (i, side_ref[p], 0, 0))
        goes = pl.BlockSpec(block, lambda i, side_ref, p=place: (i, 1 - side_ref[p], 0, 0))
        specs.extend([stays, stays, goes, goes])
        operands.extend([kept.reshape(shape), value.reshape(shape)] * 2)
        out_specs.extend([pl.BlockSpec((part, rows, cols), lambda i, side_ref: (i, 0, 0))] * 2)
        out_shapes.extend([jax.ShapeDtypeStruct((blocks // 2, rows, cols), kept.dtype)] * 2)
    outs = pl.pallas_call(
        add_split_kernel,
        grid_spec=pltpu.PrefetchScalarGridSpec(
            num_scalar_prefetch=1,
            grid=(blocks // (2 * part),),
            in_specs=specs,
            out_specs=out_specs,
        ),
        out_shape=out_shapes,
        cost_estimate=LIGHT,
        name="add_split",
    )(jnp.stack(bits), *operands)
    return list(outs[::2]), list(outs[1::2])


def add_join_kernel(count, place_ref, *refs):
    for slot, out in enumerate(refs[2 * count :]):

        @pl.when(pl.program_id(1) == slot)
        def _(out=out):
            start = 0
            for one, two in zip(refs[:count], refs[count : 2 * count]):
                total = one[0] + two[0]
                width = total.shape[-1]
                out[0, :, start : start + width] = total
                start += width


def add_join(kept, received, bit):
    blocks, rows, unused = kept[0].shape
    width = sum(value.shape[2] for value in kept)
    specs = [
        pl.BlockSpec(
            (1, rows, value.shape[2]), lambda i, j, side_ref: (2 * i + (side_ref[0] ^ j), 0, 0)
        )
        for value in kept
    ]
    return pl.pallas_call(
        functools.partial(add_join_kernel, len(kept)),
        grid_spec=pltpu.PrefetchScalarGridSpec(
            num_scalar_prefetch=1,
            grid=(blocks // 2, 2),
            in_specs=specs + specs,
            out_specs=[pl.BlockSpec((1, rows, width), lambda i, j, side_ref: (i, 0, 0))] * 2,
        ),
        out_shape=[jax.ShapeDtypeStruct((blocks // 2, rows, width), kept[0].dtype)] * 2,
        cost_estimate=LIGHT,
        name="add_join",
    )(bit.reshape(1), *kept, *received)


class Joint:
    def __init__(self, parts, sizes):
        self.sizes = sizes
        masks, core = bit_masks(sizes)
        self.near = masks[-2:]
        self.far = far_groups(sizes)[0]
        self.flips, self.kept, self.away = [], [], []
        for exchange, flips in parts:
            outs = split_product(exchange.acts, exchange.grad, exchange.theirs, sizes, flips)
            self.kept.extend(outs[::2])
            self.away.extend(outs[1::2])
            self.flips.extend(flips)
        self.masks = [self.near[0] if flip else self.near[1] for flip in self.flips]
        self.received = None
        self.stage = 0

    def send(self):
        self.received = [swap(away, mask, self.sizes) for away, mask in zip(self.away, self.masks)]

    def take(self):
        received, self.received = self.received, None
        self.stage += 1
        if self.stage == 1:
            self.masks = [self.near[1] if flip else self.near[0] for flip in self.flips]
            bits = [small_index([mask], self.sizes) for mask in self.masks]
            self.kept, self.away = add_split(self.kept, received, bits)
        elif self.stage == 2:
            self.masks = [self.far[1]]
            kept, away = add_join(self.kept, received, small_index(self.masks, self.sizes))
            self.kept, self.away = [kept], [away]
        elif self.stage == 3:
            self.masks = [self.far[0]]
            bits = [small_index(self.masks, self.sizes)]
            self.kept, self.away = add_split(self.kept, received, bits)
        else:
            self.total = self.kept[0][0].astype(jnp.float32) + received[0][0].astype(jnp.float32)
            self.away = []

    def result(self):
        return self.total


class Plain:
    def __init__(self, parts, sizes):
        self.chains = []
        for exchange, flips in parts:
            kept = half_product(exchange.acts, exchange.grad, sizes, exchange.theirs)
            self.chains.append(Scatter([kept], sizes, flips[0]))
        self.received = None

    @property
    def away(self):
        return [away for chain in self.chains for away in chain.away]

    @away.setter
    def away(self, values):
        values = list(values)
        for chain in self.chains:
            count = len(chain.away)
            chain.away, values = values[:count], values[count:]

    def send(self):
        for chain in self.chains:
            chain.send()
        self.received = [value for chain in self.chains for value in chain.received]

    def take(self):
        values, self.received = list(self.received), None
        for chain in self.chains:
            count = len(chain.received)
            chain.received, values = values[:count], values[count:]
            chain.take()

    def result(self):
        return jnp.concatenate([chain.states[0][0] for chain in self.chains], axis=1)


def summed(parts, sizes):
    heights = [exchange.acts.shape[1] // (sizes[0] * sizes[1]) for exchange, unused in parts]
    groups = far_groups(sizes)
    fits = all(height % 16 == 0 for height in heights)
    if len(groups) == 1 and len(groups[0]) == 2 and fits:
        return Joint(parts, sizes)
    return Plain(parts, sizes)


class VectorScatter:
    def __init__(self, terms, sizes):
        self.sizes = sizes
        masks, core = bit_masks(sizes)
        self.bits = masks
        self.todo = [masks[core]] + [mask for mask in masks[::-1] if mask != masks[core]]
        self.state = terms
        self.received = None
        self.prepare()

    def prepare(self):
        bit = self.todo[0]
        high = 2 ** self.bits.index(bit)
        self.bits = [other for other in self.bits if other != bit]
        view = self.state.reshape(high, 2, -1, self.state.shape[-1])
        place = small_index([bit], self.sizes)
        away = lax.dynamic_index_in_dim(view, 1 - place, 1, keepdims=False)
        kept = lax.dynamic_index_in_dim(view, place, 1, keepdims=False)
        self.away = [away.reshape(-1, away.shape[-1])]
        self.kept = kept.reshape(-1, kept.shape[-1])
        self.mask = bit
        self.todo = self.todo[1:]

    def send(self):
        self.received = [swap(self.away[0], self.mask, self.sizes)]

    def take(self):
        self.state = self.kept + self.received[0]
        self.received = None
        self.away = []
        if self.todo:
            self.prepare()


def scatter_round(ending, starting, *others):
    ending = [chain for chain in ending if chain.received is not None]
    others = ended(ending, *others)
    going = [chain for chain in starting if chain.away and chain.received is None]
    flat = [value for chain in going for value in chain.away]
    held = list(pinned(*flat, *others))
    for chain in going:
        count = len(chain.away)
        chain.away, held = held[:count], held[count:]
        chain.send()
    return held


def gelu_and_slope(preact):
    square = preact * preact
    bent = jnp.tanh(preact * (0.7978845608028654 + (0.7978845608028654 * 0.044715) * square))
    half = 0.5 + 0.5 * bent
    value = preact * half
    inner = 0.7978845608028654 + (3 * 0.7978845608028654 * 0.044715) * square
    slope = half + value * (1.0 - bent) * inner
    return value.astype(jnp.bfloat16), slope.astype(jnp.bfloat16)


def times(left, right):
    return jnp.dot(left, right, preferred_element_type=jnp.float32)


def grad_pre_kernel(grad_ref, weight_ref, slope_ref, out_ref, bias_ref):
    weight = weight_ref[...]
    total = None
    for start in range(0, grad_ref.shape[0], 256):
        grad_act = against(grad_ref[start : start + 256], weight)
        slope = slope_ref[start : start + 256].astype(jnp.float32)
        grad_pre = (grad_act * slope).astype(jnp.bfloat16)
        out_ref[start : start + 256] = grad_pre
        term = jnp.sum(grad_pre.astype(jnp.float32), axis=0, keepdims=True)
        total = term if total is None else total + term
    bias_ref[...] = total


def grad_two_kernel(grad_ref, weight_ref, out_ref):
    term = against(grad_ref[...], weight_ref[...])

    @pl.when(pl.program_id(0) == 0)
    def _():
        out_ref[...] = term

    @pl.when(pl.program_id(0) != 0)
    def _():
        out_ref[...] += term


def grad_two_of(grad_pre, w_up):
    rows, hidden = grad_pre.shape
    width = w_up.shape[0]
    tile = 1024
    return pl.pallas_call(
        grad_two_kernel,
        grid=(hidden // tile,),
        in_specs=[
            pl.BlockSpec((rows, tile), lambda i: (0, i)),
            pl.BlockSpec((width, tile), lambda i: (0, i)),
        ],
        out_specs=pl.BlockSpec((rows, width), lambda i: (0, 0)),
        out_shape=jax.ShapeDtypeStruct((rows, width), jnp.float32),
        cost_estimate=LIGHT,
        name="grad_two",
    )(grad_pre, w_up)


def grad_pre_of(grad_low, w_down, slope):
    rows, width = grad_low.shape
    hidden = w_down.shape[0]
    tile = 1024
    grad_pre, bias = pl.pallas_call(
        grad_pre_kernel,
        grid=(hidden // tile,),
        in_specs=[
            pl.BlockSpec((rows, width), lambda i: (0, 0)),
            pl.BlockSpec((tile, width), lambda i: (i, 0)),
            pl.BlockSpec((rows, tile), lambda i: (0, i)),
        ],
        out_specs=[
            pl.BlockSpec((rows, tile), lambda i: (0, i)),
            pl.BlockSpec((1, tile), lambda i: (0, i)),
        ],
        out_shape=[
            jax.ShapeDtypeStruct((rows, hidden), jnp.bfloat16),
            jax.ShapeDtypeStruct((1, hidden), jnp.float32),
        ],
        cost_estimate=LIGHT,
        name="grad_pre",
    )(grad_low, w_down, slope)
    return grad_pre, bias.reshape(hidden)


def local(
    sizes,
    frame_input,
    code_embed,
    segment_ids,
    frame_cotangent,
    code_cotangent,
    frame_prenorm,
    frame_query,
    frame_keys,
    frame_values,
    frame_outproj,
    frame_midnorm,
    frame_upproj,
    frame_upbias,
    frame_downproj,
    frame_downbias,
    code_prenorm,
    code_query,
    code_keys,
    code_values,
    code_outproj,
    code_midnorm,
    code_upproj,
    code_upbias,
    code_downproj,
    code_downbias,
):
    low = jnp.bfloat16
    frames = frame_input.shape[0]
    devices = sizes[0] * sizes[1]
    vectors = (
        frame_prenorm,
        frame_midnorm,
        frame_upbias,
        frame_downbias,
        code_prenorm,
        code_midnorm,
        code_upbias,
        code_downbias,
    )
    widths = [vec.shape[0] for vec in vectors]

    shard_rows = frame_values.shape[0]
    packed = jnp.concatenate([vec[None] for vec in vectors], axis=1)
    packed = jnp.pad(packed, ((0, 0), (0, shard_rows * 128 - packed.shape[1])))
    packed = packed.reshape(shard_rows, 128)
    f_ab = Gather(
        jnp.stack(
            [
                jnp.concatenate([frame_query, frame_keys, packed], axis=1),
                jnp.concatenate([frame_values, frame_outproj, packed], axis=1),
            ]
        ),
        sizes,
        (False, True),
        ([2 * D, 128], [D, D, 128]),
    )
    c_ab = Gather(
        jnp.stack(
            [
                jnp.concatenate([code_query, code_keys], axis=1),
                jnp.concatenate([code_values, code_outproj], axis=1),
            ]
        ),
        sizes,
        (False, True),
        ([2 * D], [D, D]),
    )

    def gathered(shard):
        return lax.all_gather(shard, ("gx", "gy"), axis=0, tiled=True)

    f_up, f_down = gathered(frame_upproj), gathered(frame_downproj)
    c_up = gathered(code_upproj)
    c_d = Gather(code_downproj[None], sizes, (True,), ([D],))
    for unused in range(len(f_ab.far) - 1):
        started([f_ab])
        ended([f_ab])
        started([c_ab])
        ended([c_ab])
        started([c_d])
        ended([c_d])
    started([f_ab])
    ended([f_ab])
    started([f_ab])
    code_rows = jnp.swapaxes(code_embed, 0, 1)
    grad_code_y = jnp.swapaxes(code_cotangent, 0, 1)
    code_rows, grad_code_y = ended([f_ab], code_rows, grad_code_y)
    started([f_ab, c_ab])
    ended([f_ab, c_ab])
    started([f_ab, c_ab])
    ended([f_ab, c_ab])
    f_pair = f_ab.whole[0][0]
    f_value, f_out, tail = f_ab.whole[1]
    whole = tail.reshape(devices, -1)[:, : sum(widths)].astype(jnp.float32)
    gains = []
    start = 0
    for width in widths:
        gains.append(whole[:, start : start + width].reshape(devices * width))
        start += width
    frame_gains = tuple(gains[:4])
    code_gains = tuple(gains[4:])
    frame_x = frame_input.astype(jnp.float32)
    f_normed = rms_scale(frame_x, frame_gains[0]).astype(low)
    started([c_ab, c_d])
    segments = segment_ids[0]
    f_qk = times(f_normed, f_pair).astype(low)
    f_v = times(f_normed, f_value).astype(low)
    f_mixed = frame_attend(f_qk, f_v, segments)
    f_qk, f_v, f_mixed = ended([c_ab, c_d], f_qk, f_v, f_mixed)
    started([c_ab, c_d])
    f_hidden = frame_x + times(f_mixed, f_out)
    f_normed_two = rms_scale(f_hidden, frame_gains[1]).astype(low)
    f_hidden, f_normed_two = ended([c_ab, c_d], f_hidden, f_normed_two)
    started([c_d])
    f_act, f_slope = gelu_and_slope(times(f_normed_two, f_up) + frame_gains[2])
    rows = CB * frames
    grad_code_y = grad_code_y.reshape(rows, D)
    frame_y = f_hidden + (times(f_act, f_down) + frame_gains[3])

    def tokens_of(value):
        return value.reshape(CB, frames, value.shape[-1])

    code_x = (code_rows.astype(jnp.float32) + frame_y[None]).reshape(rows, D)
    c_normed = rms_scale(code_x, code_gains[0]).astype(low)
    c_pair = c_ab.whole[0][0]
    c_value, c_out = c_ab.whole[1]
    c_qk = times(c_normed, c_pair).astype(low)
    c_v = times(c_normed, c_value).astype(low)
    c_mixed = code_attend(tokens_of(c_qk), tokens_of(c_v)).reshape(rows, D)
    c_hidden = code_x + times(c_mixed, c_out)
    (c_hidden,) = ended([c_d], c_hidden)
    started([c_d])
    c_normed_two = rms_scale(c_hidden, code_gains[1]).astype(low)
    c_act, c_slope = gelu_and_slope(times(c_normed_two, c_up) + code_gains[2])
    c_act, c_slope = ended([c_d], c_act, c_slope)
    ((c_down,),) = c_d.whole

    def both(exchange):
        return [summed([(exchange, (True, False))], sizes)]

    def attention_sums(pair, value, outproj):
        parts = [(pair, (False,)), (value, (True,)), (outproj, (True,))]
        return [summed(parts, sizes)]

    def norm_back(grad_out, inputs, gain):
        unused, back = jax.vjp(rms_scale, inputs, gain)
        return back(grad_out)

    grad_low = grad_code_y
    c_d_core = Core(c_act, grad_low, sizes)
    c_slope, grad_low = scatter_round([], [c_d_core], c_slope, grad_low)
    c_grad_b_down = jnp.sum(grad_low.astype(jnp.float32), axis=0)
    c_grad_b_down, c_down = ended([c_d_core], c_grad_b_down, c_down)
    c_d_chain = both(c_d_core)
    c_slope, grad_low = scatter_round([], c_d_chain, c_slope, grad_low)
    grad_pre, c_grad_b_up = grad_pre_of(grad_low, c_down, c_slope)
    c_u_core = Core(c_normed_two, grad_pre, sizes)
    (grad_pre,) = scatter_round(c_d_chain, c_d_chain + [c_u_core], grad_pre)
    grad_two = grad_two_of(grad_pre, c_up)
    (grad_two,) = scatter_round(c_d_chain + [c_u_core], c_d_chain, grad_two)
    c_u_chain = both(c_u_core)
    grad_part, c_grad_mid = norm_back(grad_two, c_hidden, code_gains[1])
    grad_hidden = grad_low.astype(jnp.float32) + grad_part
    grad_attn = grad_hidden.astype(low)
    grad_attn, grad_hidden = scatter_round(
        c_d_chain, c_d_chain + c_u_chain, grad_attn, grad_hidden
    )
    c_o_core = Core(c_mixed, grad_attn, sizes)
    grad_mixed = against(grad_attn, c_out).astype(low)
    grad_pair, grad_values = code_attend_back(
        tokens_of(c_qk), tokens_of(c_v), tokens_of(grad_mixed)
    )
    grad_pair = grad_pair.reshape(rows, 2 * D)
    grad_values = grad_values.reshape(rows, D)
    grad_pair, grad_values = scatter_round(
        c_d_chain + c_u_chain, c_u_chain + [c_o_core], grad_pair, grad_values
    )
    c_p_core = Core(c_normed, grad_pair, sizes)
    c_v_core = Core(c_normed, grad_values, sizes)
    grad_pair, grad_values = scatter_round(
        c_u_chain + [c_o_core], c_u_chain + [c_p_core, c_v_core], grad_pair, grad_values
    )
    grad_normed = against(grad_pair, c_pair) + against(grad_values, c_value)
    grad_part, c_grad_pre = norm_back(grad_normed, code_x, code_gains[0])
    grad_code_x = grad_hidden + grad_part
    grad_frame_y = frame_cotangent.astype(jnp.float32) + jnp.sum(tokens_of(grad_code_x), axis=0)
    grad_code_x, grad_frame_y = scatter_round(
        c_u_chain + [c_p_core, c_v_core], c_u_chain, grad_code_x, grad_frame_y
    )
    c_sums = attention_sums(c_p_core, c_v_core, c_o_core)
    (grad_frame_y,) = scatter_round(c_u_chain, c_sums, grad_frame_y)

    grad_low = grad_frame_y.astype(low)
    f_d_core = Core(f_act, grad_low, sizes)
    grad_pre, f_grad_b_up = grad_pre_of(grad_low, f_down, f_slope)
    f_u_core = Core(f_normed_two, grad_pre, sizes)
    (grad_pre,) = scatter_round(c_sums, c_sums + [f_d_core, f_u_core], grad_pre)
    grad_two = grad_two_of(grad_pre, f_up)
    grad_part, f_grad_mid = norm_back(grad_two, f_hidden, frame_gains[1])
    grad_hidden = grad_frame_y + grad_part
    grad_attn = grad_hidden.astype(low)
    grad_attn, grad_hidden = scatter_round(
        c_sums + [f_d_core, f_u_core], c_sums, grad_attn, grad_hidden
    )
    f_d_chain = both(f_d_core)
    grad_attn, grad_hidden = scatter_round(
        c_sums, c_sums + f_d_chain, grad_attn, grad_hidden
    )
    f_u_chain = both(f_u_core)
    f_o_core = Core(f_mixed, grad_attn, sizes)
    grad_mixed = against(grad_attn, f_out).astype(low)
    grad_pair, grad_values = frame_attend_back(f_qk, f_v, grad_mixed, segments)
    grad_pair, grad_values, c_act = scatter_round(
        c_sums + f_d_chain, f_d_chain + f_u_chain + [f_o_core], grad_pair, grad_values, c_act
    )
    f_p_core = Core(f_normed, grad_pair, sizes)
    f_v_core = Core(f_normed, grad_values, sizes)
    code_y = c_hidden + (times(c_act, c_down) + code_gains[3])
    code_y, grad_pair, grad_values = scatter_round(
        f_d_chain + f_u_chain + [f_o_core],
        f_d_chain + f_u_chain + [f_p_core, f_v_core],
        code_y,
        grad_pair,
        grad_values,
    )
    grad_normed = against(grad_pair, f_pair) + against(grad_values, f_value)
    grad_part, f_grad_pre = norm_back(grad_normed, frame_x, frame_gains[0])
    grad_frame_x = grad_hidden + grad_part
    f_grad_b_down = jnp.sum(grad_low.astype(jnp.float32), axis=0)
    terms = jnp.concatenate(
        [
            term.reshape(devices, -1)
            for term in (
                f_grad_pre,
                f_grad_mid,
                f_grad_b_up,
                f_grad_b_down,
                c_grad_pre,
                c_grad_mid,
                c_grad_b_up,
                c_grad_b_down,
            )
        ],
        axis=1,
    )
    row = VectorScatter(terms, sizes)
    (grad_frame_x,) = scatter_round(
        f_d_chain + f_u_chain + [f_p_core, f_v_core],
        f_d_chain + f_u_chain + [row],
        grad_frame_x,
    )
    f_sums = attention_sums(f_p_core, f_v_core, f_o_core)
    (code_y,) = scatter_round(
        f_d_chain + f_u_chain + [row], f_d_chain + f_u_chain + f_sums + [row], code_y
    )
    frame_output = frame_y.astype(low)
    code_output = jnp.swapaxes(tokens_of(code_y.astype(low)), 0, 1)
    (code_output,) = scatter_round(f_u_chain + f_sums + [row], f_sums + [row], code_output)
    code_embed_grad = jnp.swapaxes(tokens_of(grad_code_x), 0, 1)
    (code_embed_grad,) = scatter_round(f_sums + [row], f_sums + [row], code_embed_grad)
    everything = c_d_chain + c_u_chain + c_sums + f_d_chain + f_u_chain + f_sums + [row]
    while True:
        started([chain for chain in everything if chain.away and chain.received is None])
        going = [chain for chain in everything if chain.received is not None]
        if not going:
            break
        ended(going)
    sums = row.state[0]
    pieces = []
    start = 0
    for width in widths:
        pieces.append(sums[start : start + width])
        start += width

    def arranged(attn_sums, up_sums, down_sums, vecs):
        total = attn_sums[0].result()
        prenorm, midnorm, upbias, downbias = vecs
        return (
            prenorm,
            total[:, :D],
            total[:, D : 2 * D],
            total[:, 2 * D : 3 * D],
            total[:, 3 * D :],
            midnorm,
            up_sums,
            upbias,
            down_sums,
            downbias,
        )

    code_outs = arranged(c_sums, c_u_chain[0].result(), c_d_chain[0].result(), pieces[4:])
    frame_outs = arranged(
        f_sums, f_u_chain[0].result(), f_d_chain[0].result(), pieces[:4]
    )
    return (frame_output, code_output, grad_frame_x, code_embed_grad) + frame_outs + code_outs


def solution(mesh):
    in_specs = (
        P(("gx", "gy"), None),
        P(("gx", "gy"), None, None),
        P(("gx", "gy"), None),
        P(("gx", "gy"), None),
        P(("gx", "gy"), None, None),
        P(("gx", "gy")),
        P(("gx", "gy"), None),
        P(("gx", "gy"), None),
        P(("gx", "gy"), None),
        P(("gx", "gy"), None),
        P(("gx", "gy")),
        P(("gx", "gy"), None),
        P(("gx", "gy")),
        P(("gx", "gy"), None),
        P(("gx", "gy")),
        P(("gx", "gy")),
        P(("gx", "gy"), None),
        P(("gx", "gy"), None),
        P(("gx", "gy"), None),
        P(("gx", "gy"), None),
        P(("gx", "gy")),
        P(("gx", "gy"), None),
        P(("gx", "gy")),
        P(("gx", "gy"), None),
        P(("gx", "gy")),
    )
    out_specs = (
        P(("gx", "gy"), None),
        P(("gx", "gy"), None, None),
        P(("gx", "gy"), None),
        P(("gx", "gy"), None, None),
        P(("gx", "gy")),
        P(("gx", "gy"), None),
        P(("gx", "gy"), None),
        P(("gx", "gy"), None),
        P(("gx", "gy"), None),
        P(("gx", "gy")),
        P(("gx", "gy"), None),
        P(("gx", "gy")),
        P(("gx", "gy"), None),
        P(("gx", "gy")),
        P(("gx", "gy")),
        P(("gx", "gy"), None),
        P(("gx", "gy"), None),
        P(("gx", "gy"), None),
        P(("gx", "gy"), None),
        P(("gx", "gy")),
        P(("gx", "gy"), None),
        P(("gx", "gy")),
        P(("gx", "gy"), None),
        P(("gx", "gy")),
    )
    sizes = (mesh.shape["gx"], mesh.shape["gy"])
    return jax.shard_map(
        functools.partial(local, sizes), mesh=mesh, in_specs=in_specs, out_specs=out_specs, check_vma=False)
```
